768 devices in a mesh: dp: 48 (over x_hi, z, core), fsdp: 16 (over x_lo, y).
Axes of the slice: x: 4 (x_hi: 2, x_lo: 2; x = x_hi * 2 + x_lo), y: 8, z: 12, core: 2. Of those that a mesh axis runs over, the one named last changes fastest.
Arguments:
- features: bfloat16 [384, 512, 640], P('dp', 'fsdp'), may hold values from -6 to 6
- skip_input: bfloat16 [384, 512, 640], P('dp', 'fsdp'), may hold values from -6 to 6
- cotangent: bfloat16 [384, 512, 640], P('dp', 'fsdp'), may hold values from -6 to 6
- temporal_weight: bfloat16 [640, 1920], P('fsdp'), may hold values from -0.125 to 0.125
- clip_lengths: int32 [48], replicated, may hold values from 1 to 16, 384 in all
- cycle_start: int32 [1], replicated, may hold values from 0 to 383
Outputs:
- block_out: bfloat16 [384, 512, 640], P('dp', 'fsdp')
- grad_features: bfloat16 [384, 512, 640], P('dp', 'fsdp')
- grad_weight: float32 [640, 1920], P('fsdp')
The draws below stay inside these ranges and needn't reach their ends.
Inputs may be any that keep to these rules, and one draw needn't show every extreme that they name: `clip_lengths`: the lengths sum to 384; the longest clip has exactly 16 frames.
All inputs are finite; a program needn't handle non-finite values.
Results may differ from the reference program's by a relative error of at most 0.001.
Values may be sent and summed in bfloat16 or wider, within the bound.
No kernel may reach another device: no remote copies, remote signals or barrier semaphores. Data moves between devices by JAX's collectives and lax.ppermute only.
A program may use at most 128 MiB of HBM per device.

```python
import math
import jax
import jax.numpy as jnp
import numpy as np
from jax import lax

C = 640
F_DEV = 8
PIX_DEV = 32
CLIP_MAX = 16
FRAMES = 384
PIX = 512
CLIPS = 48
N_DP = 48
N_FSDP = 16


def strengthened(entries, rng, source, target, blocks, factor):
    owner, partner = [(jnp.arange(entries.shape[dim]) // (entries.shape[dim] // blocks)).reshape([-1 if axis == dim else 1 for axis in range(entries.ndim)]) for dim in (source, target)]
    chosen = jax.random.permutation(rng, blocks)[partner]
    strong = (owner == chosen) | (owner == (partner + blocks // 2) % blocks)
    return jnp.where(strong, factor * entries, entries)


def levels(own_key, dims, shards, smallest, high):
    gain, own = 1.0, jax.random.fold_in(own_key, 6)
    for dim, blocks in shards:
        steps = jnp.exp(jax.random.uniform(jax.random.fold_in(own, dim), (blocks,), jnp.float32, smallest / len(shards), high / len(shards)))
        gain = gain * jnp.repeat(steps, dims[dim] // blocks).reshape([-1 if axis == dim else 1 for axis in range(len(dims))])
    return gain


def profile(amount, total, bound, lean):
    loads = [(1 << 20) // math.isqrt(rank ** lean) + 1 for rank in range(2, amount + 1)]
    surplus, counts = total - bound - (amount - 1), [1] * (amount - 1)
    while surplus > 0:
        free = [i for i in range(amount - 1) if counts[i] < bound]
        pool, left = sum([loads[i] for i in free]), surplus
        for i in free:
            more = min(bound - counts[i], max(1, left * loads[i] // pool), surplus)
            counts[i] = counts[i] + more
            surplus = surplus - more
    return np.array([bound] + counts)


def ragged(rng, number_of, total, bound, slope):
    if number_of == 2:
        one = jax.random.randint(rng, (), max(1, total - bound), min(bound, total - 1) + 1)
        return jnp.stack([one, total - one])
    tallies = jnp.asarray(profile(number_of, total, bound, slope), jnp.int32)
    twos = (number_of - 1) // 2
    giver, taker = tallies[1:1 + 2 * twos:2], tallies[2:2 + 2 * twos:2]
    room = jnp.minimum(giver - 1, bound - taker)
    moved = jax.random.randint(jax.random.fold_in(rng, 1), (twos,), 0, 1 << 20) % (room + 1)
    tallies = tallies.at[1:1 + 2 * twos:2].set(giver - moved).at[2:2 + 2 * twos:2].set(taker + moved)
    return tallies[jax.random.permutation(jax.random.fold_in(rng, 2), number_of)]


def normal_values(rng, extent, spread, limit, pieces=(), kind=jnp.bfloat16):
    gain = levels(rng, extent, pieces, -0.22, 0.18) if pieces else 1.0
    drawn = jax.random.normal(rng, extent, jnp.float32) * spread * gain
    return jnp.minimum(jnp.maximum(drawn, -limit), limit).astype(kind)


def noise_with(rng, dims, spread, limit, shards, heavy, kind=jnp.bfloat16):
    values = spread * jax.random.normal(rng, dims, jnp.float32)
    if shards:
        values = values * levels(rng, dims, shards, -0.22, 0.18)
    return jnp.clip(strengthened(values, jax.random.fold_in(rng, 3), *heavy), -limit, limit).astype(kind)


def setup_inputs(seed: int = 0) -> dict:
    arg_keys = jax.random.split(jax.random.key(seed), 7)
    return {
        "features": noise_with(arg_keys[0], (FRAMES, PIX, C), 1.0, 6.0, ((0, 48), (1, 16)), (1, 2, 16, 2.0)),
        "skip_input": normal_values(arg_keys[1], (FRAMES, PIX, C), 1.0, 6.0, ((0, 48), (1, 16))),
        "cotangent": normal_values(arg_keys[2], (FRAMES, PIX, C), 1.0, 6.0, ((0, 48), (1, 16))),
        "temporal_weight": normal_values(arg_keys[3], (C, 3 * C), (3 * C) ** -0.5, 0.125, ((0, 16),)),
        "clip_lengths": ragged(arg_keys[4], CLIPS, FRAMES, CLIP_MAX, 2).astype(jnp.int32),
        "cycle_start": jax.random.randint(arg_keys[5], (1,), 0, FRAMES).astype(jnp.int32),
    }


def border_flags(clip_lengths, cycle_start, frame_index, total):
    lengths = clip_lengths.astype(jnp.int32)
    starts = (jnp.cumsum(lengths) - lengths).astype(jnp.int32)
    position = jnp.mod(frame_index - cycle_start[0], total).astype(jnp.int32)
    following = jnp.mod(frame_index + 1 - cycle_start[0], total).astype(jnp.int32)
    first_here = jnp.any(position[:, None] == starts[None, :], axis=1)
    first_next = jnp.any(following[:, None] == starts[None, :], axis=1)
    return (1 - first_here.astype(jnp.int32), 1 - first_next.astype(jnp.int32))

def reference(features, skip_input, cotangent, temporal_weight, clip_lengths, cycle_start):
    frame_index = jnp.arange(FRAMES, dtype=jnp.int32)
    prev_ok, next_ok = border_flags(clip_lengths, cycle_start, frame_index, FRAMES)
    prev_scale = prev_ok.astype(jnp.bfloat16)[:, None, None]
    next_scale = next_ok.astype(jnp.bfloat16)[:, None, None]
    features_prev = prev_scale * jnp.roll(features, 1, axis=0)
    features_next = next_scale * jnp.roll(features, -1, axis=0)
    cot_prev = prev_scale * jnp.roll(cotangent, 1, axis=0)
    cot_next = next_scale * jnp.roll(cotangent, -1, axis=0)
    weight_full = temporal_weight.astype(jnp.float32).reshape(C, 3, C)

    def tile_step(carry, index):
        begin = (index * F_DEV).astype(jnp.int32)

        def cut(array):
            return lax.dynamic_slice_in_dim(array, begin, F_DEV, 0)
        stacked_in = jnp.stack([cut(features_prev), cut(features), cut(features_next)], axis=2)
        stacked_back = jnp.stack([cut(cot_next), cut(cotangent), cut(cot_prev)], axis=2)
        mixed = jnp.einsum('fpkr,rkc->fpc', stacked_in.astype(jnp.float32), weight_full)
        out_tile = (cut(skip_input).astype(jnp.float32) + mixed).astype(jnp.bfloat16)
        back_tile = jnp.einsum('fpkc,rkc->fpr', stacked_back.astype(jnp.float32), weight_full).astype(jnp.bfloat16)
        strips_in = stacked_in.reshape(F_DEV, N_FSDP, PIX_DEV, 3, C).astype(jnp.float32)
        strips_cot = cut(cotangent).reshape(F_DEV, N_FSDP, PIX_DEV, C).astype(jnp.float32)
        terms = jnp.einsum('fspkr,fspc->srkc', strips_in, strips_cot)
        return (carry + lax.optimization_barrier(jnp.sum(terms, axis=0)), (out_tile, back_tile))
    initial = jnp.zeros((C, 3, C), jnp.float32)
    total_grad, (out_tiles, back_tiles) = lax.scan(tile_step, initial, jnp.arange(N_DP, dtype=jnp.int32))
    block_out = out_tiles.reshape(FRAMES, PIX, C)
    grad_features = back_tiles.reshape(FRAMES, PIX, C)
    grad_weight = total_grad.reshape(C, 3 * C) / jnp.sqrt(jnp.float32(FRAMES * PIX))
    return (block_out, grad_features, grad_weight)
```

```python
import jax
import jax.numpy as jnp
from jax import lax
from jax.experimental import pallas as pl
from jax.experimental.pallas import tpu as pltpu
from jax.sharding import Mesh, PartitionSpec as P

DP = ("xh", "z", "c")
FSDP = ("xl", "y")
X = ("xh", "xl")


def border_flags(clip_lengths, cycle_start, frame_index, total):
    starts = jnp.cumsum(clip_lengths) - clip_lengths
    position = jnp.mod(frame_index - cycle_start[0], total)
    following = jnp.mod(frame_index + 1 - cycle_start[0], total)
    first_here = jnp.any(position[:, None] == starts[None, :], axis=1)
    first_next = jnp.any(following[:, None] == starts[None, :], axis=1)
    return (1 - first_here.astype(jnp.int32), 1 - first_next.astype(jnp.int32))


def term_kernel(core_ref, prev_ref, next_ref, f_ref, sf_ref, g_ref, sg_ref, halo_ref, out_ref, fa, fc, gg):
    frames, strip, width = f_ref.shape
    half = frames * strip
    core = core_ref[0]

    def put(slot, value, ok):
        fa[pl.ds(slot * strip, strip), :] = jnp.where(ok != 0, value, jnp.zeros_like(value))

    for ref, offset, dst in ((f_ref, 0, fc), (sf_ref, half, fc), (g_ref, 0, gg), (sg_ref, half, gg)):
        dst[pl.ds(offset, half), :] = ref[...].reshape(half, width)

    @pl.when(core == 0)
    def _():
        for j in range(frames):
            put(j, halo_ref[...] if j == 0 else f_ref[j - 1], prev_ref[j])
            put(frames + j, f_ref[frames - 1] if j == 0 else sf_ref[j - 1], prev_ref[frames + j])

    @pl.when(core != 0)
    def _():
        for j in range(frames):
            put(j, halo_ref[...] if j == frames - 1 else f_ref[j + 1], next_ref[frames + j])
            put(frames + j, f_ref[0] if j == frames - 1 else sf_ref[j + 1], next_ref[j])

    def dot(a, b):
        return lax.dot_general(a, b, (((0,), (0,)), ((), ())), preferred_element_type=jnp.float32)

    rows = width // 2
    wide = out_ref.shape[3]
    rest = width - wide
    first = dot(fa[...], gg[...])
    for xl in range(2):
        out_ref[0, xl] = first[xl * rows:(xl + 1) * rows, :wide]
        out_ref[1, xl, :, :rest] = first[xl * rows:(xl + 1) * rows, wide:]

    @pl.when(core == 0)
    def _():
        second = dot(fc[...], gg[:, :384])
        for xl in range(2):
            out_ref[1, xl, :, rest:] = second[xl * rows:(xl + 1) * rows]

    @pl.when(core != 0)
    def _():
        second = dot(fc[...], gg[:, 384:])
        for xl in range(2):
            out_ref[1, xl, :, rest:rest + 256] = second[xl * rows:(xl + 1) * rows]
            out_ref[1, xl, :, rest + 256:] = jnp.zeros((rows, 128), jnp.float32)


def chip_term(core, prev_ok, next_ok, features, sib_features, cotangent, sib_cotangent, halo):
    frames, strip, width = features.shape
    smem = pl.BlockSpec(memory_space=pltpu.SMEM)
    vmem = pl.BlockSpec(memory_space=pltpu.VMEM)
    buf = pltpu.VMEM((2 * frames * strip, width), jnp.bfloat16)
    return pl.pallas_call(
        term_kernel,
        out_shape=jax.ShapeDtypeStruct((2, 2, width // 2, 512), jnp.float32),
        in_specs=[smem] * 3 + [vmem] * 5,
        out_specs=vmem,
        scratch_shapes=[buf, buf, buf],
        compiler_params=pltpu.CompilerParams(vmem_limit_bytes=48 << 20),
        name="chip_term",
    )(core, prev_ok, next_ok, features, sib_features, cotangent, sib_cotangent, halo)


def shards(features, skip_input, cotangent, temporal_weight, clip_lengths, cycle_start):
    frames, strip, width = features.shape
    core = lax.axis_index("c")
    chip = lax.axis_index("xh") * lax.axis_size("z") + lax.axis_index("z")
    n_dp = lax.axis_size(DP)
    total_frames = frames * n_dp
    tokens = frames * strip

    weight_all = lax.all_gather(temporal_weight, FSDP, axis=0, tiled=True)

    both = [(0, 1), (1, 0)]
    sib_features = lax.ppermute(features, "c", both)
    sib_cotangent = lax.ppermute(cotangent, "c", both)
    edge_f = jnp.where(core == 0, features[0], features[-1])
    edge_g = jnp.where(core == 0, cotangent[0], cotangent[-1])
    across = [(d, (d - 1) % n_dp if d % 2 == 0 else (d + 1) % n_dp) for d in range(n_dp)]
    halo = lax.ppermute(jnp.concatenate([edge_f, edge_g], axis=1), DP, across)
    halo_f, halo_g = halo[:, :width], halo[:, width:]

    chip_frames = chip * (2 * frames) + jnp.arange(2 * frames, dtype=jnp.int32)
    prev_all, next_all = border_flags(clip_lengths, cycle_start, chip_frames, total_frames)

    term = chip_term(
        core.astype(jnp.int32).reshape(1), prev_all, next_all,
        features, sib_features, cotangent, sib_cotangent, halo_f,
    )
    n_x, n_y, n_z = lax.axis_size(X), lax.axis_size("y"), lax.axis_size("z")
    part = lax.all_to_all(term.reshape(n_x, width // 2, 512), X, 0, 0, tiled=True).sum(0)
    part = lax.all_to_all(part.reshape(n_y, width // 2 // n_y, 512), "y", 0, 0, tiled=True).sum(0)
    part, weight_all = lax.optimization_barrier((part, weight_all))
    local_rows = part.shape[0]
    blocks = jnp.pad(part, ((0, 48 - local_rows), (0, 0))).reshape(6, 8, 2, 256).transpose(0, 2, 1, 3)
    mine = lax.all_to_all(blocks.reshape(n_z, 8, 256), "z", 0, 0, tiled=True).sum(0)
    mine = mine / jnp.sqrt(jnp.float32(total_frames * strip * lax.axis_size(FSDP)))
    n_xz = 2 * n_z
    gathered = lax.all_to_all(jnp.broadcast_to(mine[None], (n_xz, 8, 256)), ("xh", "z"), 0, 0, tiled=True)
    other = lax.ppermute(gathered, "c", both)

    def flat(a):
        a = a.reshape(2, 6, 2, 8, 256).transpose(1, 3, 0, 2, 4)
        return a.reshape(48, 1024)[:local_rows]

    low = flat(jnp.where(core == 0, gathered, other))
    high = flat(jnp.where(core == 0, other, gathered))
    grad_weight = jnp.concatenate([low, high[:, 640:896], high[:, :640]], axis=1)

    own = core * frames
    prev_scale = lax.dynamic_slice_in_dim(prev_all, own, frames).astype(jnp.bfloat16)[:, None, None]
    next_scale = lax.dynamic_slice_in_dim(next_all, own, frames).astype(jnp.bfloat16)[:, None, None]

    def around(x, sib, edge):
        before = jnp.where(core == 0, edge, sib[-1])[None]
        after = jnp.where(core == 0, sib[0], edge)[None]
        wide = jnp.concatenate([before, x, after], axis=0)
        return prev_scale * wide[:-2], next_scale * wide[2:]

    features_prev, features_next = around(features, sib_features, halo_f)
    cot_prev, cot_next = around(cotangent, sib_cotangent, halo_g)
    kernel_rows = weight_all.reshape(width, 3, width)
    stacked_in = jnp.stack([features_prev, features, features_next], axis=2).reshape(tokens, 3, width)
    stacked_back = jnp.stack([cot_next, cotangent, cot_prev], axis=2).reshape(tokens, 3, width)
    mixed = jnp.einsum("nkr,rkc->nc", stacked_in, kernel_rows, preferred_element_type=jnp.float32)
    back = jnp.einsum("nkc,rkc->nr", stacked_back, kernel_rows, preferred_element_type=jnp.float32)
    block_out = (skip_input.astype(jnp.float32) + mixed.reshape(frames, strip, width)).astype(jnp.bfloat16)
    grad_features = back.reshape(frames, strip, width).astype(jnp.bfloat16)
    return (block_out, grad_features, grad_weight)


def solution(mesh):
    split = Mesh(mesh.devices.reshape(2, 12, 2, 2, 8), DP + FSDP)
    tokens = P(DP, FSDP, None)
    in_specs = (tokens, tokens, tokens, P(FSDP, None), P(), P())
    out_specs = (tokens, tokens, P(FSDP, None))
    return jax.shard_map(shards, mesh=split, in_specs=in_specs, out_specs=out_specs, check_vma=False)
```

```python
import jax
import jax.numpy as jnp
from jax import lax
from jax.experimental import pallas as pl
from jax.experimental.pallas import tpu as pltpu
from jax.sharding import Mesh, PartitionSpec as P

DP = ("xh", "z", "c")
FSDP = ("xl", "y")
X = ("xh", "xl")


def border_flags(clip_lengths, cycle_start, frame_index, total):
    starts = jnp.cumsum(clip_lengths) - clip_lengths
    position = jnp.mod(frame_index - cycle_start[0], total)
    following = jnp.mod(frame_index + 1 - cycle_start[0], total)
    first_here = jnp.any(position[:, None] == starts[None, :], axis=1)
    first_next = jnp.any(following[:, None] == starts[None, :], axis=1)
    return (1 - first_here.astype(jnp.int32), 1 - first_next.astype(jnp.int32))


def pack_kernel(f_ref, g_ref, out_ref):
    frames, strip, width = f_ref.shape
    f = f_ref[...].reshape(frames * strip, width)
    g = g_ref[...].reshape(frames * strip, width)
    f_mid, g_mid = f[:, 256:384], g[:, 256:384]
    f_rolled, g_rolled = [pltpu.roll(m.astype(jnp.float32), 64, 1).astype(jnp.bfloat16) for m in (f_mid, g_mid)]
    left = lax.broadcasted_iota(jnp.int32, f_mid.shape, 1) < 64
    for xh in range(2):
        for xl in range(2):
            j = 2 * xh + xl
            out_ref[j, :, :256] = f[:, 384 * xl:384 * xl + 256]
            out_ref[j, :, 256:384] = jnp.where(left, f_rolled if xl else f_mid, g_mid if xh else g_rolled)
            out_ref[j, :, 384:] = g[:, 384 * xh:384 * xh + 256]


def pack(features, cotangent):
    frames, strip, width = features.shape
    vmem = pl.BlockSpec(memory_space=pltpu.VMEM)
    return pl.pallas_call(
        pack_kernel,
        out_shape=jax.ShapeDtypeStruct((4, frames * strip, width), jnp.bfloat16),
        in_specs=[vmem] * 2,
        out_specs=vmem,
        compiler_params=pltpu.CompilerParams(vmem_limit_bytes=48 << 20),
        name="pack",
    )(features, cotangent)


def term_kernel(place_ref, prev_ref, next_ref, own_ref, sib_ref, halo_ref, out_ref, fa_own, fa_sib):
    chips, frames, strip, _ = own_ref.shape
    core, xl, wrapped = place_ref[0], place_ref[1], place_ref[2]

    def put(dst, chip, slot, value, ok):
        dst[pl.ds((chip * frames + slot) * strip, strip), :] = jnp.where(ok != 0, value, jnp.zeros_like(value))

    def halo(chip):
        return halo_ref[(chip // 2 + wrapped) % 2 * 2 + chip % 2]

    @pl.when(core == 0)
    def _():
        for chip in range(chips):
            at = chip // 2 * 2 * frames
            for j in range(frames):
                mine = halo(chip) if j == 0 else own_ref[chip, j - 1, :, :384]
                its = own_ref[chip, frames - 1, :, :384] if j == 0 else sib_ref[chip, j - 1, :, :384]
                put(fa_own, chip, j, mine, prev_ref[at + j])
                put(fa_sib, chip, j, its, prev_ref[at + frames + j])

    @pl.when(core != 0)
    def _():
        for chip in range(chips):
            at = chip // 2 * 2 * frames
            for j in range(frames):
                mine = halo(chip) if j == frames - 1 else own_ref[chip, j + 1, :, :384]
                its = own_ref[chip, 0, :, :384] if j == frames - 1 else sib_ref[chip, j + 1, :, :384]
                put(fa_own, chip, j, mine, next_ref[at + frames + j])
                put(fa_sib, chip, j, its, next_ref[at + j])

    def flat(ref, start, stop):
        return ref[:, :, :, start:stop].reshape(chips * frames * strip, stop - start)

    def dot(a, b):
        return lax.dot_general(a, b, (((0,), (0,)), ((), ())), preferred_element_type=jnp.float32)

    def center(start, stop):
        return dot(flat(own_ref, 0, 384), flat(own_ref, start, stop)) + dot(flat(sib_ref, 0, 384), flat(sib_ref, start, stop))

    outer = dot(fa_own[...], flat(own_ref, 256, 640)) + dot(fa_sib[...], flat(sib_ref, 256, 640))
    left = lax.broadcasted_iota(jnp.int32, (384, 128), 1) < 64
    rolled = pltpu.roll(outer[:, :128], 64, 1)

    def store(start, stop, value):
        @pl.when(xl == 0)
        def _():
            out_ref[:, start:stop] = value[:320]

        @pl.when(xl != 0)
        def _():
            out_ref[64:, start:stop] = value[:256]
            out_ref[:64, start:stop] = value[256:320]

    store(0, 256, outer[:, 128:])

    @pl.when(core == 0)
    def _():
        mid = center(256, 512)
        store(256, 384, jnp.where(left, rolled, mid[:, :128]))
        store(384, 512, mid[:, 128:])

    @pl.when(core != 0)
    def _():
        store(256, 384, jnp.where(left, rolled, jnp.zeros_like(rolled)))
        store(384, 512, center(512, 640))


def x_term(place, prev_ok, next_ok, own, sib, halo):
    smem = pl.BlockSpec(memory_space=pltpu.SMEM)
    vmem = pl.BlockSpec(memory_space=pltpu.VMEM)
    chips, frames, strip, _ = own.shape
    buf = pltpu.VMEM((chips * frames * strip, 384), jnp.bfloat16)
    return pl.pallas_call(
        term_kernel,
        out_shape=jax.ShapeDtypeStruct((320, 512), jnp.float32),
        in_specs=[smem] * 3 + [vmem] * 3,
        out_specs=vmem,
        scratch_shapes=[buf, buf],
        compiler_params=pltpu.CompilerParams(vmem_limit_bytes=48 << 20),
        name="x_term",
    )(place, prev_ok, next_ok, own, sib, halo)


def shards(features, skip_input, cotangent, temporal_weight, clip_lengths, cycle_start):
    frames, strip, width = features.shape
    core, xl, xh, z = [lax.axis_index(a) for a in ("c", "xl", "xh", "z")]
    n_x, n_y, n_z = lax.axis_size(X), lax.axis_size("y"), lax.axis_size("z")
    n_dp = lax.axis_size(DP)
    total_frames = frames * n_dp
    tokens = frames * strip

    weight_all = lax.all_gather(temporal_weight, FSDP, axis=0, tiled=True)

    both = [(0, 1), (1, 0)]
    own = lax.all_to_all(pack(features, cotangent), X, 0, 0, tiled=True).reshape(n_x, frames, strip, width)
    sib = lax.ppermute(own, "c", both)
    z_next = [(2 * i, (2 * i - 1) % (2 * n_z)) for i in range(n_z)] + [(2 * i + 1, (2 * i + 2) % (2 * n_z)) for i in range(n_z)]
    edge = jnp.where(core == 0, own[:, 0, :, :384], own[:, -1, :, :384])
    halo_x = lax.ppermute(edge, ("z", "c"), z_next)

    first = (jnp.arange(2, dtype=jnp.int32) * n_z + z)[:, None] * (2 * frames)
    chip_frames = (first + jnp.arange(2 * frames, dtype=jnp.int32)).reshape(-1)
    prev_all, next_all = border_flags(clip_lengths, cycle_start, chip_frames, total_frames)
    wrapped = jnp.where(core == 0, z == 0, z == n_z - 1)
    place = jnp.stack([core, xl, wrapped.astype(jnp.int32)]).astype(jnp.int32)
    term = x_term(place, prev_all, next_all, own, sib, halo_x)

    part = lax.all_to_all(term.reshape(n_y, 320 // n_y, 512), "y", 0, 0, tiled=True).sum(0)
    part, weight_all = lax.optimization_barrier((part, weight_all))
    local_rows = part.shape[0]
    blocks = jnp.pad(part, ((0, 48 - local_rows), (0, 0))).reshape(6, 8, 2, 256).transpose(0, 2, 1, 3)
    mine = lax.all_to_all(blocks.reshape(n_z, 8, 256), "z", 0, 0, tiled=True).sum(0)
    mine = mine / jnp.sqrt(jnp.float32(total_frames * strip * lax.axis_size(FSDP)))
    n_xz = 2 * n_z
    gathered = lax.all_to_all(jnp.broadcast_to(mine[None], (n_xz, 8, 256)), ("xh", "z"), 0, 0, tiled=True)
    other = lax.ppermute(gathered, "c", both)

    def flat(a):
        a = a.reshape(2, 6, 2, 8, 256).transpose(0, 1, 3, 2, 4)
        return a.reshape(2, 48, 512)[:, :local_rows]

    low = flat(jnp.where(core == 0, gathered, other))
    high = flat(jnp.where(core == 0, other, gathered))

    def outer_tap(b):
        return [b[0, :, :320], b[1, :, 256:320], b[1, :, :256]]

    tap_1 = [low[0, :, 384:], high[0, :, 384:], low[0, :, 320:384], low[1, :, 320:], high[1, :, 384:]]
    grad_weight = jnp.concatenate(outer_tap(low) + tap_1 + outer_tap(high), axis=1)

    ends = [jnp.concatenate([features[i], cotangent[i]], axis=1) for i in (0, -1)]
    sib_edge = lax.ppermute(jnp.where(core == 0, ends[1], ends[0]), "c", both)
    across = [(d, (d - 1) % n_dp if d % 2 == 0 else (d + 1) % n_dp) for d in range(n_dp)]
    halo = lax.ppermute(jnp.where(core == 0, ends[0], ends[1]), DP, across)
    before = jnp.where(core == 0, halo, sib_edge)[None]
    after = jnp.where(core == 0, sib_edge, halo)[None]
    at = xh * (2 * frames) + core * frames
    prev_scale = lax.dynamic_slice_in_dim(prev_all, at, frames).astype(jnp.bfloat16)[:, None, None]
    next_scale = lax.dynamic_slice_in_dim(next_all, at, frames).astype(jnp.bfloat16)[:, None, None]

    def around(x, lanes):
        wide = jnp.concatenate([before[:, :, lanes], x, after[:, :, lanes]], axis=0)
        return prev_scale * wide[:-2], next_scale * wide[2:]

    features_prev, features_next = around(features, slice(0, width))
    cot_prev, cot_next = around(cotangent, slice(width, 2 * width))
    kernel_rows = weight_all.reshape(width, 3, width)
    stacked_in = jnp.stack([features_prev, features, features_next], axis=2).reshape(tokens, 3, width)
    stacked_back = jnp.stack([cot_next, cotangent, cot_prev], axis=2).reshape(tokens, 3, width)
    mixed = jnp.einsum("nkr,rkc->nc", stacked_in, kernel_rows, preferred_element_type=jnp.float32)
    back = jnp.einsum("nkc,rkc->nr", stacked_back, kernel_rows, preferred_element_type=jnp.float32)
    block_out = (skip_input.astype(jnp.float32) + mixed.reshape(frames, strip, width)).astype(jnp.bfloat16)
    grad_features = back.reshape(frames, strip, width).astype(jnp.bfloat16)
    return (block_out, grad_features, grad_weight)


def solution(mesh):
    split = Mesh(mesh.devices.reshape(2, 12, 2, 2, 8), DP + FSDP)
    tokens = P(DP, FSDP, None)
    in_specs = (tokens, tokens, tokens, P(FSDP, None), P(), P())
    out_specs = (tokens, tokens, P(FSDP, None))
    return jax.shard_map(shards, mesh=split, in_specs=in_specs, out_specs=out_specs, check_vma=False)
```

```python
import jax
import jax.numpy as jnp
from jax import lax
from jax.experimental import pallas as pl
from jax.experimental.pallas import tpu as pltpu
from jax.sharding import Mesh, PartitionSpec as P

DP = ("xh", "z", "c")
FSDP = ("xl", "y")
X = ("xh", "xl")


def border_flags(clip_lengths, cycle_start, frame_index, total):
    starts = jnp.cumsum(clip_lengths) - clip_lengths
    position = jnp.mod(frame_index - cycle_start[0], total)
    following = jnp.mod(frame_index + 1 - cycle_start[0], total)
    first_here = jnp.any(position[:, None] == starts[None, :], axis=1)
    first_next = jnp.any(following[:, None] == starts[None, :], axis=1)
    return (1 - first_here.astype(jnp.int32), 1 - first_next.astype(jnp.int32))


def pack_kernel(f_ref, g_ref, out_ref):
    frames, strip, width = f_ref.shape
    f = f_ref[...].reshape(frames * strip, width)
    g = g_ref[...].reshape(frames * strip, width)
    f_mid, g_mid = f[:, 256:384], g[:, 256:384]
    f_rolled, g_rolled = [pltpu.roll(m.astype(jnp.float32), 64, 1).astype(jnp.bfloat16) for m in (f_mid, g_mid)]
    left = lax.broadcasted_iota(jnp.int32, f_mid.shape, 1) < 64
    for xh in range(2):
        for xl in range(2):
            j = 2 * xh + xl
            out_ref[j, :, :256] = f[:, 384 * xl:384 * xl + 256]
            out_ref[j, :, 256:384] = jnp.where(left, f_rolled if xl else f_mid, g_mid if xh else g_rolled)
            out_ref[j, :, 384:] = g[:, 384 * xh:384 * xh + 256]


def pack(features, cotangent):
    frames, strip, width = features.shape
    vmem = pl.BlockSpec(memory_space=pltpu.VMEM)
    return pl.pallas_call(
        pack_kernel,
        out_shape=jax.ShapeDtypeStruct((4, frames * strip, width), jnp.bfloat16),
        in_specs=[vmem] * 2,
        out_specs=vmem,
        compiler_params=pltpu.CompilerParams(vmem_limit_bytes=48 << 20),
        name="pack",
    )(features, cotangent)


def term_kernel(place_ref, prev_ref, next_ref, own_ref, sib_ref, halo_ref, out_ref, fa_own, fa_sib):
    chips, frames, strip, _ = own_ref.shape
    core, xl, wrapped = place_ref[0], place_ref[1], place_ref[2]

    def put(dst, chip, slot, value, ok):
        dst[pl.ds((chip * frames + slot) * strip, strip), :] = jnp.where(ok != 0, value, jnp.zeros_like(value))

    def halo(chip):
        return halo_ref[(chip // 2 + wrapped) % 2 * 2 + chip % 2]

    @pl.when(core == 0)
    def _():
        for chip in range(chips):
            at = chip // 2 * 2 * frames
            for j in range(frames):
                mine = halo(chip) if j == 0 else own_ref[chip, j - 1, :, :384]
                its = own_ref[chip, frames - 1, :, :384] if j == 0 else sib_ref[chip, j - 1, :, :384]
                put(fa_own, chip, j, mine, prev_ref[at + j])
                put(fa_sib, chip, j, its, prev_ref[at + frames + j])

    @pl.when(core != 0)
    def _():
        for chip in range(chips):
            at = chip // 2 * 2 * frames
            for j in range(frames):
                mine = halo(chip) if j == frames - 1 else own_ref[chip, j + 1, :, :384]
                its = own_ref[chip, 0, :, :384] if j == frames - 1 else sib_ref[chip, j + 1, :, :384]
                put(fa_own, chip, j, mine, next_ref[at + frames + j])
                put(fa_sib, chip, j, its, next_ref[at + j])

    def flat(ref, start, stop):
        return ref[:, :, :, start:stop].reshape(chips * frames * strip, stop - start)

    def dot(a, b):
        return lax.dot_general(a, b, (((0,), (0,)), ((), ())), preferred_element_type=jnp.float32)

    def center(start, stop):
        return dot(flat(own_ref, 0, 384), flat(own_ref, start, stop)) + dot(flat(sib_ref, 0, 384), flat(sib_ref, start, stop))

    outer = dot(fa_own[...], flat(own_ref, 256, 640)) + dot(fa_sib[...], flat(sib_ref, 256, 640))
    left = lax.broadcasted_iota(jnp.int32, (384, 128), 1) < 64
    rolled = pltpu.roll(outer[:, :128], 64, 1)

    def store(start, stop, value):
        @pl.when(xl == 0)
        def _():
            out_ref[:, start:stop] = value[:320]

        @pl.when(xl != 0)
        def _():
            out_ref[64:, start:stop] = value[:256]
            out_ref[:64, start:stop] = value[256:320]

    store(0, 256, outer[:, 128:])

    @pl.when(core == 0)
    def _():
        mid = center(256, 512)
        store(256, 384, jnp.where(left, rolled, mid[:, :128]))
        store(384, 512, mid[:, 128:])

    @pl.when(core != 0)
    def _():
        store(256, 384, jnp.where(left, rolled, jnp.zeros_like(rolled)))
        store(384, 512, center(512, 640))


def x_term(place, prev_ok, next_ok, own, sib, halo):
    smem = pl.BlockSpec(memory_space=pltpu.SMEM)
    vmem = pl.BlockSpec(memory_space=pltpu.VMEM)
    chips, frames, strip, _ = own.shape
    buf = pltpu.VMEM((chips * frames * strip, 384), jnp.bfloat16)
    return pl.pallas_call(
        term_kernel,
        out_shape=jax.ShapeDtypeStruct((320, 512), jnp.float32),
        in_specs=[smem] * 3 + [vmem] * 3,
        out_specs=vmem,
        scratch_shapes=[buf, buf],
        compiler_params=pltpu.CompilerParams(vmem_limit_bytes=48 << 20),
        name="x_term",
    )(place, prev_ok, next_ok, own, sib, halo)


def out_kernel(place_ref, prev_ref, next_ref, f_ref, g_ref, skip_ref, halo_ref, edge_ref, own_ref, sib_ref, out_ref, back_ref, f_lo, f_hi, g_lo, g_hi):
    frames, strip, width = f_ref.shape
    tokens = frames * strip
    core, at = place_ref[0], place_ref[1]

    def put(dst, j, value, ok):
        dst[pl.ds(j * strip, strip), :] = jnp.where(ok != 0, value, jnp.zeros_like(value))

    for src, lo, hi, lanes in ((f_ref, f_lo, f_hi, slice(0, width)), (g_ref, g_lo, g_hi, slice(width, 2 * width))):
        halo, edge = halo_ref[:, lanes], edge_ref[:, lanes]
        for j in range(frames):
            put(lo, j, jnp.where(core == 0, halo, edge) if j == 0 else src[j - 1], prev_ref[at + j])
            put(hi, j, jnp.where(core == 0, edge, halo) if j == frames - 1 else src[j + 1], next_ref[at + j])

    def run(low, high):
        def dot(a, b):
            return jnp.dot(a, b, preferred_element_type=jnp.float32)

        def dot_t(a, b):
            return lax.dot_general(a, b, (((1,), (1,)), ((), ())), preferred_element_type=jnp.float32)

        f = f_ref[...].reshape(tokens, width)
        g = g_ref[...].reshape(tokens, width)
        for lanes, center in ((slice(0, 384), low[:, 640:1024]), (slice(384, 640), high[:, 128:384])):
            outer = slice(384 + lanes.start, 384 + lanes.stop)
            mixed = dot(f_lo[...], low[:, lanes]) + dot(f, center) + dot(f_hi[...], high[:, outer])
            mixed = mixed.reshape(frames, strip, -1) + skip_ref[:, :, lanes].astype(jnp.float32)
            out_ref[:, :, lanes] = mixed.astype(jnp.bfloat16)
        back = dot_t(g_hi[...], low[:, :640]) + dot_t(g[:, :384], low[:, 640:1024])
        back = back + dot_t(g[:, 384:], high[:, 128:384]) + dot_t(g_lo[...], high[:, 384:])
        back_ref[...] = back.reshape(frames, strip, width).astype(jnp.bfloat16)

    @pl.when(core == 0)
    def _():
        run(own_ref, sib_ref)

    @pl.when(core != 0)
    def _():
        run(sib_ref, own_ref)


def outputs(place, prev_ok, next_ok, features, cotangent, skip_input, halo, edge, weight_own, weight_sib):
    frames, strip, width = features.shape
    smem = pl.BlockSpec(memory_space=pltpu.SMEM)
    vmem = pl.BlockSpec(memory_space=pltpu.VMEM)
    buf = pltpu.VMEM((frames * strip, width), jnp.bfloat16)
    out = jax.ShapeDtypeStruct(features.shape, jnp.bfloat16)
    return pl.pallas_call(
        out_kernel,
        out_shape=(out, out),
        in_specs=[smem] * 3 + [vmem] * 7,
        out_specs=(vmem, vmem),
        scratch_shapes=[buf] * 4,
        compiler_params=pltpu.CompilerParams(vmem_limit_bytes=48 << 20),
        name="outputs",
    )(place, prev_ok, next_ok, features, cotangent, skip_input, halo, edge, weight_own, weight_sib)


def shards(features, skip_input, cotangent, temporal_weight, clip_lengths, cycle_start):
    frames, strip, width = features.shape
    core, xl, xh, z = [lax.axis_index(a) for a in ("c", "xl", "xh", "z")]
    n_x, n_y, n_z = lax.axis_size(X), lax.axis_size("y"), lax.axis_size("z")
    n_dp = lax.axis_size(DP)
    total_frames = frames * n_dp

    weight_half = lax.dynamic_slice_in_dim(temporal_weight, core * 896, 1024, axis=1)
    weight_half = lax.all_gather(weight_half, FSDP, axis=0, tiled=True)

    both = [(0, 1), (1, 0)]
    own = lax.all_to_all(pack(features, cotangent), X, 0, 0, tiled=True).reshape(n_x, frames, strip, width)
    ends = [jnp.concatenate([features[i], cotangent[i]], axis=1) for i in (0, -1)]
    sib_edge = lax.ppermute(jnp.where(core == 0, ends[1], ends[0]), "c", both)
    across = [(d, (d - 1) % n_dp if d % 2 == 0 else (d + 1) % n_dp) for d in range(n_dp)]
    halo = lax.ppermute(jnp.where(core == 0, ends[0], ends[1]), DP, across)
    own, halo, sib_edge = lax.optimization_barrier((own, halo, sib_edge))
    sib = lax.ppermute(own, "c", both)
    z_next = [(2 * i, (2 * i - 1) % (2 * n_z)) for i in range(n_z)] + [(2 * i + 1, (2 * i + 2) % (2 * n_z)) for i in range(n_z)]
    edge = jnp.where(core == 0, own[:, 0, :, :384], own[:, -1, :, :384])
    halo_x = lax.ppermute(edge, ("z", "c"), z_next)

    first = (jnp.arange(2, dtype=jnp.int32) * n_z + z)[:, None] * (2 * frames)
    chip_frames = (first + jnp.arange(2 * frames, dtype=jnp.int32)).reshape(-1)
    prev_all, next_all = border_flags(clip_lengths, cycle_start, chip_frames, total_frames)
    wrapped = jnp.where(core == 0, z == 0, z == n_z - 1)
    place = jnp.stack([core, xl, wrapped.astype(jnp.int32)]).astype(jnp.int32)
    term = x_term(place, prev_all, next_all, own, sib, halo_x)

    part = lax.all_to_all(term.reshape(n_y, 320 // n_y, 512), "y", 0, 0, tiled=True).sum(0)
    local_rows = part.shape[0]
    blocks = jnp.pad(part, ((0, 48 - local_rows), (0, 0))).reshape(6, 8, 2, 256).transpose(0, 2, 1, 3)
    mine = lax.all_to_all(blocks.reshape(n_z, 8, 256), "z", 0, 0, tiled=True).sum(0)
    mine = mine / jnp.sqrt(jnp.float32(total_frames * strip * lax.axis_size(FSDP)))
    mine, weight_half = lax.optimization_barrier((mine, weight_half))
    weight_sib = lax.ppermute(weight_half, "c", both)
    n_xz = 2 * n_z
    gathered = lax.all_to_all(jnp.broadcast_to(mine[None], (n_xz, 8, 256)), ("xh", "z"), 0, 0, tiled=True)
    place_out = jnp.stack([core, xh * (2 * frames) + core * frames]).astype(jnp.int32)
    block_out, grad_features = outputs(
        place_out, prev_all, next_all, features, cotangent, skip_input, halo, sib_edge, weight_half, weight_sib
    )
    gathered, block_out, grad_features = lax.optimization_barrier((gathered, block_out, grad_features))
    other = lax.ppermute(gathered, "c", both)

    def flat(a):
        a = a.reshape(2, 6, 2, 8, 256).transpose(0, 1, 3, 2, 4)
        return a.reshape(2, 48, 512)[:, :local_rows]

    low = flat(jnp.where(core == 0, gathered, other))
    high = flat(jnp.where(core == 0, other, gathered))

    def outer_tap(b):
        return [b[0, :, :320], b[1, :, 256:320], b[1, :, :256]]

    tap_1 = [low[0, :, 384:], high[0, :, 384:], low[0, :, 320:384], low[1, :, 320:], high[1, :, 384:]]
    grad_weight = jnp.concatenate(outer_tap(low) + tap_1 + outer_tap(high), axis=1)

    return (block_out, grad_features, grad_weight)


def solution(mesh):
    split = Mesh(mesh.devices.reshape(2, 12, 2, 2, 8), DP + FSDP)
    tokens = P(DP, FSDP, None)
    in_specs = (tokens, tokens, tokens, P(FSDP, None), P(), P())
    out_specs = (tokens, tokens, P(FSDP, None))
    return jax.shard_map(shards, mesh=split, in_specs=in_specs, out_specs=out_specs, check_vma=False)
```

```python
import jax
import jax.numpy as jnp
from jax import lax
from jax.experimental import pallas as pl
from jax.experimental.pallas import tpu as pltpu
from jax.sharding import Mesh, PartitionSpec as P

DP = ("xh", "z", "c")
FSDP = ("xl", "y")
X = ("xh", "xl")


def border_flags(clip_lengths, cycle_start, frame_index, total):
    starts = jnp.cumsum(clip_lengths) - clip_lengths
    position = jnp.mod(frame_index - cycle_start[0], total)
    following = jnp.mod(frame_index + 1 - cycle_start[0], total)
    first_here = jnp.any(position[:, None] == starts[None, :], axis=1)
    first_next = jnp.any(following[:, None] == starts[None, :], axis=1)
    return (1 - first_here.astype(jnp.int32), 1 - first_next.astype(jnp.int32))


def pack_kernel(f_ref, g_ref, out_ref):
    frames, strip, width = f_ref.shape
    f = f_ref[...].reshape(frames * strip, width)
    g = g_ref[...].reshape(frames * strip, width)
    f_mid, g_mid = f[:, 256:384], g[:, 256:384]
    f_rolled, g_rolled = [pltpu.roll(m.astype(jnp.float32), 64, 1).astype(jnp.bfloat16) for m in (f_mid, g_mid)]
    left = lax.broadcasted_iota(jnp.int32, f_mid.shape, 1) < 64
    for xh in range(2):
        for xl in range(2):
            j = 2 * xh + xl
            out_ref[j, :, :256] = f[:, 384 * xl:384 * xl + 256]
            out_ref[j, :, 256:384] = jnp.where(left, f_rolled if xl else f_mid, g_mid if xh else g_rolled)
            out_ref[j, :, 384:] = g[:, 384 * xh:384 * xh + 256]


def pack(features, cotangent):
    frames, strip, width = features.shape
    steps = 4
    block = pl.BlockSpec((frames // steps, strip, width), lambda i: (i, 0, 0))
    return pl.pallas_call(
        pack_kernel,
        out_shape=jax.ShapeDtypeStruct((4, frames * strip, width), jnp.bfloat16),
        grid=(steps,),
        in_specs=[block] * 2,
        out_specs=pl.BlockSpec((4, frames * strip // steps, width), lambda i: (0, i, 0)),
        compiler_params=pltpu.CompilerParams(vmem_limit_bytes=48 << 20),
        name="pack",
    )(features, cotangent)


def term_kernel(place_ref, prev_ref, next_ref, own_ref, sib_ref, halo_ref, out_ref, fa_own, fa_sib):
    chips, frames, strip, _ = own_ref.shape
    core, xl, wrapped = place_ref[0], place_ref[1], place_ref[2]

    def put(dst, chip, slot, value, ok):
        dst[pl.ds((chip * frames + slot) * strip, strip), :] = jnp.where(ok != 0, value, jnp.zeros_like(value))

    def halo(chip):
        return halo_ref[(chip // 2 + wrapped) % 2 * 2 + chip % 2]

    @pl.when(core == 0)
    def _():
        for chip in range(chips):
            at = chip // 2 * 2 * frames
            for j in range(frames):
                mine = halo(chip) if j == 0 else own_ref[chip, j - 1, :, :384]
                its = own_ref[chip, frames - 1, :, :384] if j == 0 else sib_ref[chip, j - 1, :, :384]
                put(fa_own, chip, j, mine, prev_ref[at + j])
                put(fa_sib, chip, j, its, prev_ref[at + frames + j])

    @pl.when(core != 0)
    def _():
        for chip in range(chips):
            at = chip // 2 * 2 * frames
            for j in range(frames):
                mine = halo(chip) if j == frames - 1 else own_ref[chip, j + 1, :, :384]
                its = own_ref[chip, 0, :, :384] if j == frames - 1 else sib_ref[chip, j + 1, :, :384]
                put(fa_own, chip, j, mine, next_ref[at + frames + j])
                put(fa_sib, chip, j, its, next_ref[at + j])

    def flat(ref, start, stop):
        return ref[:, :, :, start:stop].reshape(chips * frames * strip, stop - start)

    def dot(a, b):
        return lax.dot_general(a, b, (((0,), (0,)), ((), ())), preferred_element_type=jnp.float32)

    def center(start, stop):
        return dot(flat(own_ref, 0, 384), flat(own_ref, start, stop)) + dot(flat(sib_ref, 0, 384), flat(sib_ref, start, stop))

    outer = dot(fa_own[...], flat(own_ref, 256, 640)) + dot(fa_sib[...], flat(sib_ref, 256, 640))
    left = lax.broadcasted_iota(jnp.int32, (384, 128), 1) < 64
    rolled = pltpu.roll(outer[:, :128], 64, 1)

    def store(start, stop, value):
        @pl.when(xl == 0)
        def _():
            out_ref[:, start:stop] = value[:320]

        @pl.when(xl != 0)
        def _():
            out_ref[64:, start:stop] = value[:256]
            out_ref[:64, start:stop] = value[256:320]

    store(0, 256, outer[:, 128:])

    @pl.when(core == 0)
    def _():
        mid = center(256, 512)
        store(256, 384, jnp.where(left, rolled, mid[:, :128]))
        store(384, 512, mid[:, 128:])

    @pl.when(core != 0)
    def _():
        store(256, 384, jnp.where(left, rolled, jnp.zeros_like(rolled)))
        store(384, 512, center(512, 640))


def x_term(place, prev_ok, next_ok, own, sib, halo):
    smem = pl.BlockSpec(memory_space=pltpu.SMEM)
    vmem = pl.BlockSpec(memory_space=pltpu.VMEM)
    chips, frames, strip, _ = own.shape
    buf = pltpu.VMEM((chips * frames * strip, 384), jnp.bfloat16)
    return pl.pallas_call(
        term_kernel,
        out_shape=jax.ShapeDtypeStruct((320, 512), jnp.float32),
        in_specs=[smem] * 3 + [vmem] * 3,
        out_specs=vmem,
        scratch_shapes=[buf, buf],
        compiler_params=pltpu.CompilerParams(vmem_limit_bytes=48 << 20),
        name="x_term",
    )(place, prev_ok, next_ok, own, sib, halo)


def out_kernel(place_ref, prev_ref, next_ref, f_ref, g_ref, skip_ref, halo_ref, edge_ref, weight, out_ref, back_ref, f_lo, f_hi, g_lo, g_hi):
    frames, strip, width = f_ref.shape
    tokens = frames * strip
    core, at = place_ref[0], place_ref[1]

    def put(dst, j, value, ok):
        dst[pl.ds(j * strip, strip), :] = jnp.where(ok != 0, value, jnp.zeros_like(value))

    for src, lo, hi, lanes in ((f_ref, f_lo, f_hi, slice(0, width)), (g_ref, g_lo, g_hi, slice(width, 2 * width))):
        halo, edge = halo_ref[:, lanes], edge_ref[:, lanes]
        for j in range(frames):
            put(lo, j, jnp.where(core == 0, halo, edge) if j == 0 else src[j - 1], prev_ref[at + j])
            put(hi, j, jnp.where(core == 0, edge, halo) if j == frames - 1 else src[j + 1], next_ref[at + j])

    def dot(a, b):
        return jnp.dot(a, b, preferred_element_type=jnp.float32)

    def dot_t(a, b):
        return lax.dot_general(a, b, (((1,), (1,)), ((), ())), preferred_element_type=jnp.float32)

    f = f_ref[...].reshape(tokens, width)
    g = g_ref[...].reshape(tokens, width)
    taps = [weight[:, k * width:(k + 1) * width] for k in range(3)]
    mixed = dot(f_lo[...], taps[0]) + dot(f, taps[1]) + dot(f_hi[...], taps[2])
    mixed = mixed.reshape(frames, strip, width) + skip_ref[...].astype(jnp.float32)
    out_ref[...] = mixed.astype(jnp.bfloat16)
    back = dot_t(g_hi[...], taps[0]) + dot_t(g, taps[1]) + dot_t(g_lo[...], taps[2])
    back_ref[...] = back.reshape(frames, strip, width).astype(jnp.bfloat16)


def outputs(place, prev_ok, next_ok, features, cotangent, skip_input, halo, edge, weight):
    frames, strip, width = features.shape
    smem = pl.BlockSpec(memory_space=pltpu.SMEM)
    vmem = pl.BlockSpec(memory_space=pltpu.VMEM)
    buf = pltpu.VMEM((frames * strip, width), jnp.bfloat16)
    out = jax.ShapeDtypeStruct(features.shape, jnp.bfloat16)
    return pl.pallas_call(
        out_kernel,
        out_shape=(out, out),
        in_specs=[smem] * 3 + [vmem] * 6,
        out_specs=(vmem, vmem),
        scratch_shapes=[buf] * 4,
        compiler_params=pltpu.CompilerParams(vmem_limit_bytes=48 << 20),
        name="outputs",
    )(place, prev_ok, next_ok, features, cotangent, skip_input, halo, edge, weight)


def shards(features, skip_input, cotangent, temporal_weight, clip_lengths, cycle_start):
    frames, strip, width = features.shape
    core, xl, xh, z = [lax.axis_index(a) for a in ("c", "xl", "xh", "z")]
    n_x, n_y, n_z = lax.axis_size(X), lax.axis_size("y"), lax.axis_size("z")
    n_dp = lax.axis_size(DP)
    total_frames = frames * n_dp

    weight_all = lax.all_gather(temporal_weight, FSDP, axis=0, tiled=True)

    both = [(0, 1), (1, 0)]
    own = lax.all_to_all(pack(features, cotangent), X, 0, 0, tiled=True).reshape(n_x, frames, strip, width)
    first = (jnp.arange(2, dtype=jnp.int32) * n_z + z)[:, None] * (2 * frames)
    chip_frames = (first + jnp.arange(2 * frames, dtype=jnp.int32)).reshape(-1)
    prev_all, next_all = border_flags(clip_lengths, cycle_start, chip_frames, total_frames)
    own, prev_all, next_all = lax.optimization_barrier((own, prev_all, next_all))
    sib = lax.ppermute(own, "c", both)
    z_next = [(2 * i, (2 * i - 1) % (2 * n_z)) for i in range(n_z)] + [(2 * i + 1, (2 * i + 2) % (2 * n_z)) for i in range(n_z)]
    edge = jnp.where(core == 0, own[:, 0, :, :384], own[:, -1, :, :384])
    halo_x = lax.ppermute(edge, ("z", "c"), z_next)

    wrapped = jnp.where(core == 0, z == 0, z == n_z - 1)
    place = jnp.stack([core, xl, wrapped.astype(jnp.int32)]).astype(jnp.int32)
    term = x_term(place, prev_all, next_all, own, sib, halo_x)

    _, features, cotangent = lax.optimization_barrier((term, features, cotangent))
    ends = [jnp.concatenate([features[i], cotangent[i]], axis=1) for i in (0, -1)]
    sib_edge = lax.ppermute(jnp.where(core == 0, ends[1], ends[0]), "c", both)
    across = [(d, (d - 1) % n_dp if d % 2 == 0 else (d + 1) % n_dp) for d in range(n_dp)]
    halo = lax.ppermute(jnp.where(core == 0, ends[0], ends[1]), DP, across)
    part = lax.all_to_all(term.reshape(n_y, 320 // n_y, 512), "y", 0, 0, tiled=True)
    part, halo, sib_edge = lax.optimization_barrier((part, halo, sib_edge))
    part = part.sum(0)
    local_rows = part.shape[0]
    blocks = jnp.pad(part, ((0, 48 - local_rows), (0, 0))).reshape(6, 8, 2, 256).transpose(0, 2, 1, 3)
    mine = lax.all_to_all(blocks.reshape(n_z, 8, 256), "z", 0, 0, tiled=True).sum(0)
    mine = mine / jnp.sqrt(jnp.float32(total_frames * strip * lax.axis_size(FSDP)))
    _, weight_all = lax.optimization_barrier((mine, weight_all))
    n_xz = 2 * n_z
    gathered = lax.all_to_all(jnp.broadcast_to(mine[None], (n_xz, 8, 256)), ("xh", "z"), 0, 0, tiled=True)
    place_out = jnp.stack([core, xh * (2 * frames) + core * frames]).astype(jnp.int32)
    block_out, grad_features = outputs(
        place_out, prev_all, next_all, features, cotangent, skip_input, halo, sib_edge, weight_all
    )
    gathered, block_out, grad_features = lax.optimization_barrier((gathered, block_out, grad_features))
    other = lax.ppermute(gathered, "c", both)

    def flat(a):
        a = a.reshape(2, 6, 2, 8, 256).transpose(0, 1, 3, 2, 4)
        return a.reshape(2, 48, 512)[:, :local_rows]

    low = flat(jnp.where(core == 0, gathered, other))
    high = flat(jnp.where(core == 0, other, gathered))

    def outer_tap(b):
        return [b[0, :, :320], b[1, :, 256:320], b[1, :, :256]]

    tap_1 = [low[0, :, 384:], high[0, :, 384:], low[0, :, 320:384], low[1, :, 320:], high[1, :, 384:]]
    grad_weight = jnp.concatenate(outer_tap(low) + tap_1 + outer_tap(high), axis=1)

    return (block_out, grad_features, grad_weight)


def solution(mesh):
    split = Mesh(mesh.devices.reshape(2, 12, 2, 2, 8), DP + FSDP)
    tokens = P(DP, FSDP, None)
    in_specs = (tokens, tokens, tokens, P(FSDP, None), P(), P())
    out_specs = (tokens, tokens, P(FSDP, None))
    return jax.shard_map(shards, mesh=split, in_specs=in_specs, out_specs=out_specs, check_vma=False)
```

```python
import jax
import jax.numpy as jnp
from jax import lax
from jax.experimental import pallas as pl
from jax.experimental.pallas import tpu as pltpu
from jax.sharding import Mesh, PartitionSpec as P

DP = ("xh", "z", "c")
FSDP = ("xl", "y")
X = ("xh", "xl")


def border_flags(clip_lengths, cycle_start, frame_index, total):
    starts = jnp.cumsum(clip_lengths) - clip_lengths
    position = jnp.mod(frame_index - cycle_start[0], total)
    following = jnp.mod(frame_index + 1 - cycle_start[0], total)
    first_here = jnp.any(position[:, None] == starts[None, :], axis=1)
    first_next = jnp.any(following[:, None] == starts[None, :], axis=1)
    return (1 - first_here.astype(jnp.int32), 1 - first_next.astype(jnp.int32))


def pack_kernel(f_hbm, g_hbm, out_hbm, f_ref, g_ref, out_ref, in_sems, out_sems):
    steps = f_ref.shape[0]
    frames, strip, width = f_ref.shape[1:]
    rows = frames * strip

    def fetch(i):
        return [
            pltpu.make_async_copy(src.at[pl.ds(i * frames, frames)], dst.at[i], in_sems.at[i, k])
            for k, (src, dst) in enumerate(((f_hbm, f_ref), (g_hbm, g_ref)))
        ]

    def send(i):
        return pltpu.make_async_copy(out_ref.at[i], out_hbm.at[:, pl.ds(i * rows, rows), :], out_sems.at[i])

    for i in range(steps):
        for copy in fetch(i):
            copy.start()
    for i in range(steps):
        for copy in fetch(i):
            copy.wait()
        f = f_ref[i].reshape(rows, width)
        g = g_ref[i].reshape(rows, width)
        f_mid, g_mid = f[:, 256:384], g[:, 256:384]
        f_rolled, g_rolled = [pltpu.roll(m.astype(jnp.float32), 64, 1).astype(jnp.bfloat16) for m in (f_mid, g_mid)]
        left = lax.broadcasted_iota(jnp.int32, f_mid.shape, 1) < 64
        for xh in range(2):
            for xl in range(2):
                j = 2 * xh + xl
                out_ref[i, j, :, :256] = f[:, 384 * xl:384 * xl + 256]
                out_ref[i, j, :, 256:384] = jnp.where(left, f_rolled if xl else f_mid, g_mid if xh else g_rolled)
                out_ref[i, j, :, 384:] = g[:, 384 * xh:384 * xh + 256]
        send(i).start()
    for i in range(steps):
        send(i).wait()


def pack(features, cotangent):
    frames, strip, width = features.shape
    steps = 2
    hbm = pl.BlockSpec(memory_space=pltpu.HBM)
    part = pltpu.VMEM((steps, frames // steps, strip, width), jnp.bfloat16)
    return pl.pallas_call(
        pack_kernel,
        out_shape=jax.ShapeDtypeStruct((4, frames * strip, width), jnp.bfloat16),
        in_specs=[hbm] * 2,
        out_specs=hbm,
        scratch_shapes=[
            part, part, pltpu.VMEM((steps, 4, frames * strip // steps, width), jnp.bfloat16),
            pltpu.SemaphoreType.DMA((steps, 2)), pltpu.SemaphoreType.DMA((steps,)),
        ],
        compiler_params=pltpu.CompilerParams(vmem_limit_bytes=48 << 20),
        name="pack",
    )(features, cotangent)


def term_kernel(place_ref, prev_ref, next_ref, own_ref, sib_ref, halo_ref, out_ref, fa_own, fa_sib):
    chips, frames, strip, _ = own_ref.shape
    core, xl, wrapped = place_ref[0], place_ref[1], place_ref[2]

    def put(dst, chip, slot, value, ok):
        dst[pl.ds((chip * frames + slot) * strip, strip), :] = jnp.where(ok != 0, value, jnp.zeros_like(value))

    def halo(chip):
        return halo_ref[(chip // 2 + wrapped) % 2 * 2 + chip % 2]

    @pl.when(core == 0)
    def _():
        for chip in range(chips):
            at = chip // 2 * 2 * frames
            for j in range(frames):
                mine = halo(chip) if j == 0 else own_ref[chip, j - 1, :, :384]
                its = own_ref[chip, frames - 1, :, :384] if j == 0 else sib_ref[chip, j - 1, :, :384]
                put(fa_own, chip, j, mine, prev_ref[at + j])
                put(fa_sib, chip, j, its, prev_ref[at + frames + j])

    @pl.when(core != 0)
    def _():
        for chip in range(chips):
            at = chip // 2 * 2 * frames
            for j in range(frames):
                mine = halo(chip) if j == frames - 1 else own_ref[chip, j + 1, :, :384]
                its = own_ref[chip, 0, :, :384] if j == frames - 1 else sib_ref[chip, j + 1, :, :384]
                put(fa_own, chip, j, mine, next_ref[at + frames + j])
                put(fa_sib, chip, j, its, next_ref[at + j])

    def flat(ref, start, stop):
        return ref[:, :, :, start:stop].reshape(chips * frames * strip, stop - start)

    def dot(a, b):
        return lax.dot_general(a, b, (((0,), (0,)), ((), ())), preferred_element_type=jnp.float32)

    def center(start, stop):
        return dot(flat(own_ref, 0, 384), flat(own_ref, start, stop)) + dot(flat(sib_ref, 0, 384), flat(sib_ref, start, stop))

    outer = dot(fa_own[...], flat(own_ref, 256, 640)) + dot(fa_sib[...], flat(sib_ref, 256, 640))
    left = lax.broadcasted_iota(jnp.int32, (384, 128), 1) < 64
    rolled = pltpu.roll(outer[:, :128], 64, 1)

    def store(start, stop, value):
        @pl.when(xl == 0)
        def _():
            out_ref[:, start:stop] = value[:320]

        @pl.when(xl != 0)
        def _():
            out_ref[64:, start:stop] = value[:256]
            out_ref[:64, start:stop] = value[256:320]

    store(0, 256, outer[:, 128:])

    @pl.when(core == 0)
    def _():
        mid = center(256, 512)
        store(256, 384, jnp.where(left, rolled, mid[:, :128]))
        store(384, 512, mid[:, 128:])

    @pl.when(core != 0)
    def _():
        store(256, 384, jnp.where(left, rolled, jnp.zeros_like(rolled)))
        store(384, 512, center(512, 640))


def x_term(place, prev_ok, next_ok, own, sib, halo):
    smem = pl.BlockSpec(memory_space=pltpu.SMEM)
    vmem = pl.BlockSpec(memory_space=pltpu.VMEM)
    chips, frames, strip, _ = own.shape
    buf = pltpu.VMEM((chips * frames * strip, 384), jnp.bfloat16)
    return pl.pallas_call(
        term_kernel,
        out_shape=jax.ShapeDtypeStruct((320, 512), jnp.float32),
        in_specs=[smem] * 3 + [vmem] * 3,
        out_specs=vmem,
        scratch_shapes=[buf, buf],
        compiler_params=pltpu.CompilerParams(vmem_limit_bytes=48 << 20),
        name="x_term",
    )(place, prev_ok, next_ok, own, sib, halo)


def out_kernel(place_ref, prev_ref, next_ref, f_ref, g_ref, skip_ref, halo_ref, edge_ref, *refs):
    weights, (out_ref, back_ref, f_lo, f_hi, g_lo, g_hi, blocks, weight) = refs[:4], refs[4:]
    frames, strip, width = f_ref.shape
    tokens = frames * strip
    core, at, xl, y = [place_ref[i] for i in range(4)]
    count, rows = weights[0].shape[:2]

    def put(dst, j, value, ok):
        dst[pl.ds(j * strip, strip), :] = jnp.where(ok != 0, value, jnp.zeros_like(value))

    for src, lo, hi, lanes in ((f_ref, f_lo, f_hi, slice(0, width)), (g_ref, g_lo, g_hi, slice(width, 2 * width))):
        halo, edge = halo_ref[:, lanes], edge_ref[:, lanes]
        for j in range(frames):
            put(lo, j, jnp.where(core == 0, halo, edge) if j == 0 else src[j - 1], prev_ref[at + j])
            put(hi, j, jnp.where(core == 0, edge, halo) if j == frames - 1 else src[j + 1], next_ref[at + j])

    for i in range(count):
        for half in range(2):
            blocks[half, core * count + i] = weights[half][i]
            blocks[half, (1 - core) * count + i] = weights[2 + half][i]
    for half in range(2):
        for i in range(2 * count):
            start = (half * 2 * count + i) * rows
            weight[start:start + rows, :] = blocks[(half + xl) % 2, (y - i + 2 * count) % (2 * count)]

    def dot(a, b):
        return jnp.dot(a, b, preferred_element_type=jnp.float32)

    def dot_t(a, b):
        return lax.dot_general(a, b, (((1,), (1,)), ((), ())), preferred_element_type=jnp.float32)

    f = f_ref[...].reshape(tokens, width)
    g = g_ref[...].reshape(tokens, width)
    taps = [weight[:, k * width:(k + 1) * width] for k in range(3)]
    mixed = dot(f_lo[...], taps[0]) + dot(f, taps[1]) + dot(f_hi[...], taps[2])
    mixed = mixed.reshape(frames, strip, width) + skip_ref[...].astype(jnp.float32)
    out_ref[...] = mixed.astype(jnp.bfloat16)
    back = dot_t(g_hi[...], taps[0]) + dot_t(g, taps[1]) + dot_t(g_lo[...], taps[2])
    back_ref[...] = back.reshape(frames, strip, width).astype(jnp.bfloat16)


def outputs(place, prev_ok, next_ok, features, cotangent, skip_input, halo, edge, *weights):
    frames, strip, width = features.shape
    smem = pl.BlockSpec(memory_space=pltpu.SMEM)
    vmem = pl.BlockSpec(memory_space=pltpu.VMEM)
    buf = pltpu.VMEM((frames * strip, width), jnp.bfloat16)
    out = jax.ShapeDtypeStruct(features.shape, jnp.bfloat16)
    return pl.pallas_call(
        out_kernel,
        out_shape=(out, out),
        in_specs=[smem] * 3 + [vmem] * 9,
        out_specs=(vmem, vmem),
        scratch_shapes=[buf] * 4 + [pltpu.VMEM((2, 8, 40, 3 * width), jnp.bfloat16), pltpu.VMEM((width, 3 * width), jnp.bfloat16)],
        compiler_params=pltpu.CompilerParams(vmem_limit_bytes=48 << 20),
        name="outputs",
    )(place, prev_ok, next_ok, features, cotangent, skip_input, halo, edge, *weights)


def shards(features, skip_input, cotangent, temporal_weight, clip_lengths, cycle_start):
    frames, strip, width = features.shape
    core, xl, xh, z, y = [lax.axis_index(a) for a in ("c", "xl", "xh", "z", "y")]
    n_x, n_y, n_z = lax.axis_size(X), lax.axis_size("y"), lax.axis_size("z")
    n_dp = lax.axis_size(DP)
    total_frames = frames * n_dp

    def from_y(k):
        far = [(n_y + i, n_y + (i - k) % n_y) for i in range(n_y)]
        near = [(i, (i + k) % n_y) for i in range(n_y)]
        return lax.ppermute(temporal_weight, ("c", "y"), far if 2 * k == n_y else near + far)

    w_1, w_2, w_3, w_4 = [from_y(k) for k in (1, 2, 3, 4)]

    both = [(0, 1), (1, 0)]
    own = lax.all_to_all(pack(features, cotangent), X, 0, 0, tiled=True).reshape(n_x, frames, strip, width)
    own, w_1, w_2, w_3, w_4 = lax.optimization_barrier((own, w_1, w_2, w_3, w_4))
    sib = lax.ppermute(own, "c", both)
    z_next = [(2 * i, (2 * i - 1) % (2 * n_z)) for i in range(n_z)] + [(2 * i + 1, (2 * i + 2) % (2 * n_z)) for i in range(n_z)]
    edge = jnp.where(core == 0, own[:, 0, :, :384], own[:, -1, :, :384])
    halo_x = lax.ppermute(edge, ("z", "c"), z_next)

    _, clip_lengths, cycle_start = lax.optimization_barrier((edge, clip_lengths, cycle_start))
    first = (jnp.arange(2, dtype=jnp.int32) * n_z + z)[:, None] * (2 * frames)
    chip_frames = (first + jnp.arange(2 * frames, dtype=jnp.int32)).reshape(-1)
    prev_all, next_all = border_flags(clip_lengths, cycle_start, chip_frames, total_frames)
    wrapped = jnp.where(core == 0, z == 0, z == n_z - 1)
    place = jnp.stack([core, xl, wrapped.astype(jnp.int32)]).astype(jnp.int32)
    term = x_term(place, prev_all, next_all, own, sib, halo_x)

    _, features, cotangent = lax.optimization_barrier((term, features, cotangent))
    ends = [jnp.concatenate([features[i], cotangent[i]], axis=1) for i in (0, -1)]
    sib_edge = lax.ppermute(jnp.where(core == 0, ends[1], ends[0]), "c", both)
    across = [(d, (d - 1) % n_dp if d % 2 == 0 else (d + 1) % n_dp) for d in range(n_dp)]
    halo = lax.ppermute(jnp.where(core == 0, ends[0], ends[1]), DP, across)
    blocks = jnp.where(core == 0, jnp.stack([temporal_weight, w_1, w_2, w_3]), jnp.stack([w_4, w_3, w_2, w_1]))
    _, blocks = lax.optimization_barrier((term, blocks))
    blocks_far = lax.ppermute(blocks, "xl", both)
    blocks_sib = lax.ppermute(blocks, "c", both)

    part = lax.all_to_all(term.reshape(n_y, 320 // n_y, 512), "y", 0, 0, tiled=True)
    part, halo, sib_edge, blocks_far, blocks_sib = lax.optimization_barrier((part, halo, sib_edge, blocks_far, blocks_sib))
    weights = (blocks, blocks_far, blocks_sib, lax.ppermute(blocks_far, "c", both))
    part = part.sum(0)
    local_rows = part.shape[0]
    blocks = jnp.pad(part, ((0, 48 - local_rows), (0, 0))).reshape(6, 8, 2, 256).transpose(0, 2, 1, 3)
    mine = lax.all_to_all(blocks.reshape(n_z, 8, 256), "z", 0, 0, tiled=True).sum(0)
    mine = mine / jnp.sqrt(jnp.float32(total_frames * strip * lax.axis_size(FSDP)))
    _, weights = lax.optimization_barrier((mine, weights))
    n_xz = 2 * n_z
    gathered = lax.all_to_all(jnp.broadcast_to(mine[None], (n_xz, 8, 256)), ("xh", "z"), 0, 0, tiled=True)
    place_out = jnp.stack([core, xh * (2 * frames) + core * frames, xl, y]).astype(jnp.int32)
    block_out, grad_features = outputs(
        place_out, prev_all, next_all, features, cotangent, skip_input, halo, sib_edge, *weights
    )
    gathered, block_out, grad_features = lax.optimization_barrier((gathered, block_out, grad_features))
    gathered = lax.all_gather(gathered, "c")

    def flat(a):
        a = a.reshape(2, 6, 2, 8, 256).transpose(0, 1, 3, 2, 4)
        return a.reshape(2, 48, 512)[:, :local_rows]

    low, high = flat(gathered[0]), flat(gathered[1])

    def outer_tap(b):
        return [b[0, :, :320], b[1, :, 256:320], b[1, :, :256]]

    tap_1 = [low[0, :, 384:], high[0, :, 384:], low[0, :, 320:384], low[1, :, 320:], high[1, :, 384:]]
    grad_weight = jnp.concatenate(outer_tap(low) + tap_1 + outer_tap(high), axis=1)

    return (block_out, grad_features, grad_weight)


def solution(mesh):
    split = Mesh(mesh.devices.reshape(2, 12, 2, 2, 8), DP + FSDP)
    tokens = P(DP, FSDP, None)
    in_specs = (tokens, tokens, tokens, P(FSDP, None), P(), P())
    out_specs = (tokens, tokens, P(FSDP, None))
    return jax.shard_map(shards, mesh=split, in_specs=in_specs, out_specs=out_specs, check_vma=False)
```

```python
import math

import jax
import jax.numpy as jnp
from jax import lax
from jax.experimental import pallas as pl
from jax.experimental.pallas import tpu as pltpu
from jax.sharding import Mesh, PartitionSpec as P

DP = ("xh", "z", "c")
FSDP = ("xl", "y")
X = ("xh", "xl")


def border_flags(clip_lengths, cycle_start, frame_index, total):
    starts = jnp.cumsum(clip_lengths) - clip_lengths
    position = jnp.mod(frame_index - cycle_start[0], total)
    following = jnp.mod(frame_index + 1 - cycle_start[0], total)
    first_here = jnp.any(position[:, None] == starts[None, :], axis=1)
    first_next = jnp.any(following[:, None] == starts[None, :], axis=1)
    return (1 - first_here.astype(jnp.int32), 1 - first_next.astype(jnp.int32))


def pack_kernel(f_hbm, g_hbm, out_hbm, f_ref, g_ref, out_ref, in_sems, out_sems):
    steps = f_ref.shape[0]
    frames, strip, width = f_ref.shape[1:]
    rows = frames * strip

    def fetch(i):
        return [
            pltpu.make_async_copy(src.at[pl.ds(i * frames, frames)], dst.at[i], in_sems.at[i, k])
            for k, (src, dst) in enumerate(((f_hbm, f_ref), (g_hbm, g_ref)))
        ]

    def send(i):
        return pltpu.make_async_copy(out_ref.at[i], out_hbm.at[:, pl.ds(i * rows, rows), :], out_sems.at[i])

    for i in range(steps):
        for copy in fetch(i):
            copy.start()
    for i in range(steps):
        for copy in fetch(i):
            copy.wait()
        f = f_ref[i].reshape(rows, width)
        g = g_ref[i].reshape(rows, width)
        f_mid, g_mid = f[:, 256:384], g[:, 256:384]
        f_rolled, g_rolled = [pltpu.roll(m.astype(jnp.float32), 64, 1).astype(jnp.bfloat16) for m in (f_mid, g_mid)]
        left = lax.broadcasted_iota(jnp.int32, f_mid.shape, 1) < 64
        for xh in range(2):
            for xl in range(2):
                j = 2 * xh + xl
                out_ref[i, j, :, :256] = f[:, 384 * xl:384 * xl + 256]
                out_ref[i, j, :, 256:384] = jnp.where(left, f_rolled if xl else f_mid, g_mid if xh else g_rolled)
                out_ref[i, j, :, 384:] = g[:, 384 * xh:384 * xh + 256]
        send(i).start()
    for i in range(steps):
        send(i).wait()


def pack(features, cotangent):
    frames, strip, width = features.shape
    steps = 2
    hbm = pl.BlockSpec(memory_space=pltpu.HBM)
    part = pltpu.VMEM((steps, frames // steps, strip, width), jnp.bfloat16)
    return pl.pallas_call(
        pack_kernel,
        out_shape=jax.ShapeDtypeStruct((4, frames * strip, width), jnp.bfloat16),
        in_specs=[hbm] * 2,
        out_specs=hbm,
        scratch_shapes=[
            part, part, pltpu.VMEM((steps, 4, frames * strip // steps, width), jnp.bfloat16),
            pltpu.SemaphoreType.DMA((steps, 2)), pltpu.SemaphoreType.DMA((steps,)),
        ],
        compiler_params=pltpu.CompilerParams(vmem_limit_bytes=48 << 20),
        name="pack",
    )(features, cotangent)


def term_kernel(place_ref, prev_ref, next_ref, own_ref, sib_ref, halo_ref, out_ref, fa_own, fa_sib):
    chips, frames, strip, _ = own_ref.shape
    core, xl, wrapped = place_ref[0], place_ref[1], place_ref[2]

    def put(dst, chip, slot, value, ok):
        dst[pl.ds((chip * frames + slot) * strip, strip), :] = jnp.where(ok != 0, value, jnp.zeros_like(value))

    def halo(chip):
        return halo_ref[(chip // 2 + wrapped) % 2 * 2 + chip % 2]

    @pl.when(core == 0)
    def _():
        for chip in range(chips):
            at = chip // 2 * 2 * frames
            for j in range(frames):
                mine = halo(chip) if j == 0 else own_ref[chip, j - 1, :, :384]
                its = own_ref[chip, frames - 1, :, :384] if j == 0 else sib_ref[chip, j - 1, :, :384]
                put(fa_own, chip, j, mine, prev_ref[at + j])
                put(fa_sib, chip, j, its, prev_ref[at + frames + j])

    @pl.when(core != 0)
    def _():
        for chip in range(chips):
            at = chip // 2 * 2 * frames
            for j in range(frames):
                mine = halo(chip) if j == frames - 1 else own_ref[chip, j + 1, :, :384]
                its = own_ref[chip, 0, :, :384] if j == frames - 1 else sib_ref[chip, j + 1, :, :384]
                put(fa_own, chip, j, mine, next_ref[at + frames + j])
                put(fa_sib, chip, j, its, next_ref[at + j])

    def flat(ref, start, stop):
        return ref[:, :, :, start:stop].reshape(chips * frames * strip, stop - start)

    def dot(a, b):
        return lax.dot_general(a, b, (((0,), (0,)), ((), ())), preferred_element_type=jnp.float32)

    def center(start, stop):
        return dot(flat(own_ref, 0, 384), flat(own_ref, start, stop)) + dot(flat(sib_ref, 0, 384), flat(sib_ref, start, stop))

    outer = dot(fa_own[...], flat(own_ref, 256, 640)) + dot(fa_sib[...], flat(sib_ref, 256, 640))
    left = lax.broadcasted_iota(jnp.int32, (384, 128), 1) < 64
    rolled = pltpu.roll(outer[:, :128], 64, 1)

    def store(start, stop, value):
        @pl.when(xl == 0)
        def _():
            out_ref[:, start:stop] = value[:320]

        @pl.when(xl != 0)
        def _():
            out_ref[64:, start:stop] = value[:256]
            out_ref[:64, start:stop] = value[256:320]

    store(0, 256, outer[:, 128:])

    @pl.when(core == 0)
    def _():
        mid = center(256, 512)
        store(256, 384, jnp.where(left, rolled, mid[:, :128]))
        store(384, 512, mid[:, 128:])

    @pl.when(core != 0)
    def _():
        store(256, 384, jnp.where(left, rolled, jnp.zeros_like(rolled)))
        store(384, 512, center(512, 640))


def x_term(place, prev_ok, next_ok, own, sib, halo):
    smem = pl.BlockSpec(memory_space=pltpu.SMEM)
    vmem = pl.BlockSpec(memory_space=pltpu.VMEM)
    chips, frames, strip, _ = own.shape
    buf = pltpu.VMEM((chips * frames * strip, 384), jnp.bfloat16)
    return pl.pallas_call(
        term_kernel,
        out_shape=jax.ShapeDtypeStruct((320, 512), jnp.float32),
        in_specs=[smem] * 3 + [vmem] * 3,
        out_specs=vmem,
        scratch_shapes=[buf, buf],
        compiler_params=pltpu.CompilerParams(vmem_limit_bytes=48 << 20),
        name="x_term",
    )(place, prev_ok, next_ok, own, sib, halo)


def y_sum_kernel(part_ref, out_ref):
    total = part_ref[0]
    for i in range(1, part_ref.shape[0]):
        total = total + part_ref[i]
    rows = total.shape[0]
    for i in range(out_ref.shape[0]):
        row, col = i // 2 * 8, i % 2 * 256
        out_ref[i] = total[row:row + 8, col:col + 256] if row < rows else jnp.zeros((8, 256), jnp.float32)


def y_sum(part, pieces):
    vmem = pl.BlockSpec(memory_space=pltpu.VMEM)
    shape = jax.ShapeDtypeStruct((pieces, 8, 256), jnp.float32)
    return pl.pallas_call(y_sum_kernel, out_shape=shape, in_specs=[vmem], out_specs=vmem, name="y_sum")(part)


def out_kernel(place_ref, prev_ref, next_ref, f_ref, g_ref, skip_ref, halo_ref, edge_ref, *refs):
    weights, (out_ref, back_ref, f_lo, f_hi, g_lo, g_hi, blocks, weight) = refs[:4], refs[4:]
    frames, strip, width = f_ref.shape
    tokens = frames * strip
    core, at, xl, y = [place_ref[i] for i in range(4)]
    count, rows = weights[0].shape[:2]

    def put(dst, j, value, ok):
        dst[pl.ds(j * strip, strip), :] = jnp.where(ok != 0, value, jnp.zeros_like(value))

    for src, lo, hi, lanes in ((f_ref, f_lo, f_hi, slice(0, width)), (g_ref, g_lo, g_hi, slice(width, 2 * width))):
        halo, edge = halo_ref[:, lanes], edge_ref[1 - core, :, lanes]
        for j in range(frames):
            put(lo, j, jnp.where(core == 0, halo, edge) if j == 0 else src[j - 1], prev_ref[at + j])
            put(hi, j, jnp.where(core == 0, edge, halo) if j == frames - 1 else src[j + 1], next_ref[at + j])

    for i in range(count):
        for half in range(2):
            blocks[half, core * count + i] = weights[half][i]
            blocks[half, (1 - core) * count + i] = weights[2 + half][i]
    for half in range(2):
        for i in range(2 * count):
            start = (half * 2 * count + i) * rows
            weight[start:start + rows, :] = blocks[(half + xl) % 2, (y - i + 2 * count) % (2 * count)]

    def dot(a, b):
        return jnp.dot(a, b, preferred_element_type=jnp.float32)

    def dot_t(a, b):
        return lax.dot_general(a, b, (((1,), (1,)), ((), ())), preferred_element_type=jnp.float32)

    f = f_ref[...].reshape(tokens, width)
    g = g_ref[...].reshape(tokens, width)
    taps = [weight[:, k * width:(k + 1) * width] for k in range(3)]
    mixed = dot(f_lo[...], taps[0]) + dot(f, taps[1]) + dot(f_hi[...], taps[2])
    mixed = mixed.reshape(frames, strip, width) + skip_ref[...].astype(jnp.float32)
    out_ref[...] = mixed.astype(jnp.bfloat16)
    back = dot_t(g_hi[...], taps[0]) + dot_t(g, taps[1]) + dot_t(g_lo[...], taps[2])
    back_ref[...] = back.reshape(frames, strip, width).astype(jnp.bfloat16)


def outputs(place, prev_ok, next_ok, features, cotangent, skip_input, halo, edge, *weights):
    frames, strip, width = features.shape
    smem = pl.BlockSpec(memory_space=pltpu.SMEM)
    vmem = pl.BlockSpec(memory_space=pltpu.VMEM)
    buf = pltpu.VMEM((frames * strip, width), jnp.bfloat16)
    out = jax.ShapeDtypeStruct(features.shape, jnp.bfloat16)
    return pl.pallas_call(
        out_kernel,
        out_shape=(out, out),
        in_specs=[smem] * 3 + [vmem] * 9,
        out_specs=(vmem, vmem),
        scratch_shapes=[buf] * 4 + [pltpu.VMEM((2, 8, 40, 3 * width), jnp.bfloat16), pltpu.VMEM((width, 3 * width), jnp.bfloat16)],
        compiler_params=pltpu.CompilerParams(vmem_limit_bytes=48 << 20),
        name="outputs",
    )(place, prev_ok, next_ok, features, cotangent, skip_input, halo, edge, *weights)


def shards(features, skip_input, cotangent, temporal_weight, clip_lengths, cycle_start):
    frames, strip, width = features.shape
    core, xl, xh, z, y = [lax.axis_index(a) for a in ("c", "xl", "xh", "z", "y")]
    n_x, n_y, n_z = lax.axis_size(X), lax.axis_size("y"), lax.axis_size("z")
    n_dp = lax.axis_size(DP)
    total_frames = frames * n_dp

    def from_y(k):
        far = [(n_y + i, n_y + (i - k) % n_y) for i in range(n_y)]
        near = [(i, (i + k) % n_y) for i in range(n_y)]
        return lax.ppermute(temporal_weight, ("c", "y"), far if 2 * k == n_y else near + far)

    w_4, w_3, w_2, w_1 = [from_y(k) for k in (4, 3, 2, 1)]

    both = [(0, 1), (1, 0)]
    own = lax.all_to_all(pack(features, cotangent), X, 0, 0, tiled=True).reshape(n_x, frames, strip, width)
    own, w_4, w_3, w_2, w_1 = lax.optimization_barrier((own, w_4, w_3, w_2, w_1))
    sib = lax.ppermute(own, "c", both)
    z_next = [(2 * i, (2 * i - 1) % (2 * n_z)) for i in range(n_z)] + [(2 * i + 1, (2 * i + 2) % (2 * n_z)) for i in range(n_z)]
    edge = jnp.where(core == 0, own[:, 0, :, :384], own[:, -1, :, :384])
    halo_x = lax.ppermute(edge, ("z", "c"), z_next)

    _, clip_lengths, cycle_start = lax.optimization_barrier((edge, clip_lengths, cycle_start))
    first = (jnp.arange(2, dtype=jnp.int32) * n_z + z)[:, None] * (2 * frames)
    chip_frames = (first + jnp.arange(2 * frames, dtype=jnp.int32)).reshape(-1)
    prev_all, next_all = border_flags(clip_lengths, cycle_start, chip_frames, total_frames)
    wrapped = jnp.where(core == 0, z == 0, z == n_z - 1)
    place = jnp.stack([core, xl, wrapped.astype(jnp.int32)]).astype(jnp.int32)
    term = x_term(place, prev_all, next_all, own, sib, halo_x)

    _, features, cotangent = lax.optimization_barrier((term, features, cotangent))
    ends = [jnp.concatenate([features[i], cotangent[i]], axis=1) for i in (0, -1)]
    edges = lax.all_gather(jnp.where(core == 0, ends[1], ends[0]), "c")
    across = [(d, (d - 1) % n_dp if d % 2 == 0 else (d + 1) % n_dp) for d in range(n_dp)]
    halo = lax.ppermute(jnp.where(core == 0, ends[0], ends[1]), DP, across)
    blocks = jnp.where(core == 0, jnp.stack([temporal_weight, w_1, w_2, w_3]), jnp.stack([w_4, w_3, w_2, w_1]))
    _, blocks = lax.optimization_barrier((term, blocks))
    blocks_far = lax.ppermute(blocks, "xl", both)
    blocks_sib = lax.ppermute(blocks, "c", both)

    part = lax.all_to_all(term.reshape(n_y, 320 // n_y, 512), "y", 0, 0, tiled=True)
    part, halo, edges, blocks_sib = lax.optimization_barrier((part, halo, edges, blocks_sib))
    local_rows = part.shape[1]
    n_xz = 2 * n_z
    pieces = y_sum(part, n_z)
    _, blocks_far = lax.optimization_barrier((pieces, blocks_far))
    mine = lax.all_to_all(pieces, "z", 0, 0, tiled=True)
    mine = mine.sum(0) * (1.0 / math.sqrt(total_frames * strip * lax.axis_size(FSDP)))
    mine = jnp.broadcast_to(mine[None], (n_xz, 8, 256))
    weights = (blocks, blocks_far, blocks_sib, lax.ppermute(blocks_far, "c", both))
    _, weights = lax.optimization_barrier((mine, weights))
    gathered = lax.all_to_all(mine, ("xh", "z"), 0, 0, tiled=True)
    place_out = jnp.stack([core, xh * (2 * frames) + core * frames, xl, y]).astype(jnp.int32)
    block_out, grad_features = outputs(
        place_out, prev_all, next_all, features, cotangent, skip_input, halo, edges, *weights
    )
    gathered, block_out, grad_features = lax.optimization_barrier((gathered, block_out, grad_features))
    gathered = lax.all_gather(gathered, "c")

    def flat(a):
        a = a.reshape(2, 6, 2, 8, 256).transpose(0, 1, 3, 2, 4)
        return a.reshape(2, 48, 512)[:, :local_rows]

    low, high = flat(gathered[0]), flat(gathered[1])

    def outer_tap(b):
        return [b[0, :, :320], b[1, :, 256:320], b[1, :, :256]]

    tap_1 = [low[0, :, 384:], high[0, :, 384:], low[0, :, 320:384], low[1, :, 320:], high[1, :, 384:]]
    grad_weight = jnp.concatenate(outer_tap(low) + tap_1 + outer_tap(high), axis=1)

    return (block_out, grad_features, grad_weight)


def solution(mesh):
    split = Mesh(mesh.devices.reshape(2, 12, 2, 2, 8), DP + FSDP)
    tokens = P(DP, FSDP, None)
    in_specs = (tokens, tokens, tokens, P(FSDP, None), P(), P())
    out_specs = (tokens, tokens, P(FSDP, None))
    return jax.shard_map(shards, mesh=split, in_specs=in_specs, out_specs=out_specs, check_vma=False)
```

```python
import math

import jax
import jax.numpy as jnp
from jax import lax
from jax.experimental import pallas as pl
from jax.experimental.pallas import tpu as pltpu
from jax.sharding import Mesh, PartitionSpec as P

DP = ("xh", "z", "c")
FSDP = ("xl", "y")
X = ("xh", "xl")


def border_flags(clip_lengths, cycle_start, frame_index, total):
    starts = jnp.cumsum(clip_lengths) - clip_lengths
    position = jnp.mod(frame_index - cycle_start[0], total)
    following = jnp.mod(frame_index + 1 - cycle_start[0], total)
    first_here = jnp.any(position[:, None] == starts[None, :], axis=1)
    first_next = jnp.any(following[:, None] == starts[None, :], axis=1)
    return (1 - first_here.astype(jnp.int32), 1 - first_next.astype(jnp.int32))


def pack_kernel(f_hbm, g_hbm, out_hbm, f_ref, g_ref, out_ref, in_sems, out_sems):
    steps = f_ref.shape[0]
    frames, strip, width = f_ref.shape[1:]
    rows = frames * strip

    def fetch(i):
        return [
            pltpu.make_async_copy(src.at[pl.ds(i * frames, frames)], dst.at[i], in_sems.at[i, k])
            for k, (src, dst) in enumerate(((f_hbm, f_ref), (g_hbm, g_ref)))
        ]

    def send(i):
        return pltpu.make_async_copy(out_ref.at[i], out_hbm.at[:, pl.ds(i * rows, rows), :], out_sems.at[i])

    for i in range(steps):
        for copy in fetch(i):
            copy.start()
    for i in range(steps):
        for copy in fetch(i):
            copy.wait()
        f = f_ref[i].reshape(rows, width)
        g = g_ref[i].reshape(rows, width)
        f_mid, g_mid = f[:, 256:384], g[:, 256:384]
        f_rolled, g_rolled = [pltpu.roll(m.astype(jnp.float32), 64, 1).astype(jnp.bfloat16) for m in (f_mid, g_mid)]
        left = lax.broadcasted_iota(jnp.int32, f_mid.shape, 1) < 64
        for xh in range(2):
            for xl in range(2):
                j = 2 * xh + xl
                out_ref[i, j, :, :256] = f[:, 384 * xl:384 * xl + 256]
                out_ref[i, j, :, 256:384] = jnp.where(left, f_rolled if xl else f_mid, g_mid if xh else g_rolled)
                out_ref[i, j, :, 384:] = g[:, 384 * xh:384 * xh + 256]
        send(i).start()
    for i in range(steps):
        send(i).wait()


def pack(features, cotangent):
    frames, strip, width = features.shape
    steps = 2
    hbm = pl.BlockSpec(memory_space=pltpu.HBM)
    part = pltpu.VMEM((steps, frames // steps, strip, width), jnp.bfloat16)
    return pl.pallas_call(
        pack_kernel,
        out_shape=jax.ShapeDtypeStruct((4, frames * strip, width), jnp.bfloat16),
        in_specs=[hbm] * 2,
        out_specs=hbm,
        scratch_shapes=[
            part, part, pltpu.VMEM((steps, 4, frames * strip // steps, width), jnp.bfloat16),
            pltpu.SemaphoreType.DMA((steps, 2)), pltpu.SemaphoreType.DMA((steps,)),
        ],
        compiler_params=pltpu.CompilerParams(vmem_limit_bytes=48 << 20),
        name="pack",
    )(features, cotangent)


def term_kernel(place_ref, prev_ref, next_ref, own_ref, sib_ref, halo_ref, out_ref, fa_own, fa_sib):
    chips, frames, strip, _ = own_ref.shape
    core, xl, wrapped = place_ref[0], place_ref[1], place_ref[2]

    def put(dst, chip, slot, value, ok):
        dst[pl.ds((chip * frames + slot) * strip, strip), :] = jnp.where(ok != 0, value, jnp.zeros_like(value))

    def halo(chip):
        return halo_ref[(chip // 2 + wrapped) % 2 * 2 + chip % 2]

    @pl.when(core == 0)
    def _():
        for chip in range(chips):
            at = chip // 2 * 2 * frames
            for j in range(frames):
                mine = halo(chip) if j == 0 else own_ref[chip, j - 1, :, :384]
                its = own_ref[chip, frames - 1, :, :384] if j == 0 else sib_ref[chip, j - 1, :, :384]
                put(fa_own, chip, j, mine, prev_ref[at + j])
                put(fa_sib, chip, j, its, prev_ref[at + frames + j])

    @pl.when(core != 0)
    def _():
        for chip in range(chips):
            at = chip // 2 * 2 * frames
            for j in range(frames):
                mine = halo(chip) if j == frames - 1 else own_ref[chip, j + 1, :, :384]
                its = own_ref[chip, 0, :, :384] if j == frames - 1 else sib_ref[chip, j + 1, :, :384]
                put(fa_own, chip, j, mine, next_ref[at + frames + j])
                put(fa_sib, chip, j, its, next_ref[at + j])

    def flat(ref, start, stop):
        return ref[:, :, :, start:stop].reshape(chips * frames * strip, stop - start)

    def dot(a, b):
        return lax.dot_general(a, b, (((0,), (0,)), ((), ())), preferred_element_type=jnp.float32)

    def center(start, stop):
        return dot(flat(own_ref, 0, 384), flat(own_ref, start, stop)) + dot(flat(sib_ref, 0, 384), flat(sib_ref, start, stop))

    outer = dot(fa_own[...], flat(own_ref, 256, 640)) + dot(fa_sib[...], flat(sib_ref, 256, 640))
    left = lax.broadcasted_iota(jnp.int32, (384, 128), 1) < 64
    rolled = pltpu.roll(outer[:, :128], 64, 1)

    def store(start, stop, value):
        @pl.when(xl == 0)
        def _():
            out_ref[:, start:stop] = value[:320]

        @pl.when(xl != 0)
        def _():
            out_ref[64:, start:stop] = value[:256]
            out_ref[:64, start:stop] = value[256:320]

    store(0, 256, outer[:, 128:])

    @pl.when(core == 0)
    def _():
        mid = center(256, 512)
        store(256, 384, jnp.where(left, rolled, mid[:, :128]))
        store(384, 512, mid[:, 128:])

    @pl.when(core != 0)
    def _():
        store(256, 384, jnp.where(left, rolled, jnp.zeros_like(rolled)))
        store(384, 512, center(512, 640))


def x_term(place, prev_ok, next_ok, own, sib, halo):
    smem = pl.BlockSpec(memory_space=pltpu.SMEM)
    vmem = pl.BlockSpec(memory_space=pltpu.VMEM)
    chips, frames, strip, _ = own.shape
    buf = pltpu.VMEM((chips * frames * strip, 384), jnp.bfloat16)
    return pl.pallas_call(
        term_kernel,
        out_shape=jax.ShapeDtypeStruct((320, 512), jnp.float32),
        in_specs=[smem] * 3 + [vmem] * 3,
        out_specs=vmem,
        scratch_shapes=[buf, buf],
        compiler_params=pltpu.CompilerParams(vmem_limit_bytes=48 << 20),
        name="x_term",
    )(place, prev_ok, next_ok, own, sib, halo)


def y_sum_kernel(part_ref, out_ref):
    total = part_ref[0]
    for i in range(1, part_ref.shape[0]):
        total = total + part_ref[i]
    rows = total.shape[0]
    for i in range(out_ref.shape[0]):
        row, col = i // 2 * 8, i % 2 * 256
        out_ref[i] = total[row:row + 8, col:col + 256] if row < rows else jnp.zeros((8, 256), jnp.float32)


def y_sum(part, pieces):
    vmem = pl.BlockSpec(memory_space=pltpu.VMEM)
    shape = jax.ShapeDtypeStruct((pieces, 8, 256), jnp.float32)
    return pl.pallas_call(y_sum_kernel, out_shape=shape, in_specs=[vmem], out_specs=vmem, name="y_sum")(part)


def out_kernel(place_ref, prev_ref, next_ref, f_ref, g_ref, skip_ref, halo_ref, edge_ref, *refs):
    weights, (out_ref, back_ref, f_lo, f_hi, g_lo, g_hi, blocks, weight) = refs[:4], refs[4:]
    frames, strip, width = f_ref.shape
    tokens = frames * strip
    core, at, xl, y, parity = [place_ref[i] for i in range(5)]
    count, rows = weights[0].shape[:2]

    def put(dst, j, value, ok):
        dst[pl.ds(j * strip, strip), :] = jnp.where(ok != 0, value, jnp.zeros_like(value))

    for src, lo, hi, lanes in ((f_ref, f_lo, f_hi, slice(0, width)), (g_ref, g_lo, g_hi, slice(width, 2 * width))):
        halo, edge = halo_ref[:, lanes], edge_ref[1 - core, :, lanes]
        for j in range(frames):
            put(lo, j, jnp.where(core == 0, halo, edge) if j == 0 else src[j - 1], prev_ref[at + j])
            put(hi, j, jnp.where(core == 0, edge, halo) if j == frames - 1 else src[j + 1], next_ref[at + j])

    for i in range(count):
        odd = parity if i < 2 else 1 - parity
        low, high = (3 + odd, jnp.where(odd == 0, 5, 0)) if i % 2 == 0 else (1 + odd, 7 - odd)
        for half in range(2):
            blocks[half, jnp.where(core == 0, low, high)] = weights[half][i]
            blocks[half, jnp.where(core == 0, high, low)] = weights[2 + half][i]
    for half in range(2):
        for i in range(2 * count):
            start = (half * 2 * count + i) * rows
            weight[start:start + rows, :] = blocks[(half + xl) % 2, (y - i + 2 * count) % (2 * count)]

    def dot(a, b):
        return jnp.dot(a, b, preferred_element_type=jnp.float32)

    def dot_t(a, b):
        return lax.dot_general(a, b, (((1,), (1,)), ((), ())), preferred_element_type=jnp.float32)

    f = f_ref[...].reshape(tokens, width)
    g = g_ref[...].reshape(tokens, width)
    taps = [weight[:, k * width:(k + 1) * width] for k in range(3)]
    mixed = dot(f_lo[...], taps[0]) + dot(f, taps[1]) + dot(f_hi[...], taps[2])
    mixed = mixed.reshape(frames, strip, width) + skip_ref[...].astype(jnp.float32)
    out_ref[...] = mixed.astype(jnp.bfloat16)
    back = dot_t(g_hi[...], taps[0]) + dot_t(g, taps[1]) + dot_t(g_lo[...], taps[2])
    back_ref[...] = back.reshape(frames, strip, width).astype(jnp.bfloat16)


def outputs(place, prev_ok, next_ok, features, cotangent, skip_input, halo, edge, *weights):
    frames, strip, width = features.shape
    smem = pl.BlockSpec(memory_space=pltpu.SMEM)
    vmem = pl.BlockSpec(memory_space=pltpu.VMEM)
    buf = pltpu.VMEM((frames * strip, width), jnp.bfloat16)
    out = jax.ShapeDtypeStruct(features.shape, jnp.bfloat16)
    return pl.pallas_call(
        out_kernel,
        out_shape=(out, out),
        in_specs=[smem] * 3 + [vmem] * 9,
        out_specs=(vmem, vmem),
        scratch_shapes=[buf] * 4 + [pltpu.VMEM((2, 8, 40, 3 * width), jnp.bfloat16), pltpu.VMEM((width, 3 * width), jnp.bfloat16)],
        compiler_params=pltpu.CompilerParams(vmem_limit_bytes=48 << 20),
        name="outputs",
    )(place, prev_ok, next_ok, features, cotangent, skip_input, halo, edge, *weights)


def shards(features, skip_input, cotangent, temporal_weight, clip_lengths, cycle_start):
    frames, strip, width = features.shape
    core, xl, xh, z, y = [lax.axis_index(a) for a in ("c", "xl", "xh", "z", "y")]
    n_x, n_y, n_z = lax.axis_size(X), lax.axis_size("y"), lax.axis_size("z")
    n_dp = lax.axis_size(DP)
    total_frames = frames * n_dp

    def from_y(even, odd):
        pairs = []
        for plane in range(n_z):
            distance = (even, odd)[plane % 2]
            for side in range(2 if 2 * distance < n_y else 1):
                base = (2 * plane + side) * n_y
                pairs += [(base + i, base + (i + (1 - 2 * side) * distance) % n_y) for i in range(n_y)]
        return lax.ppermute(temporal_weight, ("z", "c", "y"), pairs)

    w_far, w_near = from_y(3, 4), from_y(1, 2)

    both = [(0, 1), (1, 0)]
    own = lax.all_to_all(pack(features, cotangent), X, 0, 0, tiled=True).reshape(n_x, frames, strip, width)
    own, w_far, w_near = lax.optimization_barrier((own, w_far, w_near))
    sib = lax.ppermute(own, "c", both)
    z_next = [(2 * i, (2 * i - 1) % (2 * n_z)) for i in range(n_z)] + [(2 * i + 1, (2 * i + 2) % (2 * n_z)) for i in range(n_z)]
    edge = jnp.where(core == 0, own[:, 0, :, :384], own[:, -1, :, :384])
    halo_x = lax.ppermute(edge, ("z", "c"), z_next)

    _, clip_lengths, cycle_start = lax.optimization_barrier((edge, clip_lengths, cycle_start))
    first = (jnp.arange(2, dtype=jnp.int32) * n_z + z)[:, None] * (2 * frames)
    chip_frames = (first + jnp.arange(2 * frames, dtype=jnp.int32)).reshape(-1)
    prev_all, next_all = border_flags(clip_lengths, cycle_start, chip_frames, total_frames)
    wrapped = jnp.where(core == 0, z == 0, z == n_z - 1)
    place = jnp.stack([core, xl, wrapped.astype(jnp.int32)]).astype(jnp.int32)
    term = x_term(place, prev_all, next_all, own, sib, halo_x)

    _, features, cotangent = lax.optimization_barrier((term, features, cotangent))
    ends = [jnp.concatenate([features[i], cotangent[i]], axis=1) for i in (0, -1)]
    edges = lax.all_gather(jnp.where(core == 0, ends[1], ends[0]), "c")
    across = [(d, (d - 1) % n_dp if d % 2 == 0 else (d + 1) % n_dp) for d in range(n_dp)]
    halo = lax.ppermute(jnp.where(core == 0, ends[0], ends[1]), DP, across)
    _, w_far, w_near = lax.optimization_barrier((term, w_far, w_near))
    parity = z % 2
    pair = jnp.stack([jnp.where((parity == 1) & (core == 1), temporal_weight, w_far), w_near])
    pair_far = lax.ppermute(pair, "z", [(i, i ^ 1) for i in range(n_z)])
    blocks = jnp.concatenate([pair, pair_far])
    blocks_far = lax.ppermute(blocks, "xl", both)
    blocks_sib = lax.ppermute(blocks, "c", both)

    part = lax.all_to_all(term.reshape(n_y, 320 // n_y, 512), "y", 0, 0, tiled=True)
    part, halo, edges = lax.optimization_barrier((part, halo, edges))
    local_rows = part.shape[1]
    n_xz = 2 * n_z
    pieces = y_sum(part, n_z)
    _, blocks_far, blocks_sib = lax.optimization_barrier((pieces, blocks_far, blocks_sib))
    mine = lax.all_to_all(pieces, "z", 0, 0, tiled=True)
    mine = mine.sum(0) * (1.0 / math.sqrt(total_frames * strip * lax.axis_size(FSDP)))
    mine = jnp.broadcast_to(mine[None], (n_xz, 8, 256))
    weights = (blocks, blocks_far, blocks_sib, lax.ppermute(blocks_far, "c", both))
    _, weights = lax.optimization_barrier((mine, weights))
    gathered = lax.all_to_all(mine, ("xh", "z"), 0, 0, tiled=True)
    place_out = jnp.stack([core, xh * (2 * frames) + core * frames, xl, y, parity]).astype(jnp.int32)
    block_out, grad_features = outputs(
        place_out, prev_all, next_all, features, cotangent, skip_input, halo, edges, *weights
    )
    gathered, block_out, grad_features = lax.optimization_barrier((gathered, block_out, grad_features))
    gathered = lax.all_gather(gathered, "c")

    def flat(a):
        a = a.reshape(2, 6, 2, 8, 256).transpose(0, 1, 3, 2, 4)
        return a.reshape(2, 48, 512)[:, :local_rows]

    low, high = flat(gathered[0]), flat(gathered[1])

    def outer_tap(b):
        return [b[0, :, :320], b[1, :, 256:320], b[1, :, :256]]

    tap_1 = [low[0, :, 384:], high[0, :, 384:], low[0, :, 320:384], low[1, :, 320:], high[1, :, 384:]]
    grad_weight = jnp.concatenate(outer_tap(low) + tap_1 + outer_tap(high), axis=1)

    return (block_out, grad_features, grad_weight)


def solution(mesh):
    split = Mesh(mesh.devices.reshape(2, 12, 2, 2, 8), DP + FSDP)
    tokens = P(DP, FSDP, None)
    in_specs = (tokens, tokens, tokens, P(FSDP, None), P(), P())
    out_specs = (tokens, tokens, P(FSDP, None))
    return jax.shard_map(shards, mesh=split, in_specs=in_specs, out_specs=out_specs, check_vma=False)
```

```python
import math

import jax
import jax.numpy as jnp
from jax import lax
from jax.experimental import pallas as pl
from jax.experimental.pallas import tpu as pltpu
from jax.sharding import Mesh, PartitionSpec as P

DP = ("xh", "z", "c")
FSDP = ("xl", "y")
X = ("xh", "xl")


def border_flags(clip_lengths, cycle_start, frame_index, total):
    starts = jnp.cumsum(clip_lengths) - clip_lengths
    position = jnp.mod(frame_index - cycle_start[0], total)
    following = jnp.mod(frame_index + 1 - cycle_start[0], total)
    first_here = jnp.any(position[:, None] == starts[None, :], axis=1)
    first_next = jnp.any(following[:, None] == starts[None, :], axis=1)
    return (1 - first_here.astype(jnp.int32), 1 - first_next.astype(jnp.int32))


def pack_kernel(f_hbm, g_hbm, out_hbm, f_ref, g_ref, out_ref, in_sems, out_sems):
    steps = f_ref.shape[0]
    frames, strip, width = f_ref.shape[1:]
    rows = frames * strip

    def fetch(i):
        return [
            pltpu.make_async_copy(src.at[pl.ds(i * frames, frames)], dst.at[i], in_sems.at[i, k])
            for k, (src, dst) in enumerate(((f_hbm, f_ref), (g_hbm, g_ref)))
        ]

    def send(i):
        return pltpu.make_async_copy(out_ref.at[i], out_hbm.at[:, pl.ds(i * rows, rows), :], out_sems.at[i])

    for i in range(steps):
        for copy in fetch(i):
            copy.start()
    for i in range(steps):
        for copy in fetch(i):
            copy.wait()
        f = f_ref[i].reshape(rows, width)
        g = g_ref[i].reshape(rows, width)
        f_mid, g_mid = f[:, 256:384], g[:, 256:384]
        f_rolled, g_rolled = [pltpu.roll(m.astype(jnp.float32), 64, 1).astype(jnp.bfloat16) for m in (f_mid, g_mid)]
        left = lax.broadcasted_iota(jnp.int32, f_mid.shape, 1) < 64
        for xh in range(2):
            for xl in range(2):
                j = 2 * xh + xl
                out_ref[i, j, :, :256] = f[:, 384 * xl:384 * xl + 256]
                out_ref[i, j, :, 256:384] = jnp.where(left, f_rolled if xl else f_mid, g_mid if xh else g_rolled)
                out_ref[i, j, :, 384:] = g[:, 384 * xh:384 * xh + 256]
        send(i).start()
    for i in range(steps):
        send(i).wait()


def pack(features, cotangent):
    frames, strip, width = features.shape
    steps = 2
    hbm = pl.BlockSpec(memory_space=pltpu.HBM)
    part = pltpu.VMEM((steps, frames // steps, strip, width), jnp.bfloat16)
    return pl.pallas_call(
        pack_kernel,
        out_shape=jax.ShapeDtypeStruct((4, frames * strip, width), jnp.bfloat16),
        in_specs=[hbm] * 2,
        out_specs=hbm,
        scratch_shapes=[
            part, part, pltpu.VMEM((steps, 4, frames * strip // steps, width), jnp.bfloat16),
            pltpu.SemaphoreType.DMA((steps, 2)), pltpu.SemaphoreType.DMA((steps,)),
        ],
        compiler_params=pltpu.CompilerParams(vmem_limit_bytes=48 << 20),
        name="pack",
    )(features, cotangent)


def term_kernel(place_ref, prev_ref, next_ref, own_ref, sib_ref, halo_ref, out_ref, fa_own, fa_sib):
    chips, frames, strip, _ = own_ref.shape
    core, xl, wrapped = place_ref[0], place_ref[1], place_ref[2]

    def put(dst, chip, slot, value, ok):
        dst[pl.ds((chip * frames + slot) * strip, strip), :] = jnp.where(ok != 0, value, jnp.zeros_like(value))

    def halo(chip):
        return halo_ref[(chip // 2 + wrapped) % 2 * 2 + chip % 2]

    @pl.when(core == 0)
    def _():
        for chip in range(chips):
            at = chip // 2 * 2 * frames
            for j in range(frames):
                mine = halo(chip) if j == 0 else own_ref[chip, j - 1, :, :384]
                its = own_ref[chip, frames - 1, :, :384] if j == 0 else sib_ref[chip, j - 1, :, :384]
                put(fa_own, chip, j, mine, prev_ref[at + j])
                put(fa_sib, chip, j, its, prev_ref[at + frames + j])

    @pl.when(core != 0)
    def _():
        for chip in range(chips):
            at = chip // 2 * 2 * frames
            for j in range(frames):
                mine = halo(chip) if j == frames - 1 else own_ref[chip, j + 1, :, :384]
                its = own_ref[chip, 0, :, :384] if j == frames - 1 else sib_ref[chip, j + 1, :, :384]
                put(fa_own, chip, j, mine, next_ref[at + frames + j])
                put(fa_sib, chip, j, its, next_ref[at + j])

    def flat(ref, start, stop):
        return ref[:, :, :, start:stop].reshape(chips * frames * strip, stop - start)

    def dot(a, b):
        return lax.dot_general(a, b, (((0,), (0,)), ((), ())), preferred_element_type=jnp.float32)

    def center(start, stop):
        return dot(flat(own_ref, 0, 384), flat(own_ref, start, stop)) + dot(flat(sib_ref, 0, 384), flat(sib_ref, start, stop))

    outer = dot(fa_own[...], flat(own_ref, 256, 640)) + dot(fa_sib[...], flat(sib_ref, 256, 640))
    left = lax.broadcasted_iota(jnp.int32, (384, 128), 1) < 64
    rolled = pltpu.roll(outer[:, :128], 64, 1)

    def store(start, stop, value):
        @pl.when(xl == 0)
        def _():
            out_ref[:, start:stop] = value[:320]

        @pl.when(xl != 0)
        def _():
            out_ref[64:, start:stop] = value[:256]
            out_ref[:64, start:stop] = value[256:320]

    store(0, 256, outer[:, 128:])

    @pl.when(core == 0)
    def _():
        mid = center(256, 512)
        store(256, 384, jnp.where(left, rolled, mid[:, :128]))
        store(384, 512, mid[:, 128:])

    @pl.when(core != 0)
    def _():
        store(256, 384, jnp.where(left, rolled, jnp.zeros_like(rolled)))
        store(384, 512, center(512, 640))


def x_term(place, prev_ok, next_ok, own, sib, halo):
    smem = pl.BlockSpec(memory_space=pltpu.SMEM)
    vmem = pl.BlockSpec(memory_space=pltpu.VMEM)
    chips, frames, strip, _ = own.shape
    buf = pltpu.VMEM((chips * frames * strip, 384), jnp.bfloat16)
    return pl.pallas_call(
        term_kernel,
        out_shape=jax.ShapeDtypeStruct((320, 512), jnp.float32),
        in_specs=[smem] * 3 + [vmem] * 3,
        out_specs=vmem,
        scratch_shapes=[buf, buf],
        compiler_params=pltpu.CompilerParams(vmem_limit_bytes=48 << 20),
        name="x_term",
    )(place, prev_ok, next_ok, own, sib, halo)


def out_kernel(place_ref, prev_ref, next_ref, f_ref, g_ref, skip_ref, halo_ref, edge_ref, *refs):
    weights, (out_ref, back_ref, f_lo, f_hi, g_lo, g_hi, blocks, weight) = refs[:4], refs[4:]
    frames, strip, width = f_ref.shape
    tokens = frames * strip
    core, at, xl, y, parity = [place_ref[i] for i in range(5)]
    count, rows = weights[0].shape[:2]

    def put(dst, j, value, ok):
        dst[pl.ds(j * strip, strip), :] = jnp.where(ok != 0, value, jnp.zeros_like(value))

    for src, lo, hi, lanes in ((f_ref, f_lo, f_hi, slice(0, width)), (g_ref, g_lo, g_hi, slice(width, 2 * width))):
        halo, edge = halo_ref[:, lanes], edge_ref[1 - core, :, lanes]
        for j in range(frames):
            put(lo, j, jnp.where(core == 0, halo, edge) if j == 0 else src[j - 1], prev_ref[at + j])
            put(hi, j, jnp.where(core == 0, edge, halo) if j == frames - 1 else src[j + 1], next_ref[at + j])

    for i in range(count):
        odd = parity if i < 2 else 1 - parity
        low, high = (3 + odd, jnp.where(odd == 0, 5, 0)) if i % 2 == 0 else (1 + odd, 7 - odd)
        for half in range(2):
            blocks[half, jnp.where(core == 0, low, high)] = weights[half][i]
            blocks[half, jnp.where(core == 0, high, low)] = weights[2 + half][i]
    for half in range(2):
        for i in range(2 * count):
            start = (half * 2 * count + i) * rows
            weight[start:start + rows, :] = blocks[(half + xl) % 2, (y - i + 2 * count) % (2 * count)]

    def dot(a, b):
        return jnp.dot(a, b, preferred_element_type=jnp.float32)

    def dot_t(a, b):
        return lax.dot_general(a, b, (((1,), (1,)), ((), ())), preferred_element_type=jnp.float32)

    f = f_ref[...].reshape(tokens, width)
    g = g_ref[...].reshape(tokens, width)
    taps = [weight[:, k * width:(k + 1) * width] for k in range(3)]
    mixed = dot(f_lo[...], taps[0]) + dot(f, taps[1]) + dot(f_hi[...], taps[2])
    mixed = mixed.reshape(frames, strip, width) + skip_ref[...].astype(jnp.float32)
    out_ref[...] = mixed.astype(jnp.bfloat16)
    back = dot_t(g_hi[...], taps[0]) + dot_t(g, taps[1]) + dot_t(g_lo[...], taps[2])
    back_ref[...] = back.reshape(frames, strip, width).astype(jnp.bfloat16)


def outputs(place, prev_ok, next_ok, features, cotangent, skip_input, halo, edge, *weights):
    frames, strip, width = features.shape
    smem = pl.BlockSpec(memory_space=pltpu.SMEM)
    vmem = pl.BlockSpec(memory_space=pltpu.VMEM)
    buf = pltpu.VMEM((frames * strip, width), jnp.bfloat16)
    out = jax.ShapeDtypeStruct(features.shape, jnp.bfloat16)
    return pl.pallas_call(
        out_kernel,
        out_shape=(out, out),
        in_specs=[smem] * 3 + [vmem] * 9,
        out_specs=(vmem, vmem),
        scratch_shapes=[buf] * 4 + [pltpu.VMEM((2, 8, 40, 3 * width), jnp.bfloat16), pltpu.VMEM((width, 3 * width), jnp.bfloat16)],
        compiler_params=pltpu.CompilerParams(vmem_limit_bytes=48 << 20),
        name="outputs",
    )(place, prev_ok, next_ok, features, cotangent, skip_input, halo, edge, *weights)


def shards(features, skip_input, cotangent, temporal_weight, clip_lengths, cycle_start):
    frames, strip, width = features.shape
    core, xl, xh, z, y = [lax.axis_index(a) for a in ("c", "xl", "xh", "z", "y")]
    n_x, n_y, n_z = lax.axis_size(X), lax.axis_size("y"), lax.axis_size("z")
    n_dp = lax.axis_size(DP)
    total_frames = frames * n_dp

    def from_y(even, odd):
        pairs = []
        for plane in range(n_z):
            distance = (even, odd)[plane % 2]
            for side in range(2 if 2 * distance < n_y else 1):
                base = (2 * plane + side) * n_y
                pairs += [(base + i, base + (i + (1 - 2 * side) * distance) % n_y) for i in range(n_y)]
        return lax.ppermute(temporal_weight, ("z", "c", "y"), pairs)

    w_far, w_near = from_y(3, 4), from_y(1, 2)

    both = [(0, 1), (1, 0)]
    own = lax.all_to_all(pack(features, cotangent), X, 0, 0, tiled=True).reshape(n_x, frames, strip, width)
    own, w_far, w_near = lax.optimization_barrier((own, w_far, w_near))
    sib = lax.ppermute(own, "c", both)
    z_next = [(2 * i, (2 * i - 1) % (2 * n_z)) for i in range(n_z)] + [(2 * i + 1, (2 * i + 2) % (2 * n_z)) for i in range(n_z)]
    edge = jnp.where(core == 0, own[:, 0, :, :384], own[:, -1, :, :384])
    halo_x = lax.ppermute(edge, ("z", "c"), z_next)

    _, clip_lengths, cycle_start = lax.optimization_barrier((edge, clip_lengths, cycle_start))
    first = (jnp.arange(2, dtype=jnp.int32) * n_z + z)[:, None] * (2 * frames)
    chip_frames = (first + jnp.arange(2 * frames, dtype=jnp.int32)).reshape(-1)
    prev_all, next_all = border_flags(clip_lengths, cycle_start, chip_frames, total_frames)
    wrapped = jnp.where(core == 0, z == 0, z == n_z - 1)
    place = jnp.stack([core, xl, wrapped.astype(jnp.int32)]).astype(jnp.int32)
    term = x_term(place, prev_all, next_all, own, sib, halo_x)

    _, features, cotangent = lax.optimization_barrier((term, features, cotangent))
    ends = [jnp.concatenate([features[i], cotangent[i]], axis=1) for i in (0, -1)]
    edges = lax.all_gather(jnp.where(core == 0, ends[1], ends[0]), "c")
    across = [(d, (d - 1) % n_dp if d % 2 == 0 else (d + 1) % n_dp) for d in range(n_dp)]
    halo = lax.ppermute(jnp.where(core == 0, ends[0], ends[1]), DP, across)
    _, w_far, w_near = lax.optimization_barrier((term, w_far, w_near))
    parity = z % 2
    pair = jnp.stack([jnp.where((parity == 1) & (core == 1), temporal_weight, w_far), w_near])
    pair_far = lax.ppermute(pair, "z", [(i, i ^ 1) for i in range(n_z)])
    pair_far, halo, edges = lax.optimization_barrier((pair_far, halo, edges))
    blocks = jnp.concatenate([pair, pair_far])
    blocks_far = lax.ppermute(blocks, "xl", both)

    part = lax.all_to_all(term.reshape(n_y, 320 // n_y, 512), "y", 0, 0, tiled=True)
    part, blocks = lax.optimization_barrier((part, blocks))
    part = part.sum(0)
    local_rows = part.shape[0]
    n_xz = 2 * n_z
    pieces = jnp.pad(part, ((0, 48 - local_rows), (0, 0))).reshape(6, 8, 2, 256).transpose(0, 2, 1, 3).reshape(n_z, 8, 256)
    _, blocks, blocks_far = lax.optimization_barrier((pieces, blocks, blocks_far))
    blocks_sib = lax.ppermute(blocks, "c", both)
    mine = lax.all_to_all(pieces, "z", 0, 0, tiled=True)
    mine = mine.sum(0) * (1.0 / math.sqrt(total_frames * strip * lax.axis_size(FSDP)))
    mine = jnp.broadcast_to(mine[None], (n_xz, 8, 256))
    weights = (blocks, blocks_far, blocks_sib, lax.ppermute(blocks_far, "c", both))
    _, weights = lax.optimization_barrier((mine, weights))
    gathered = lax.all_to_all(mine, ("xh", "z"), 0, 0, tiled=True)
    place_out = jnp.stack([core, xh * (2 * frames) + core * frames, xl, y, parity]).astype(jnp.int32)
    block_out, grad_features = outputs(
        place_out, prev_all, next_all, features, cotangent, skip_input, halo, edges, *weights
    )
    gathered, block_out, grad_features = lax.optimization_barrier((gathered, block_out, grad_features))
    gathered = lax.all_gather(gathered, "c")

    def flat(a):
        a = a.reshape(2, 6, 2, 8, 256).transpose(0, 1, 3, 2, 4)
        return a.reshape(2, 48, 512)[:, :local_rows]

    low, high = flat(gathered[0]), flat(gathered[1])

    def outer_tap(b):
        return [b[0, :, :320], b[1, :, 256:320], b[1, :, :256]]

    tap_1 = [low[0, :, 384:], high[0, :, 384:], low[0, :, 320:384], low[1, :, 320:], high[1, :, 384:]]
    grad_weight = jnp.concatenate(outer_tap(low) + tap_1 + outer_tap(high), axis=1)

    return (block_out, grad_features, grad_weight)


def solution(mesh):
    split = Mesh(mesh.devices.reshape(2, 12, 2, 2, 8), DP + FSDP)
    tokens = P(DP, FSDP, None)
    in_specs = (tokens, tokens, tokens, P(FSDP, None), P(), P())
    out_specs = (tokens, tokens, P(FSDP, None))
    return jax.shard_map(shards, mesh=split, in_specs=in_specs, out_specs=out_specs, check_vma=False)
```

```python
import math

import jax
import jax.numpy as jnp
from jax import lax
from jax.experimental import pallas as pl
from jax.experimental.pallas import tpu as pltpu
from jax.sharding import Mesh, PartitionSpec as P

DP = ("xh", "z", "c")
FSDP = ("xl", "y")
X = ("xh", "xl")


def border_flags(clip_lengths, cycle_start, frame_index, total):
    starts = jnp.cumsum(clip_lengths) - clip_lengths
    position = jnp.mod(frame_index - cycle_start[0], total)
    following = jnp.mod(frame_index + 1 - cycle_start[0], total)
    first_here = jnp.any(position[:, None] == starts[None, :], axis=1)
    first_next = jnp.any(following[:, None] == starts[None, :], axis=1)
    return (1 - first_here.astype(jnp.int32), 1 - first_next.astype(jnp.int32))


def pack_kernel(f_hbm, g_hbm, out_hbm, f_ref, g_ref, out_ref, in_sems, out_sems):
    steps = f_ref.shape[0]
    frames, strip, width = f_ref.shape[1:]
    rows = frames * strip

    def fetch(i):
        return [
            pltpu.make_async_copy(src.at[pl.ds(i * frames, frames)], dst.at[i], in_sems.at[i, k])
            for k, (src, dst) in enumerate(((f_hbm, f_ref), (g_hbm, g_ref)))
        ]

    def send(i):
        return pltpu.make_async_copy(out_ref.at[i], out_hbm.at[:, pl.ds(i * rows, rows), :], out_sems.at[i])

    for i in range(steps):
        for copy in fetch(i):
            copy.start()
    for i in range(steps):
        for copy in fetch(i):
            copy.wait()
        f = f_ref[i].reshape(rows, width)
        g = g_ref[i].reshape(rows, width)
        f_mid, g_mid = f[:, 256:384], g[:, 256:384]
        f_rolled, g_rolled = [pltpu.roll(m.astype(jnp.float32), 64, 1).astype(jnp.bfloat16) for m in (f_mid, g_mid)]
        left = lax.broadcasted_iota(jnp.int32, f_mid.shape, 1) < 64
        for xh in range(2):
            for xl in range(2):
                j = 2 * xh + xl
                out_ref[i, j, :, :256] = f[:, 384 * xl:384 * xl + 256]
                out_ref[i, j, :, 256:384] = jnp.where(left, f_rolled if xl else f_mid, g_mid if xh else g_rolled)
                out_ref[i, j, :, 384:] = g[:, 384 * xh:384 * xh + 256]
        send(i).start()
    for i in range(steps):
        send(i).wait()


def pack(features, cotangent):
    frames, strip, width = features.shape
    steps = 2
    hbm = pl.BlockSpec(memory_space=pltpu.HBM)
    part = pltpu.VMEM((steps, frames // steps, strip, width), jnp.bfloat16)
    return pl.pallas_call(
        pack_kernel,
        out_shape=jax.ShapeDtypeStruct((4, frames * strip, width), jnp.bfloat16),
        in_specs=[hbm] * 2,
        out_specs=hbm,
        scratch_shapes=[
            part, part, pltpu.VMEM((steps, 4, frames * strip // steps, width), jnp.bfloat16),
            pltpu.SemaphoreType.DMA((steps, 2)), pltpu.SemaphoreType.DMA((steps,)),
        ],
        compiler_params=pltpu.CompilerParams(vmem_limit_bytes=60 << 20),
        name="pack",
    )(features, cotangent)


def term_kernel(place_ref, prev_ref, next_ref, own_ref, sib_ref, halo_ref, out_ref, fa_own, fa_sib):
    chips, frames, strip, _ = own_ref.shape
    core, xl, wrapped = place_ref[0], place_ref[1], place_ref[2]

    def put(dst, chip, slot, value, ok):
        dst[pl.ds((chip * frames + slot) * strip, strip), :] = jnp.where(ok != 0, value, jnp.zeros_like(value))

    def halo(chip):
        return halo_ref[(chip // 2 + wrapped) % 2 * 2 + chip % 2]

    @pl.when(core == 0)
    def _():
        for chip in range(chips):
            at = chip // 2 * 2 * frames
            for j in range(frames):
                mine = halo(chip) if j == 0 else own_ref[chip, j - 1, :, :384]
                its = own_ref[chip, frames - 1, :, :384] if j == 0 else sib_ref[chip, j - 1, :, :384]
                put(fa_own, chip, j, mine, prev_ref[at + j])
                put(fa_sib, chip, j, its, prev_ref[at + frames + j])

    @pl.when(core != 0)
    def _():
        for chip in range(chips):
            at = chip // 2 * 2 * frames
            for j in range(frames):
                mine = halo(chip) if j == frames - 1 else own_ref[chip, j + 1, :, :384]
                its = own_ref[chip, 0, :, :384] if j == frames - 1 else sib_ref[chip, j + 1, :, :384]
                put(fa_own, chip, j, mine, next_ref[at + frames + j])
                put(fa_sib, chip, j, its, next_ref[at + j])

    def flat(ref, start, stop):
        return ref[:, :, :, start:stop].reshape(chips * frames * strip, stop - start)

    def dot(a, b):
        return lax.dot_general(a, b, (((0,), (0,)), ((), ())), preferred_element_type=jnp.float32)

    def center(start, stop):
        return dot(flat(own_ref, 0, 384), flat(own_ref, start, stop)) + dot(flat(sib_ref, 0, 384), flat(sib_ref, start, stop))

    outer = dot(fa_own[...], flat(own_ref, 256, 640)) + dot(fa_sib[...], flat(sib_ref, 256, 640))
    left = lax.broadcasted_iota(jnp.int32, (384, 128), 1) < 64
    rolled = pltpu.roll(outer[:, :128], 64, 1)

    def store(start, stop, value):
        @pl.when(xl == 0)
        def _():
            out_ref[:, start:stop] = value[:320]

        @pl.when(xl != 0)
        def _():
            out_ref[64:, start:stop] = value[:256]
            out_ref[:64, start:stop] = value[256:320]

    store(0, 256, outer[:, 128:])

    @pl.when(core == 0)
    def _():
        mid = center(256, 512)
        store(256, 384, jnp.where(left, rolled, mid[:, :128]))
        store(384, 512, mid[:, 128:])

    @pl.when(core != 0)
    def _():
        store(256, 384, jnp.where(left, rolled, jnp.zeros_like(rolled)))
        store(384, 512, center(512, 640))


def x_term(place, prev_ok, next_ok, own, sib, halo):
    smem = pl.BlockSpec(memory_space=pltpu.SMEM)
    vmem = pl.BlockSpec(memory_space=pltpu.VMEM)
    chips, frames, strip, _ = own.shape
    buf = pltpu.VMEM((chips * frames * strip, 384), jnp.bfloat16)
    return pl.pallas_call(
        term_kernel,
        out_shape=jax.ShapeDtypeStruct((320, 512), jnp.float32),
        in_specs=[smem] * 3 + [vmem] * 3,
        out_specs=vmem,
        scratch_shapes=[buf, buf],
        compiler_params=pltpu.CompilerParams(vmem_limit_bytes=48 << 20),
        name="x_term",
    )(place, prev_ok, next_ok, own, sib, halo)


def out_kernel(place_ref, prev_ref, next_ref, f_ref, g_ref, skip_ref, halo_ref, edge_ref, *refs):
    weights, (out_ref, back_ref, f_lo, f_hi, g_lo, g_hi, blocks, weight) = refs[:4], refs[4:]
    frames, strip, width = f_ref.shape
    tokens = frames * strip
    core, at, xl, y, parity = [place_ref[i] for i in range(5)]
    count, rows = weights[0].shape[:2]

    def put(dst, j, value, ok):
        dst[pl.ds(j * strip, strip), :] = jnp.where(ok != 0, value, jnp.zeros_like(value))

    for src, lo, hi, lanes in ((f_ref, f_lo, f_hi, slice(0, width)), (g_ref, g_lo, g_hi, slice(width, 2 * width))):
        halo, edge = halo_ref[:, lanes], edge_ref[1 - core, :, lanes]
        for j in range(frames):
            put(lo, j, jnp.where(core == 0, halo, edge) if j == 0 else src[j - 1], prev_ref[at + j])
            put(hi, j, jnp.where(core == 0, edge, halo) if j == frames - 1 else src[j + 1], next_ref[at + j])

    for i in range(count):
        odd = parity if i < 2 else 1 - parity
        low, high = (3 + odd, jnp.where(odd == 0, 5, 0)) if i % 2 == 0 else (1 + odd, 7 - odd)
        for half in range(2):
            blocks[half, jnp.where(core == 0, low, high)] = weights[half][i]
            blocks[half, jnp.where(core == 0, high, low)] = weights[2 + half][i]
    for half in range(2):
        for i in range(2 * count):
            start = (half * 2 * count + i) * rows
            weight[start:start + rows, :] = blocks[(half + xl) % 2, (y - i + 2 * count) % (2 * count)]

    def dot(a, b):
        return jnp.dot(a, b, preferred_element_type=jnp.float32)

    def dot_t(a, b):
        return lax.dot_general(a, b, (((1,), (1,)), ((), ())), preferred_element_type=jnp.float32)

    f = f_ref[...].reshape(tokens, width)
    g = g_ref[...].reshape(tokens, width)
    taps = [weight[:, k * width:(k + 1) * width] for k in range(3)]
    mixed = dot(f_lo[...], taps[0]) + dot(f, taps[1]) + dot(f_hi[...], taps[2])
    mixed = mixed.reshape(frames, strip, width) + skip_ref[...].astype(jnp.float32)
    out_ref[...] = mixed.astype(jnp.bfloat16)
    back = dot_t(g_hi[...], taps[0]) + dot_t(g, taps[1]) + dot_t(g_lo[...], taps[2])
    back_ref[...] = back.reshape(frames, strip, width).astype(jnp.bfloat16)


def outputs(place, prev_ok, next_ok, features, cotangent, skip_input, halo, edge, *weights):
    frames, strip, width = features.shape
    smem = pl.BlockSpec(memory_space=pltpu.SMEM)
    vmem = pl.BlockSpec(memory_space=pltpu.VMEM)
    buf = pltpu.VMEM((frames * strip, width), jnp.bfloat16)
    out = jax.ShapeDtypeStruct(features.shape, jnp.bfloat16)
    return pl.pallas_call(
        out_kernel,
        out_shape=(out, out),
        in_specs=[smem] * 3 + [vmem] * 9,
        out_specs=(vmem, vmem),
        scratch_shapes=[buf] * 4 + [pltpu.VMEM((2, 8, 40, 3 * width), jnp.bfloat16), pltpu.VMEM((width, 3 * width), jnp.bfloat16)],
        compiler_params=pltpu.CompilerParams(vmem_limit_bytes=48 << 20),
        name="outputs",
    )(place, prev_ok, next_ok, features, cotangent, skip_input, halo, edge, *weights)


def shards(features, skip_input, cotangent, temporal_weight, clip_lengths, cycle_start):
    frames, strip, width = features.shape
    core, xl, xh, z, y = [lax.axis_index(a) for a in ("c", "xl", "xh", "z", "y")]
    n_x, n_y, n_z = lax.axis_size(X), lax.axis_size("y"), lax.axis_size("z")
    n_dp = lax.axis_size(DP)
    total_frames = frames * n_dp

    def from_y(even, odd):
        pairs = []
        for plane in range(n_z):
            distance = (even, odd)[plane % 2]
            for side in range(2 if 2 * distance < n_y else 1):
                base = (2 * plane + side) * n_y
                pairs += [(base + i, base + (i + (1 - 2 * side) * distance) % n_y) for i in range(n_y)]
        return lax.ppermute(temporal_weight, ("z", "c", "y"), pairs)

    w_far, w_near = from_y(3, 4), from_y(1, 2)

    both = [(0, 1), (1, 0)]
    own = lax.all_to_all(pack(features, cotangent), X, 0, 0, tiled=True).reshape(n_x, frames, strip, width)
    own, w_far, w_near = lax.optimization_barrier((own, w_far, w_near))
    sib = lax.ppermute(own, "c", both)
    z_next = [(2 * i, (2 * i - 1) % (2 * n_z)) for i in range(n_z)] + [(2 * i + 1, (2 * i + 2) % (2 * n_z)) for i in range(n_z)]
    edge = jnp.where(core == 0, own[:, 0, :, :384], own[:, -1, :, :384])
    halo_x = lax.ppermute(edge, ("z", "c"), z_next)

    _, clip_lengths, cycle_start = lax.optimization_barrier((edge, clip_lengths, cycle_start))
    first = (jnp.arange(2, dtype=jnp.int32) * n_z + z)[:, None] * (2 * frames)
    chip_frames = (first + jnp.arange(2 * frames, dtype=jnp.int32)).reshape(-1)
    prev_all, next_all = border_flags(clip_lengths, cycle_start, chip_frames, total_frames)
    wrapped = jnp.where(core == 0, z == 0, z == n_z - 1)
    place = jnp.stack([core, xl, wrapped.astype(jnp.int32)]).astype(jnp.int32)
    term = x_term(place, prev_all, next_all, own, sib, halo_x)

    _, features, cotangent = lax.optimization_barrier((term, features, cotangent))
    ends = [jnp.concatenate([features[i], cotangent[i]], axis=1) for i in (0, -1)]
    edges = lax.all_gather(jnp.where(core == 0, ends[1], ends[0]), "c")
    across = [(d, (d - 1) % n_dp if d % 2 == 0 else (d + 1) % n_dp) for d in range(n_dp)]
    halo = lax.ppermute(jnp.where(core == 0, ends[0], ends[1]), DP, across)
    _, w_far, w_near = lax.optimization_barrier((term, w_far, w_near))
    parity = z % 2
    pair = jnp.stack([jnp.where((parity == 1) & (core == 1), temporal_weight, w_far), w_near])
    pair_far = lax.ppermute(pair, "z", [(i, i ^ 1) for i in range(n_z)])
    pair_far, halo, edges = lax.optimization_barrier((pair_far, halo, edges))
    blocks = jnp.concatenate([pair, pair_far])
    pairs = [(i, i ^ (1 if i // 2 % 2 == 0 else 5)) for i in range(8)]
    blocks_far = lax.ppermute(blocks, ("xh", "c", "xl"), pairs)

    part = lax.all_to_all(term.reshape(n_y, 320 // n_y, 512), "y", 0, 0, tiled=True)
    part, blocks = lax.optimization_barrier((part, blocks))
    part = part.sum(0)
    local_rows = part.shape[0]
    n_xz = 2 * n_z
    pieces = jnp.pad(part, ((0, 48 - local_rows), (0, 0))).reshape(6, 8, 2, 256).transpose(0, 2, 1, 3).reshape(n_z, 8, 256)
    _, blocks, blocks_far = lax.optimization_barrier((pieces, blocks, blocks_far))
    blocks_sib = lax.ppermute(blocks, "c", both)
    mine = lax.all_to_all(pieces, "z", 0, 0, tiled=True)
    mine = mine.sum(0) * (1.0 / math.sqrt(total_frames * strip * lax.axis_size(FSDP)))
    mine = jnp.broadcast_to(mine[None], (n_xz, 8, 256))
    weights = (blocks, blocks_far, blocks_sib, lax.ppermute(blocks_far, "c", both))
    _, weights = lax.optimization_barrier((mine, weights))
    gathered = lax.all_to_all(mine, ("xh", "z"), 0, 0, tiled=True)
    place_out = jnp.stack([core, xh * (2 * frames) + core * frames, xl, y, parity]).astype(jnp.int32)
    block_out, grad_features = outputs(
        place_out, prev_all, next_all, features, cotangent, skip_input, halo, edges, *weights
    )
    gathered, block_out, grad_features = lax.optimization_barrier((gathered, block_out, grad_features))
    gathered = lax.all_gather(gathered, "c")

    def flat(a):
        a = a.reshape(2, 6, 2, 8, 256).transpose(0, 1, 3, 2, 4)
        return a.reshape(2, 48, 512)[:, :local_rows]

    low, high = flat(gathered[0]), flat(gathered[1])

    def outer_tap(b):
        return [b[0, :, :320], b[1, :, 256:320], b[1, :, :256]]

    tap_1 = [low[0, :, 384:], high[0, :, 384:], low[0, :, 320:384], low[1, :, 320:], high[1, :, 384:]]
    grad_weight = jnp.concatenate(outer_tap(low) + tap_1 + outer_tap(high), axis=1)

    return (block_out, grad_features, grad_weight)


def solution(mesh):
    split = Mesh(mesh.devices.reshape(2, 12, 2, 2, 8), DP + FSDP)
    tokens = P(DP, FSDP, None)
    in_specs = (tokens, tokens, tokens, P(FSDP, None), P(), P())
    out_specs = (tokens, tokens, P(FSDP, None))
    return jax.shard_map(shards, mesh=split, in_specs=in_specs, out_specs=out_specs, check_vma=False)
```

```python
import math

import jax
import jax.numpy as jnp
from jax import lax
from jax.experimental import pallas as pl
from jax.experimental.pallas import tpu as pltpu
from jax.sharding import Mesh, PartitionSpec as P

DP = ("xh", "z", "c")
FSDP = ("xl", "y")
X = ("xh", "xl")


def border_flags(clip_lengths, cycle_start, frame_index, total):
    starts = jnp.cumsum(clip_lengths) - clip_lengths
    position = jnp.mod(frame_index - cycle_start[0], total)
    following = jnp.mod(frame_index + 1 - cycle_start[0], total)
    first_here = jnp.any(position[:, None] == starts[None, :], axis=1)
    first_next = jnp.any(following[:, None] == starts[None, :], axis=1)
    return (1 - first_here.astype(jnp.int32), 1 - first_next.astype(jnp.int32))


def pack_kernel(f_hbm, g_hbm, out_hbm, f_ref, g_ref, out_ref, in_sems, out_sems):
    steps = f_ref.shape[0]
    frames, strip, width = f_ref.shape[1:]
    rows = frames * strip

    def fetch(i):
        return [
            pltpu.make_async_copy(src.at[pl.ds(i * frames, frames)], dst.at[i], in_sems.at[i, k])
            for k, (src, dst) in enumerate(((f_hbm, f_ref), (g_hbm, g_ref)))
        ]

    def send(i):
        return pltpu.make_async_copy(out_ref.at[i], out_hbm.at[:, pl.ds(i * rows, rows), :], out_sems.at[i])

    for i in range(steps):
        for copy in fetch(i):
            copy.start()
    for i in range(steps):
        for copy in fetch(i):
            copy.wait()
        f = f_ref[i].reshape(rows, width)
        g = g_ref[i].reshape(rows, width)
        f_mid, g_mid = f[:, 256:384], g[:, 256:384]
        f_rolled, g_rolled = [pltpu.roll(m.astype(jnp.float32), 64, 1).astype(jnp.bfloat16) for m in (f_mid, g_mid)]
        left = lax.broadcasted_iota(jnp.int32, f_mid.shape, 1) < 64
        for xh in range(2):
            for xl in range(2):
                j = 2 * xh + xl
                out_ref[i, j, :, :256] = f[:, 384 * xl:384 * xl + 256]
                out_ref[i, j, :, 256:384] = jnp.where(left, f_rolled if xl else f_mid, g_mid if xh else g_rolled)
                out_ref[i, j, :, 384:] = g[:, 384 * xh:384 * xh + 256]
        send(i).start()
    for i in range(steps):
        send(i).wait()


def pack(features, cotangent):
    frames, strip, width = features.shape
    steps = 2
    hbm = pl.BlockSpec(memory_space=pltpu.HBM)
    part = pltpu.VMEM((steps, frames // steps, strip, width), jnp.bfloat16)
    return pl.pallas_call(
        pack_kernel,
        out_shape=jax.ShapeDtypeStruct((4, frames * strip, width), jnp.bfloat16),
        in_specs=[hbm] * 2,
        out_specs=hbm,
        scratch_shapes=[
            part, part, pltpu.VMEM((steps, 4, frames * strip // steps, width), jnp.bfloat16),
            pltpu.SemaphoreType.DMA((steps, 2)), pltpu.SemaphoreType.DMA((steps,)),
        ],
        compiler_params=pltpu.CompilerParams(vmem_limit_bytes=60 << 20),
        name="pack",
    )(features, cotangent)


def term_kernel(place_ref, prev_ref, next_ref, own_ref, sib_ref, halo_ref, out_ref, fa_own, fa_sib):
    chips, frames, strip, _ = own_ref.shape
    core, xl, wrapped = place_ref[0], place_ref[1], place_ref[2]

    def put(dst, chip, slot, value, ok):
        dst[pl.ds((chip * frames + slot) * strip, strip), :] = jnp.where(ok != 0, value, jnp.zeros_like(value))

    def halo(chip):
        return halo_ref[(chip // 2 + wrapped) % 2 * 2 + chip % 2]

    @pl.when(core == 0)
    def _():
        for chip in range(chips):
            at = chip // 2 * 2 * frames
            for j in range(frames):
                mine = halo(chip) if j == 0 else own_ref[chip, j - 1, :, :384]
                its = own_ref[chip, frames - 1, :, :384] if j == 0 else sib_ref[chip, j - 1, :, :384]
                put(fa_own, chip, j, mine, prev_ref[at + j])
                put(fa_sib, chip, j, its, prev_ref[at + frames + j])

    @pl.when(core != 0)
    def _():
        for chip in range(chips):
            at = chip // 2 * 2 * frames
            for j in range(frames):
                mine = halo(chip) if j == frames - 1 else own_ref[chip, j + 1, :, :384]
                its = own_ref[chip, 0, :, :384] if j == frames - 1 else sib_ref[chip, j + 1, :, :384]
                put(fa_own, chip, j, mine, next_ref[at + frames + j])
                put(fa_sib, chip, j, its, next_ref[at + j])

    def flat(ref, start, stop):
        return ref[:, :, :, start:stop].reshape(chips * frames * strip, stop - start)

    def dot(a, b):
        return lax.dot_general(a, b, (((0,), (0,)), ((), ())), preferred_element_type=jnp.float32)

    def center(start, stop):
        return dot(flat(own_ref, 0, 384), flat(own_ref, start, stop)) + dot(flat(sib_ref, 0, 384), flat(sib_ref, start, stop))

    outer = dot(fa_own[...], flat(own_ref, 256, 640)) + dot(fa_sib[...], flat(sib_ref, 256, 640))
    left = lax.broadcasted_iota(jnp.int32, (384, 128), 1) < 64
    rolled = pltpu.roll(outer[:, :128], 64, 1)

    def store(start, stop, value):
        @pl.when(xl == 0)
        def _():
            out_ref[:, start:stop] = value[:320]

        @pl.when(xl != 0)
        def _():
            out_ref[64:, start:stop] = value[:256]
            out_ref[:64, start:stop] = value[256:320]

    store(0, 256, outer[:, 128:])

    @pl.when(core == 0)
    def _():
        mid = center(256, 512)
        store(256, 384, jnp.where(left, rolled, mid[:, :128]))
        store(384, 512, mid[:, 128:])

    @pl.when(core != 0)
    def _():
        store(256, 384, jnp.where(left, rolled, jnp.zeros_like(rolled)))
        store(384, 512, center(512, 640))


def x_term(place, prev_ok, next_ok, own, sib, halo):
    smem = pl.BlockSpec(memory_space=pltpu.SMEM)
    vmem = pl.BlockSpec(memory_space=pltpu.VMEM)
    chips, frames, strip, _ = own.shape
    buf = pltpu.VMEM((chips * frames * strip, 384), jnp.bfloat16)
    return pl.pallas_call(
        term_kernel,
        out_shape=jax.ShapeDtypeStruct((320, 512), jnp.float32),
        in_specs=[smem] * 3 + [vmem] * 3,
        out_specs=vmem,
        scratch_shapes=[buf, buf],
        compiler_params=pltpu.CompilerParams(vmem_limit_bytes=20 << 20),
        name="x_term",
    )(place, prev_ok, next_ok, own, sib, halo)


def out_kernel(place_ref, prev_ref, next_ref, f_ref, g_ref, skip_ref, halo_ref, edge_ref, *refs):
    weights, (out_ref, back_ref, f_lo, f_hi, g_lo, g_hi, blocks, weight) = refs[:4], refs[4:]
    frames, strip, width = f_ref.shape
    tokens = frames * strip
    core, at, xl, y, parity = [place_ref[i] for i in range(5)]
    count, rows = weights[0].shape[:2]

    def put(dst, j, value, ok):
        dst[pl.ds(j * strip, strip), :] = jnp.where(ok != 0, value, jnp.zeros_like(value))

    for src, lo, hi, lanes in ((f_ref, f_lo, f_hi, slice(0, width)), (g_ref, g_lo, g_hi, slice(width, 2 * width))):
        halo, edge = halo_ref[:, lanes], edge_ref[1 - core, :, lanes]
        for j in range(frames):
            put(lo, j, jnp.where(core == 0, halo, edge) if j == 0 else src[j - 1], prev_ref[at + j])
            put(hi, j, jnp.where(core == 0, edge, halo) if j == frames - 1 else src[j + 1], next_ref[at + j])

    for i in range(count):
        odd = parity if i < 2 else 1 - parity
        low, high = (3 + odd, jnp.where(odd == 0, 5, 0)) if i % 2 == 0 else (1 + odd, 7 - odd)
        for half in range(2):
            blocks[half, jnp.where(core == 0, low, high)] = weights[half][i]
            blocks[half, jnp.where(core == 0, high, low)] = weights[2 + half][i]
    for half in range(2):
        for i in range(2 * count):
            start = (half * 2 * count + i) * rows
            weight[start:start + rows, :] = blocks[(half + xl) % 2, (y - i + 2 * count) % (2 * count)]

    def dot(a, b):
        return jnp.dot(a, b, preferred_element_type=jnp.float32)

    def dot_t(a, b):
        return lax.dot_general(a, b, (((1,), (1,)), ((), ())), preferred_element_type=jnp.float32)

    f = f_ref[...].reshape(tokens, width)
    g = g_ref[...].reshape(tokens, width)
    taps = [weight[:, k * width:(k + 1) * width] for k in range(3)]
    mixed = dot(f_lo[...], taps[0]) + dot(f, taps[1]) + dot(f_hi[...], taps[2])
    mixed = mixed.reshape(frames, strip, width) + skip_ref[...].astype(jnp.float32)
    out_ref[...] = mixed.astype(jnp.bfloat16)
    back = dot_t(g_hi[...], taps[0]) + dot_t(g, taps[1]) + dot_t(g_lo[...], taps[2])
    back_ref[...] = back.reshape(frames, strip, width).astype(jnp.bfloat16)


def outputs(place, prev_ok, next_ok, features, cotangent, skip_input, halo, edge, *weights):
    frames, strip, width = features.shape
    smem = pl.BlockSpec(memory_space=pltpu.SMEM)
    vmem = pl.BlockSpec(memory_space=pltpu.VMEM)
    buf = pltpu.VMEM((frames * strip, width), jnp.bfloat16)
    out = jax.ShapeDtypeStruct(features.shape, jnp.bfloat16)
    return pl.pallas_call(
        out_kernel,
        out_shape=(out, out),
        in_specs=[smem] * 3 + [vmem] * 9,
        out_specs=(vmem, vmem),
        scratch_shapes=[buf] * 4 + [pltpu.VMEM((2, 8, 40, 3 * width), jnp.bfloat16), pltpu.VMEM((width, 3 * width), jnp.bfloat16)],
        compiler_params=pltpu.CompilerParams(vmem_limit_bytes=28 << 20),
        name="outputs",
    )(place, prev_ok, next_ok, features, cotangent, skip_input, halo, edge, *weights)


def shards(features, skip_input, cotangent, temporal_weight, clip_lengths, cycle_start):
    frames, strip, width = features.shape
    core, xl, xh, z, y = [lax.axis_index(a) for a in ("c", "xl", "xh", "z", "y")]
    n_x, n_y, n_z = lax.axis_size(X), lax.axis_size("y"), lax.axis_size("z")
    n_dp = lax.axis_size(DP)
    total_frames = frames * n_dp

    packed = pack(features, cotangent)
    _, temporal_weight = lax.optimization_barrier((packed, temporal_weight))

    def from_y(even, odd):
        pairs = []
        for plane in range(n_z):
            distance = (even, odd)[plane % 2]
            for side in range(2 if 2 * distance < n_y else 1):
                base = (2 * plane + side) * n_y
                pairs += [(base + i, base + (i + (1 - 2 * side) * distance) % n_y) for i in range(n_y)]
        return lax.ppermute(temporal_weight, ("z", "c", "y"), pairs)

    w_far, w_near = from_y(3, 4), from_y(1, 2)

    both = [(0, 1), (1, 0)]
    own = lax.all_to_all(packed, X, 0, 0, tiled=True).reshape(n_x, frames, strip, width)
    ends = [jnp.concatenate([features[i], cotangent[i]], axis=1) for i in (0, -1)]
    edges = lax.all_gather(jnp.where(core == 0, ends[1], ends[0]), "c")
    across = [(d, (d - 1) % n_dp if d % 2 == 0 else (d + 1) % n_dp) for d in range(n_dp)]
    halo = lax.ppermute(jnp.where(core == 0, ends[0], ends[1]), DP, across)
    own, w_far, w_near, halo, edges = lax.optimization_barrier((own, w_far, w_near, halo, edges))
    sib = lax.ppermute(own, "c", both)
    z_next = [(2 * i, (2 * i - 1) % (2 * n_z)) for i in range(n_z)] + [(2 * i + 1, (2 * i + 2) % (2 * n_z)) for i in range(n_z)]
    edge = jnp.where(core == 0, own[:, 0, :, :384], own[:, -1, :, :384])
    halo_x = lax.ppermute(edge, ("z", "c"), z_next)

    _, clip_lengths, cycle_start = lax.optimization_barrier((edge, clip_lengths, cycle_start))
    first = (jnp.arange(2, dtype=jnp.int32) * n_z + z)[:, None] * (2 * frames)
    chip_frames = (first + jnp.arange(2 * frames, dtype=jnp.int32)).reshape(-1)
    prev_all, next_all = border_flags(clip_lengths, cycle_start, chip_frames, total_frames)
    wrapped = jnp.where(core == 0, z == 0, z == n_z - 1)
    place = jnp.stack([core, xl, wrapped.astype(jnp.int32)]).astype(jnp.int32)
    term = x_term(place, prev_all, next_all, own, sib, halo_x)

    _, w_far, w_near = lax.optimization_barrier((term, w_far, w_near))
    parity = z % 2
    pair = jnp.stack([jnp.where((parity == 1) & (core == 1), temporal_weight, w_far), w_near])
    pair_far = lax.ppermute(pair, "z", [(i, i ^ 1) for i in range(n_z)])
    blocks = jnp.concatenate([pair, pair_far])
    pairs = [(i, i ^ (1 if i // 2 % 2 == 0 else 5)) for i in range(8)]
    blocks_far = lax.ppermute(blocks, ("xh", "c", "xl"), pairs)

    part = lax.all_to_all(term.reshape(n_y, 320 // n_y, 512), "y", 0, 0, tiled=True)
    part, blocks = lax.optimization_barrier((part, blocks))
    part = part.sum(0)
    local_rows = part.shape[0]
    n_xz = 2 * n_z
    pieces = jnp.pad(part, ((0, 48 - local_rows), (0, 0))).reshape(6, 8, 2, 256).transpose(0, 2, 1, 3).reshape(n_z, 8, 256)
    _, blocks, blocks_far = lax.optimization_barrier((pieces, blocks, blocks_far))
    blocks_sib = lax.ppermute(blocks, "c", both)
    mine = lax.all_to_all(pieces, "z", 0, 0, tiled=True)
    mine = mine.sum(0) * (1.0 / math.sqrt(total_frames * strip * lax.axis_size(FSDP)))
    mine = jnp.broadcast_to(mine[None], (n_xz, 8, 256))
    weights = (blocks, blocks_far, blocks_sib, lax.ppermute(blocks_far, "c", both))
    _, weights = lax.optimization_barrier((mine, weights))
    gathered = lax.all_to_all(mine, ("xh", "z"), 0, 0, tiled=True)
    place_out = jnp.stack([core, xh * (2 * frames) + core * frames, xl, y, parity]).astype(jnp.int32)
    block_out, grad_features = outputs(
        place_out, prev_all, next_all, features, cotangent, skip_input, halo, edges, *weights
    )
    gathered, block_out, grad_features = lax.optimization_barrier((gathered, block_out, grad_features))
    gathered = lax.all_gather(gathered, "c")

    def flat(a):
        a = a.reshape(2, 6, 2, 8, 256).transpose(0, 1, 3, 2, 4)
        return a.reshape(2, 48, 512)[:, :local_rows]

    low, high = flat(gathered[0]), flat(gathered[1])

    def outer_tap(b):
        return [b[0, :, :320], b[1, :, 256:320], b[1, :, :256]]

    tap_1 = [low[0, :, 384:], high[0, :, 384:], low[0, :, 320:384], low[1, :, 320:], high[1, :, 384:]]
    grad_weight = jnp.concatenate(outer_tap(low) + tap_1 + outer_tap(high), axis=1)

    return (block_out, grad_features, grad_weight)


def solution(mesh):
    split = Mesh(mesh.devices.reshape(2, 12, 2, 2, 8), DP + FSDP)
    tokens = P(DP, FSDP, None)
    in_specs = (tokens, tokens, tokens, P(FSDP, None), P(), P())
    out_specs = (tokens, tokens, P(FSDP, None))
    return jax.shard_map(shards, mesh=split, in_specs=in_specs, out_specs=out_specs, check_vma=False)
```

```python
import math

import jax
import jax.numpy as jnp
from jax import lax
from jax.experimental import pallas as pl
from jax.experimental.pallas import tpu as pltpu
from jax.sharding import Mesh, PartitionSpec as P

DP = ("xh", "z", "c")
FSDP = ("xl", "y")
X = ("xh", "xl")


def border_flags(clip_lengths, cycle_start, frame_index, total):
    clip = jnp.arange(clip_lengths.shape[0], dtype=jnp.int32)
    starts = jnp.sum(jnp.where(clip[None, :] < clip[:, None], clip_lengths[None, :], 0), axis=1)
    position = jnp.mod(frame_index - cycle_start[0], total)
    following = jnp.mod(frame_index + 1 - cycle_start[0], total)
    first_here = jnp.any(starts[:, None] == position[None, :], axis=0)
    first_next = jnp.any(starts[:, None] == following[None, :], axis=0)
    return (1 - first_here.astype(jnp.int32), 1 - first_next.astype(jnp.int32))


def pack_kernel(f_hbm, g_hbm, out_hbm, f_ref, g_ref, out_ref, in_sems, out_sems):
    steps = f_ref.shape[0]
    frames, strip, width = f_ref.shape[1:]
    rows = frames * strip

    def fetch(i):
        return [
            pltpu.make_async_copy(src.at[pl.ds(i * frames, frames)], dst.at[i], in_sems.at[i, k])
            for k, (src, dst) in enumerate(((f_hbm, f_ref), (g_hbm, g_ref)))
        ]

    def send(i):
        return pltpu.make_async_copy(out_ref.at[i], out_hbm.at[:, pl.ds(i * rows, rows), :], out_sems.at[i])

    for i in range(steps):
        for copy in fetch(i):
            copy.start()
    for i in range(steps):
        for copy in fetch(i):
            copy.wait()
        f = f_ref[i].reshape(rows, width)
        g = g_ref[i].reshape(rows, width)
        f_mid, g_mid = f[:, 256:384], g[:, 256:384]
        f_rolled, g_rolled = [pltpu.roll(m.astype(jnp.float32), 64, 1).astype(jnp.bfloat16) for m in (f_mid, g_mid)]
        left = lax.broadcasted_iota(jnp.int32, f_mid.shape, 1) < 64
        for xh in range(2):
            for xl in range(2):
                j = 2 * xh + xl
                out_ref[i, j, :, :256] = f[:, 384 * xl:384 * xl + 256]
                out_ref[i, j, :, 256:384] = jnp.where(left, f_rolled if xl else f_mid, g_mid if xh else g_rolled)
                out_ref[i, j, :, 384:] = g[:, 384 * xh:384 * xh + 256]
        send(i).start()
    for i in range(steps):
        send(i).wait()


def pack(features, cotangent):
    frames, strip, width = features.shape
    steps = 2
    hbm = pl.BlockSpec(memory_space=pltpu.HBM)
    part = pltpu.VMEM((steps, frames // steps, strip, width), jnp.bfloat16)
    return pl.pallas_call(
        pack_kernel,
        out_shape=jax.ShapeDtypeStruct((4, frames * strip, width), jnp.bfloat16),
        in_specs=[hbm] * 2,
        out_specs=hbm,
        scratch_shapes=[
            part, part, pltpu.VMEM((steps, 4, frames * strip // steps, width), jnp.bfloat16),
            pltpu.SemaphoreType.DMA((steps, 2)), pltpu.SemaphoreType.DMA((steps,)),
        ],
        compiler_params=pltpu.CompilerParams(vmem_limit_bytes=60 << 20),
        name="pack",
    )(features, cotangent)


def term_kernel(place_ref, prev_ref, next_ref, own_ref, sib_ref, halo_ref, out_ref, fa_own, fa_sib):
    chips, frames, strip, _ = own_ref.shape
    core, xl, wrapped = place_ref[0], place_ref[1], place_ref[2]

    def put(dst, chip, slot, value, ok):
        dst[pl.ds((chip * frames + slot) * strip, strip), :] = jnp.where(ok != 0, value, jnp.zeros_like(value))

    def halo(chip):
        return halo_ref[(chip // 2 + wrapped) % 2 * 2 + chip % 2]

    @pl.when(core == 0)
    def _():
        for chip in range(chips):
            at = chip // 2 * 2 * frames
            for j in range(frames):
                mine = halo(chip) if j == 0 else own_ref[chip, j - 1, :, :384]
                its = own_ref[chip, frames - 1, :, :384] if j == 0 else sib_ref[chip, j - 1, :, :384]
                put(fa_own, chip, j, mine, prev_ref[at + j])
                put(fa_sib, chip, j, its, prev_ref[at + frames + j])

    @pl.when(core != 0)
    def _():
        for chip in range(chips):
            at = chip // 2 * 2 * frames
            for j in range(frames):
                mine = halo(chip) if j == frames - 1 else own_ref[chip, j + 1, :, :384]
                its = own_ref[chip, 0, :, :384] if j == frames - 1 else sib_ref[chip, j + 1, :, :384]
                put(fa_own, chip, j, mine, next_ref[at + frames + j])
                put(fa_sib, chip, j, its, next_ref[at + j])

    def flat(ref, start, stop):
        return ref[:, :, :, start:stop].reshape(chips * frames * strip, stop - start)

    def dot(a, b):
        return lax.dot_general(a, b, (((0,), (0,)), ((), ())), preferred_element_type=jnp.float32)

    def center(start, stop):
        return dot(flat(own_ref, 0, 384), flat(own_ref, start, stop)) + dot(flat(sib_ref, 0, 384), flat(sib_ref, start, stop))

    outer = dot(fa_own[...], flat(own_ref, 256, 640)) + dot(fa_sib[...], flat(sib_ref, 256, 640))
    left = lax.broadcasted_iota(jnp.int32, (384, 128), 1) < 64
    rolled = pltpu.roll(outer[:, :128], 64, 1)

    def store(start, stop, value):
        @pl.when(xl == 0)
        def _():
            out_ref[:, start:stop] = value[:320]

        @pl.when(xl != 0)
        def _():
            out_ref[64:, start:stop] = value[:256]
            out_ref[:64, start:stop] = value[256:320]

    store(0, 256, outer[:, 128:])

    @pl.when(core == 0)
    def _():
        mid = center(256, 512)
        store(256, 384, jnp.where(left, rolled, mid[:, :128]))
        store(384, 512, mid[:, 128:])

    @pl.when(core != 0)
    def _():
        store(256, 384, jnp.where(left, rolled, jnp.zeros_like(rolled)))
        store(384, 512, center(512, 640))


def x_term(place, prev_ok, next_ok, own, sib, halo):
    smem = pl.BlockSpec(memory_space=pltpu.SMEM)
    vmem = pl.BlockSpec(memory_space=pltpu.VMEM)
    chips, frames, strip, _ = own.shape
    buf = pltpu.VMEM((chips * frames * strip, 384), jnp.bfloat16)
    return pl.pallas_call(
        term_kernel,
        out_shape=jax.ShapeDtypeStruct((320, 512), jnp.float32),
        in_specs=[smem] * 3 + [vmem] * 3,
        out_specs=vmem,
        scratch_shapes=[buf, buf],
        compiler_params=pltpu.CompilerParams(vmem_limit_bytes=20 << 20),
        name="x_term",
    )(place, prev_ok, next_ok, own, sib, halo)


def out_kernel(place_ref, prev_ref, next_ref, f_ref, g_ref, skip_ref, halo_ref, edge_ref, *refs):
    weights, (out_ref, back_ref, f_lo, f_hi, g_lo, g_hi, blocks, weight) = refs[:4], refs[4:]
    frames, strip, width = f_ref.shape
    tokens = frames * strip
    core, at, xl, y, parity = [place_ref[i] for i in range(5)]
    count, rows = weights[0].shape[:2]

    def put(dst, j, value, ok):
        dst[pl.ds(j * strip, strip), :] = jnp.where(ok != 0, value, jnp.zeros_like(value))

    for src, lo, hi, lanes in ((f_ref, f_lo, f_hi, slice(0, width)), (g_ref, g_lo, g_hi, slice(width, 2 * width))):
        halo, edge = halo_ref[:, lanes], edge_ref[1 - core, :, lanes]
        for j in range(frames):
            put(lo, j, jnp.where(core == 0, halo, edge) if j == 0 else src[j - 1], prev_ref[at + j])
            put(hi, j, jnp.where(core == 0, edge, halo) if j == frames - 1 else src[j + 1], next_ref[at + j])

    for i in range(count):
        odd = parity if i < 2 else 1 - parity
        low, high = (3 + odd, jnp.where(odd == 0, 5, 0)) if i % 2 == 0 else (1 + odd, 7 - odd)
        for half in range(2):
            blocks[half, jnp.where(core == 0, low, high)] = weights[half][i]
            blocks[half, jnp.where(core == 0, high, low)] = weights[2 + half][i]
    for half in range(2):
        for i in range(2 * count):
            start = (half * 2 * count + i) * rows
            weight[start:start + rows, :] = blocks[(half + xl) % 2, (y - i + 2 * count) % (2 * count)]

    def dot(a, b):
        return jnp.dot(a, b, preferred_element_type=jnp.float32)

    def dot_t(a, b):
        return lax.dot_general(a, b, (((1,), (1,)), ((), ())), preferred_element_type=jnp.float32)

    f = f_ref[...].reshape(tokens, width)
    g = g_ref[...].reshape(tokens, width)
    taps = [weight[:, k * width:(k + 1) * width] for k in range(3)]
    mixed = dot(f_lo[...], taps[0]) + dot(f, taps[1]) + dot(f_hi[...], taps[2])
    mixed = mixed.reshape(frames, strip, width) + skip_ref[...].astype(jnp.float32)
    out_ref[...] = mixed.astype(jnp.bfloat16)
    back = dot_t(g_hi[...], taps[0]) + dot_t(g, taps[1]) + dot_t(g_lo[...], taps[2])
    back_ref[...] = back.reshape(frames, strip, width).astype(jnp.bfloat16)


def outputs(place, prev_ok, next_ok, features, cotangent, skip_input, halo, edge, *weights):
    frames, strip, width = features.shape
    smem = pl.BlockSpec(memory_space=pltpu.SMEM)
    vmem = pl.BlockSpec(memory_space=pltpu.VMEM)
    buf = pltpu.VMEM((frames * strip, width), jnp.bfloat16)
    out = jax.ShapeDtypeStruct(features.shape, jnp.bfloat16)
    return pl.pallas_call(
        out_kernel,
        out_shape=(out, out),
        in_specs=[smem] * 3 + [vmem] * 9,
        out_specs=(vmem, vmem),
        scratch_shapes=[buf] * 4 + [pltpu.VMEM((2, 8, 40, 3 * width), jnp.bfloat16), pltpu.VMEM((width, 3 * width), jnp.bfloat16)],
        compiler_params=pltpu.CompilerParams(vmem_limit_bytes=28 << 20),
        name="outputs",
    )(place, prev_ok, next_ok, features, cotangent, skip_input, halo, edge, *weights)


def shards(features, skip_input, cotangent, temporal_weight, clip_lengths, cycle_start):
    frames, strip, width = features.shape
    core, xl, xh, z, y = [lax.axis_index(a) for a in ("c", "xl", "xh", "z", "y")]
    n_x, n_y, n_z = lax.axis_size(X), lax.axis_size("y"), lax.axis_size("z")
    n_dp = lax.axis_size(DP)
    total_frames = frames * n_dp

    packed = pack(features, cotangent)
    _, temporal_weight = lax.optimization_barrier((packed, temporal_weight))

    def from_y(even, odd):
        pairs = []
        for plane in range(n_z):
            distance = (even, odd)[plane % 2]
            for side in range(2 if 2 * distance < n_y else 1):
                base = (2 * plane + side) * n_y
                pairs += [(base + i, base + (i + (1 - 2 * side) * distance) % n_y) for i in range(n_y)]
        return lax.ppermute(temporal_weight, ("z", "c", "y"), pairs)

    w_far, w_near = from_y(3, 4), from_y(1, 2)

    both = [(0, 1), (1, 0)]
    own = lax.all_to_all(packed, X, 0, 0, tiled=True).reshape(n_x, frames, strip, width)
    ends = [jnp.concatenate([features[i], cotangent[i]], axis=1) for i in (0, -1)]
    edges = lax.all_gather(jnp.where(core == 0, ends[1], ends[0]), "c")
    across = [(d, (d - 1) % n_dp if d % 2 == 0 else (d + 1) % n_dp) for d in range(n_dp)]
    halo = lax.ppermute(jnp.where(core == 0, ends[0], ends[1]), DP, across)
    own, w_far, w_near, halo, edges = lax.optimization_barrier((own, w_far, w_near, halo, edges))
    sib = lax.ppermute(own, "c", both)
    z_next = [(2 * i, (2 * i - 1) % (2 * n_z)) for i in range(n_z)] + [(2 * i + 1, (2 * i + 2) % (2 * n_z)) for i in range(n_z)]
    edge = jnp.where(core == 0, own[:, 0, :, :384], own[:, -1, :, :384])
    halo_x = lax.ppermute(edge, ("z", "c"), z_next)

    _, clip_lengths, cycle_start = lax.optimization_barrier((edge, clip_lengths, cycle_start))
    first = (jnp.arange(2, dtype=jnp.int32) * n_z + z)[:, None] * (2 * frames)
    chip_frames = (first + jnp.arange(2 * frames, dtype=jnp.int32)).reshape(-1)
    prev_all, next_all = border_flags(clip_lengths, cycle_start, chip_frames, total_frames)
    wrapped = jnp.where(core == 0, z == 0, z == n_z - 1)
    place = jnp.stack([core, xl, wrapped.astype(jnp.int32)]).astype(jnp.int32)
    term = x_term(place, prev_all, next_all, own, sib, halo_x)

    _, w_far, w_near = lax.optimization_barrier((term, w_far, w_near))
    parity = z % 2
    pair = jnp.stack([jnp.where((parity == 1) & (core == 1), temporal_weight, w_far), w_near])
    pair_far = lax.ppermute(pair, "z", [(i, i ^ 1) for i in range(n_z)])
    blocks = jnp.concatenate([pair, pair_far])
    pairs = [(i, i ^ (1 if i // 2 % 2 == 0 else 5)) for i in range(8)]
    blocks_far = lax.ppermute(blocks, ("xh", "c", "xl"), pairs)

    part = lax.all_to_all(term.reshape(n_y, 320 // n_y, 512), "y", 0, 0, tiled=True)
    part, blocks = lax.optimization_barrier((part, blocks))
    part = part.sum(0)
    local_rows = part.shape[0]
    n_xz = 2 * n_z
    pieces = jnp.pad(part, ((0, 48 - local_rows), (0, 0))).reshape(6, 8, 2, 256).transpose(0, 2, 1, 3).reshape(n_z, 8, 256)
    _, blocks, blocks_far = lax.optimization_barrier((pieces, blocks, blocks_far))
    blocks_sib = lax.ppermute(blocks, "c", both)
    mine = lax.all_to_all(pieces, "z", 0, 0, tiled=True)
    mine = mine.sum(0) * (1.0 / math.sqrt(total_frames * strip * lax.axis_size(FSDP)))
    mine = jnp.broadcast_to(mine[None], (n_xz, 8, 256))
    weights = (blocks, blocks_far, blocks_sib, lax.ppermute(blocks_far, "c", both))
    _, weights = lax.optimization_barrier((mine, weights))
    gathered = lax.all_to_all(mine, ("xh", "z"), 0, 0, tiled=True)
    place_out = jnp.stack([core, xh * (2 * frames) + core * frames, xl, y, parity]).astype(jnp.int32)
    block_out, grad_features = outputs(
        place_out, prev_all, next_all, features, cotangent, skip_input, halo, edges, *weights
    )
    gathered, block_out, grad_features = lax.optimization_barrier((gathered, block_out, grad_features))
    gathered = lax.all_gather(gathered, "c")

    def flat(a):
        a = a.reshape(2, 6, 2, 8, 256).transpose(0, 1, 3, 2, 4)
        return a.reshape(2, 48, 512)[:, :local_rows]

    low, high = flat(gathered[0]), flat(gathered[1])

    def outer_tap(b):
        return [b[0, :, :320], b[1, :, 256:320], b[1, :, :256]]

    tap_1 = [low[0, :, 384:], high[0, :, 384:], low[0, :, 320:384], low[1, :, 320:], high[1, :, 384:]]
    grad_weight = jnp.concatenate(outer_tap(low) + tap_1 + outer_tap(high), axis=1)

    return (block_out, grad_features, grad_weight)


def solution(mesh):
    split = Mesh(mesh.devices.reshape(2, 12, 2, 2, 8), DP + FSDP)
    tokens = P(DP, FSDP, None)
    in_specs = (tokens, tokens, tokens, P(FSDP, None), P(), P())
    out_specs = (tokens, tokens, P(FSDP, None))
    return jax.shard_map(shards, mesh=split, in_specs=in_specs, out_specs=out_specs, check_vma=False)
```

```python
import math

import jax
import jax.numpy as jnp
from jax import lax
from jax.experimental import pallas as pl
from jax.experimental.pallas import tpu as pltpu
from jax.sharding import Mesh, PartitionSpec as P

DP = ("xh", "z", "c")
FSDP = ("xl", "y")
X = ("xh", "xl")


def border_flags(clip_lengths, cycle_start, frame_index, total):
    clip = jnp.arange(clip_lengths.shape[0], dtype=jnp.int32)
    starts = jnp.sum(jnp.where(clip[None, :] < clip[:, None], clip_lengths[None, :], 0), axis=1)
    position = jnp.mod(frame_index - cycle_start[0], total)
    following = jnp.mod(frame_index + 1 - cycle_start[0], total)
    first_here = jnp.any(starts[:, None] == position[None, :], axis=0)
    first_next = jnp.any(starts[:, None] == following[None, :], axis=0)
    return (1 - first_here.astype(jnp.int32), 1 - first_next.astype(jnp.int32))


def pack_kernel(f_hbm, g_hbm, out_hbm, f_ref, g_ref, out_ref, in_sems, out_sems):
    steps = f_ref.shape[0]
    frames, strip, width = f_ref.shape[1:]
    rows = frames * strip

    def fetch(i):
        return [
            pltpu.make_async_copy(src.at[pl.ds(i * frames, frames)], dst.at[i], in_sems.at[i, k])
            for k, (src, dst) in enumerate(((f_hbm, f_ref), (g_hbm, g_ref)))
        ]

    def send(i):
        return pltpu.make_async_copy(out_ref.at[i], out_hbm.at[:, pl.ds(i * rows, rows), :], out_sems.at[i])

    for i in range(steps):
        for copy in fetch(i):
            copy.start()
    for i in range(steps):
        for copy in fetch(i):
            copy.wait()
        f = f_ref[i].reshape(rows, width)
        g = g_ref[i].reshape(rows, width)
        f_mid, g_mid = f[:, 256:384], g[:, 256:384]
        f_rolled, g_rolled = [pltpu.roll(m.astype(jnp.float32), 64, 1).astype(jnp.bfloat16) for m in (f_mid, g_mid)]
        left = lax.broadcasted_iota(jnp.int32, f_mid.shape, 1) < 64
        for xh in range(2):
            for xl in range(2):
                j = 2 * xh + xl
                out_ref[i, j, :, :256] = f[:, 384 * xl:384 * xl + 256]
                out_ref[i, j, :, 256:384] = jnp.where(left, f_rolled if xl else f_mid, g_mid if xh else g_rolled)
                out_ref[i, j, :, 384:] = g[:, 384 * xh:384 * xh + 256]
        send(i).start()
    for i in range(steps):
        send(i).wait()


def pack(features, cotangent):
    frames, strip, width = features.shape
    steps = 2
    hbm = pl.BlockSpec(memory_space=pltpu.HBM)
    part = pltpu.VMEM((steps, frames // steps, strip, width), jnp.bfloat16)
    return pl.pallas_call(
        pack_kernel,
        out_shape=jax.ShapeDtypeStruct((4, frames * strip, width), jnp.bfloat16),
        in_specs=[hbm] * 2,
        out_specs=hbm,
        scratch_shapes=[
            part, part, pltpu.VMEM((steps, 4, frames * strip // steps, width), jnp.bfloat16),
            pltpu.SemaphoreType.DMA((steps, 2)), pltpu.SemaphoreType.DMA((steps,)),
        ],
        compiler_params=pltpu.CompilerParams(vmem_limit_bytes=60 << 20),
        name="pack",
    )(features, cotangent)


def put(dst, slot, value, ok):
    rows = value.shape[0]
    dst[pl.ds(slot * rows, rows), :] = jnp.where(ok != 0, value, jnp.zeros_like(value))


def lanes(ref, start, stop):
    return ref[:, :, :, start:stop].reshape(-1, stop - start)


def term_dot(a, b):
    return lax.dot_general(a, b, (((0,), (0,)), ((), ())), preferred_element_type=jnp.float32)


def own_kernel(place_ref, prev_ref, next_ref, own_ref, outer_ref, mid_ref, fa):
    chips, frames, strip, _ = own_ref.shape
    core = place_ref[0]
    nothing = jnp.zeros((strip, 384), jnp.bfloat16)

    @pl.when(core == 0)
    def _():
        for chip in range(chips):
            at = chip // 2 * 2 * frames
            for j in range(frames):
                put(fa, chip * frames + j, nothing if j == 0 else own_ref[chip, j - 1, :, :384], prev_ref[at + j])
        mid_ref[...] = term_dot(lanes(own_ref, 0, 384), lanes(own_ref, 256, 512))

    @pl.when(core != 0)
    def _():
        for chip in range(chips):
            at = chip // 2 * 2 * frames + frames
            for j in range(frames):
                put(fa, chip * frames + j, nothing if j == frames - 1 else own_ref[chip, j + 1, :, :384], next_ref[at + j])
        mid_ref[:, :128] = term_dot(lanes(own_ref, 0, 384), lanes(own_ref, 512, 640))
        mid_ref[:, 128:] = jnp.zeros((384, 128), jnp.float32)

    outer_ref[...] = term_dot(fa[...], lanes(own_ref, 256, 640))


def own_term(place, prev_ok, next_ok, own):
    smem = pl.BlockSpec(memory_space=pltpu.SMEM)
    vmem = pl.BlockSpec(memory_space=pltpu.VMEM)
    chips, frames, strip, _ = own.shape
    return pl.pallas_call(
        own_kernel,
        out_shape=(jax.ShapeDtypeStruct((384, 384), jnp.float32), jax.ShapeDtypeStruct((384, 256), jnp.float32)),
        in_specs=[smem] * 3 + [vmem],
        out_specs=(vmem, vmem),
        scratch_shapes=[pltpu.VMEM((chips * frames * strip, 384), jnp.bfloat16)],
        compiler_params=pltpu.CompilerParams(vmem_limit_bytes=20 << 20),
        name="own_term",
    )(place, prev_ok, next_ok, own)


def term_kernel(place_ref, prev_ref, next_ref, own_ref, sib_ref, halo_ref, outer_ref, mid_ref, out_ref, fa, fh, gh):
    chips, frames, strip, _ = own_ref.shape
    core, xl, wrapped = place_ref[0], place_ref[1], place_ref[2]

    def halo(chip):
        return halo_ref[(chip // 2 + wrapped) % 2 * 2 + chip % 2]

    @pl.when(core == 0)
    def _():
        for chip in range(chips):
            at = chip // 2 * 2 * frames
            put(fh, chip, halo(chip), prev_ref[at])
            gh[pl.ds(chip * strip, strip), :] = own_ref[chip, 0, :, 256:]
            for j in range(frames):
                its = own_ref[chip, frames - 1, :, :384] if j == 0 else sib_ref[chip, j - 1, :, :384]
                put(fa, chip * frames + j, its, prev_ref[at + frames + j])

    @pl.when(core != 0)
    def _():
        for chip in range(chips):
            at = chip // 2 * 2 * frames
            put(fh, chip, halo(chip), next_ref[at + 2 * frames - 1])
            gh[pl.ds(chip * strip, strip), :] = own_ref[chip, frames - 1, :, 256:]
            for j in range(frames):
                its = own_ref[chip, 0, :, :384] if j == frames - 1 else sib_ref[chip, j + 1, :, :384]
                put(fa, chip * frames + j, its, next_ref[at + j])

    def center(start, stop):
        return mid_ref[:, :stop - start] + term_dot(lanes(sib_ref, 0, 384), lanes(sib_ref, start, stop))

    outer = outer_ref[...] + term_dot(fa[...], lanes(sib_ref, 256, 640)) + term_dot(fh[...], gh[...])
    left = lax.broadcasted_iota(jnp.int32, (384, 128), 1) < 64
    rolled = pltpu.roll(outer[:, :128], 64, 1)

    def store(start, stop, value):
        @pl.when(xl == 0)
        def _():
            out_ref[:, start:stop] = value[:320]

        @pl.when(xl != 0)
        def _():
            out_ref[64:, start:stop] = value[:256]
            out_ref[:64, start:stop] = value[256:320]

    store(0, 256, outer[:, 128:])

    @pl.when(core == 0)
    def _():
        mid = center(256, 512)
        store(256, 384, jnp.where(left, rolled, mid[:, :128]))
        store(384, 512, mid[:, 128:])

    @pl.when(core != 0)
    def _():
        store(256, 384, jnp.where(left, rolled, jnp.zeros_like(rolled)))
        store(384, 512, center(512, 640))


def x_term(place, prev_ok, next_ok, own, sib, halo, outer, mid):
    smem = pl.BlockSpec(memory_space=pltpu.SMEM)
    vmem = pl.BlockSpec(memory_space=pltpu.VMEM)
    chips, frames, strip, _ = own.shape
    few = pltpu.VMEM((chips * strip, 384), jnp.bfloat16)
    return pl.pallas_call(
        term_kernel,
        out_shape=jax.ShapeDtypeStruct((320, 512), jnp.float32),
        in_specs=[smem] * 3 + [vmem] * 5,
        out_specs=vmem,
        scratch_shapes=[pltpu.VMEM((chips * frames * strip, 384), jnp.bfloat16), few, few],
        compiler_params=pltpu.CompilerParams(vmem_limit_bytes=20 << 20),
        name="x_term",
    )(place, prev_ok, next_ok, own, sib, halo, outer, mid)


def out_kernel(place_ref, prev_ref, next_ref, f_ref, g_ref, skip_ref, halo_ref, edge_ref, *refs):
    weights, (out_ref, back_ref, f_lo, f_hi, g_lo, g_hi, blocks, weight) = refs[:4], refs[4:]
    frames, strip, width = f_ref.shape
    tokens = frames * strip
    core, at, xl, y, parity = [place_ref[i] for i in range(5)]
    count, rows = weights[0].shape[:2]

    def put(dst, j, value, ok):
        dst[pl.ds(j * strip, strip), :] = jnp.where(ok != 0, value, jnp.zeros_like(value))

    for src, lo, hi, lanes in ((f_ref, f_lo, f_hi, slice(0, width)), (g_ref, g_lo, g_hi, slice(width, 2 * width))):
        halo, edge = halo_ref[:, lanes], edge_ref[1 - core, :, lanes]
        for j in range(frames):
            put(lo, j, jnp.where(core == 0, halo, edge) if j == 0 else src[j - 1], prev_ref[at + j])
            put(hi, j, jnp.where(core == 0, edge, halo) if j == frames - 1 else src[j + 1], next_ref[at + j])

    for i in range(count):
        odd = parity if i < 2 else 1 - parity
        low, high = (3 + odd, jnp.where(odd == 0, 5, 0)) if i % 2 == 0 else (1 + odd, 7 - odd)
        for half in range(2):
            blocks[half, jnp.where(core == 0, low, high)] = weights[half][i]
            blocks[half, jnp.where(core == 0, high, low)] = weights[2 + half][i]
    for half in range(2):
        for i in range(2 * count):
            start = (half * 2 * count + i) * rows
            weight[start:start + rows, :] = blocks[(half + xl) % 2, (y - i + 2 * count) % (2 * count)]

    def dot(a, b):
        return jnp.dot(a, b, preferred_element_type=jnp.float32)

    def dot_t(a, b):
        return lax.dot_general(a, b, (((1,), (1,)), ((), ())), preferred_element_type=jnp.float32)

    f = f_ref[...].reshape(tokens, width)
    g = g_ref[...].reshape(tokens, width)
    taps = [weight[:, k * width:(k + 1) * width] for k in range(3)]
    mixed = dot(f_lo[...], taps[0]) + dot(f, taps[1]) + dot(f_hi[...], taps[2])
    mixed = mixed.reshape(frames, strip, width) + skip_ref[...].astype(jnp.float32)
    out_ref[...] = mixed.astype(jnp.bfloat16)
    back = dot_t(g_hi[...], taps[0]) + dot_t(g, taps[1]) + dot_t(g_lo[...], taps[2])
    back_ref[...] = back.reshape(frames, strip, width).astype(jnp.bfloat16)


def outputs(place, prev_ok, next_ok, features, cotangent, skip_input, halo, edge, *weights):
    frames, strip, width = features.shape
    smem = pl.BlockSpec(memory_space=pltpu.SMEM)
    vmem = pl.BlockSpec(memory_space=pltpu.VMEM)
    buf = pltpu.VMEM((frames * strip, width), jnp.bfloat16)
    out = jax.ShapeDtypeStruct(features.shape, jnp.bfloat16)
    return pl.pallas_call(
        out_kernel,
        out_shape=(out, out),
        in_specs=[smem] * 3 + [vmem] * 9,
        out_specs=(vmem, vmem),
        scratch_shapes=[buf] * 4 + [pltpu.VMEM((2, 8, 40, 3 * width), jnp.bfloat16), pltpu.VMEM((width, 3 * width), jnp.bfloat16)],
        compiler_params=pltpu.CompilerParams(vmem_limit_bytes=28 << 20),
        name="outputs",
    )(place, prev_ok, next_ok, features, cotangent, skip_input, halo, edge, *weights)


def shards(features, skip_input, cotangent, temporal_weight, clip_lengths, cycle_start):
    frames, strip, width = features.shape
    core, xl, xh, z, y = [lax.axis_index(a) for a in ("c", "xl", "xh", "z", "y")]
    n_x, n_y, n_z = lax.axis_size(X), lax.axis_size("y"), lax.axis_size("z")
    n_dp = lax.axis_size(DP)
    total_frames = frames * n_dp

    packed = pack(features, cotangent)
    _, temporal_weight = lax.optimization_barrier((packed, temporal_weight))

    def from_y(even, odd):
        pairs = []
        for plane in range(n_z):
            distance = (even, odd)[plane % 2]
            for side in range(2 if 2 * distance < n_y else 1):
                base = (2 * plane + side) * n_y
                pairs += [(base + i, base + (i + (1 - 2 * side) * distance) % n_y) for i in range(n_y)]
        return lax.ppermute(temporal_weight, ("z", "c", "y"), pairs)

    w_far, w_near = from_y(3, 4), from_y(1, 2)

    both = [(0, 1), (1, 0)]
    own = lax.all_to_all(packed, X, 0, 0, tiled=True).reshape(n_x, frames, strip, width)
    ends = [jnp.concatenate([features[i], cotangent[i]], axis=1) for i in (0, -1)]
    edges = lax.all_gather(jnp.where(core == 0, ends[1], ends[0]), "c")
    across = [(d, (d - 1) % n_dp if d % 2 == 0 else (d + 1) % n_dp) for d in range(n_dp)]
    halo = lax.ppermute(jnp.where(core == 0, ends[0], ends[1]), DP, across)
    own, w_far, w_near, halo, edges = lax.optimization_barrier((own, w_far, w_near, halo, edges))
    sib = lax.ppermute(own, "c", both)
    z_next = [(2 * i, (2 * i - 1) % (2 * n_z)) for i in range(n_z)] + [(2 * i + 1, (2 * i + 2) % (2 * n_z)) for i in range(n_z)]
    edge = jnp.where(core == 0, own[:, 0, :, :384], own[:, -1, :, :384])
    halo_x = lax.ppermute(edge, ("z", "c"), z_next)

    _, clip_lengths, cycle_start = lax.optimization_barrier((edge, clip_lengths, cycle_start))
    first = (jnp.arange(2, dtype=jnp.int32) * n_z + z)[:, None] * (2 * frames)
    chip_frames = (first + jnp.arange(2 * frames, dtype=jnp.int32)).reshape(-1)
    prev_all, next_all = border_flags(clip_lengths, cycle_start, chip_frames, total_frames)
    wrapped = jnp.where(core == 0, z == 0, z == n_z - 1)
    place = jnp.stack([core, xl, wrapped.astype(jnp.int32)]).astype(jnp.int32)
    outer, mid = own_term(place, prev_all, next_all, own)
    term = x_term(place, prev_all, next_all, own, sib, halo_x, outer, mid)

    _, w_far, w_near = lax.optimization_barrier((term, w_far, w_near))
    parity = z % 2
    pair = jnp.stack([jnp.where((parity == 1) & (core == 1), temporal_weight, w_far), w_near])
    pair_far = lax.ppermute(pair, "z", [(i, i ^ 1) for i in range(n_z)])
    blocks = jnp.concatenate([pair, pair_far])
    pairs = [(i, i ^ (1 if i // 2 % 2 == 0 else 5)) for i in range(8)]
    blocks_far = lax.ppermute(blocks, ("xh", "c", "xl"), pairs)

    part = lax.all_to_all(term.reshape(n_y, 320 // n_y, 512), "y", 0, 0, tiled=True)
    part, blocks = lax.optimization_barrier((part, blocks))
    part = part.sum(0)
    local_rows = part.shape[0]
    n_xz = 2 * n_z
    pieces = jnp.pad(part, ((0, 48 - local_rows), (0, 0))).reshape(6, 8, 2, 256).transpose(0, 2, 1, 3).reshape(n_z, 8, 256)
    _, blocks, blocks_far = lax.optimization_barrier((pieces, blocks, blocks_far))
    blocks_sib = lax.ppermute(blocks, "c", both)
    mine = lax.all_to_all(pieces, "z", 0, 0, tiled=True)
    mine = mine.sum(0) * (1.0 / math.sqrt(total_frames * strip * lax.axis_size(FSDP)))
    mine = jnp.broadcast_to(mine[None], (n_xz, 8, 256))
    weights = (blocks, blocks_far, blocks_sib, lax.ppermute(blocks_far, "c", both))
    _, weights = lax.optimization_barrier((mine, weights))
    gathered = lax.all_to_all(mine, ("xh", "z"), 0, 0, tiled=True)
    place_out = jnp.stack([core, xh * (2 * frames) + core * frames, xl, y, parity]).astype(jnp.int32)
    block_out, grad_features = outputs(
        place_out, prev_all, next_all, features, cotangent, skip_input, halo, edges, *weights
    )
    gathered, block_out, grad_features = lax.optimization_barrier((gathered, block_out, grad_features))
    gathered = lax.all_gather(gathered, "c")

    def flat(a):
        a = a.reshape(2, 6, 2, 8, 256).transpose(0, 1, 3, 2, 4)
        return a.reshape(2, 48, 512)[:, :local_rows]

    low, high = flat(gathered[0]), flat(gathered[1])

    def outer_tap(b):
        return [b[0, :, :320], b[1, :, 256:320], b[1, :, :256]]

    tap_1 = [low[0, :, 384:], high[0, :, 384:], low[0, :, 320:384], low[1, :, 320:], high[1, :, 384:]]
    grad_weight = jnp.concatenate(outer_tap(low) + tap_1 + outer_tap(high), axis=1)

    return (block_out, grad_features, grad_weight)


def solution(mesh):
    split = Mesh(mesh.devices.reshape(2, 12, 2, 2, 8), DP + FSDP)
    tokens = P(DP, FSDP, None)
    in_specs = (tokens, tokens, tokens, P(FSDP, None), P(), P())
    out_specs = (tokens, tokens, P(FSDP, None))
    return jax.shard_map(shards, mesh=split, in_specs=in_specs, out_specs=out_specs, check_vma=False)
```

```python
import math

import jax
import jax.numpy as jnp
from jax import lax
from jax.experimental import pallas as pl
from jax.experimental.pallas import tpu as pltpu
from jax.sharding import Mesh, PartitionSpec as P

DP = ("xh", "z", "c")
FSDP = ("xl", "y")
X = ("xh", "xl")


def border_flags(clip_lengths, cycle_start, frame_index, total):
    clip = jnp.arange(clip_lengths.shape[0], dtype=jnp.int32)
    starts = jnp.sum(jnp.where(clip[None, :] < clip[:, None], clip_lengths[None, :], 0), axis=1)
    position = jnp.mod(frame_index - cycle_start[0], total)
    following = jnp.mod(frame_index + 1 - cycle_start[0], total)
    first_here = jnp.any(starts[:, None] == position[None, :], axis=0)
    first_next = jnp.any(starts[:, None] == following[None, :], axis=0)
    return (1 - first_here.astype(jnp.int32), 1 - first_next.astype(jnp.int32))


def pack_kernel(f_hbm, g_hbm, out_hbm, f_ref, g_ref, out_ref, in_sems, out_sems):
    steps = f_ref.shape[0]
    frames, strip, width = f_ref.shape[1:]
    rows = frames * strip

    def fetch(i):
        return [
            pltpu.make_async_copy(src.at[pl.ds(i * frames, frames)], dst.at[i], in_sems.at[i, k])
            for k, (src, dst) in enumerate(((f_hbm, f_ref), (g_hbm, g_ref)))
        ]

    def send(i):
        return pltpu.make_async_copy(out_ref.at[i], out_hbm.at[:, pl.ds(i * rows, rows), :], out_sems.at[i])

    for i in range(steps):
        for copy in fetch(i):
            copy.start()
    for i in range(steps):
        for copy in fetch(i):
            copy.wait()
        f = f_ref[i].reshape(rows, width)
        g = g_ref[i].reshape(rows, width)
        f_mid, g_mid = f[:, 256:384], g[:, 256:384]
        f_rolled, g_rolled = [pltpu.roll(m.astype(jnp.float32), 64, 1).astype(jnp.bfloat16) for m in (f_mid, g_mid)]
        left = lax.broadcasted_iota(jnp.int32, f_mid.shape, 1) < 64
        for xh in range(2):
            for xl in range(2):
                j = 2 * xh + xl
                out_ref[i, j, :, :256] = f[:, 384 * xl:384 * xl + 256]
                out_ref[i, j, :, 256:384] = jnp.where(left, f_rolled if xl else f_mid, g_mid if xh else g_rolled)
                out_ref[i, j, :, 384:] = g[:, 384 * xh:384 * xh + 256]
        send(i).start()
    for i in range(steps):
        send(i).wait()


def pack(features, cotangent):
    frames, strip, width = features.shape
    steps = 2
    hbm = pl.BlockSpec(memory_space=pltpu.HBM)
    part = pltpu.VMEM((steps, frames // steps, strip, width), jnp.bfloat16)
    return pl.pallas_call(
        pack_kernel,
        out_shape=jax.ShapeDtypeStruct((4, frames * strip, width), jnp.bfloat16),
        in_specs=[hbm] * 2,
        out_specs=hbm,
        scratch_shapes=[
            part, part, pltpu.VMEM((steps, 4, frames * strip // steps, width), jnp.bfloat16),
            pltpu.SemaphoreType.DMA((steps, 2)), pltpu.SemaphoreType.DMA((steps,)),
        ],
        compiler_params=pltpu.CompilerParams(vmem_limit_bytes=60 << 20),
        name="pack",
    )(features, cotangent)


def put(dst, slot, value, ok):
    rows = value.shape[0]
    dst[pl.ds(slot * rows, rows), :] = jnp.where(ok != 0, value, jnp.zeros_like(value))


def lanes(ref, start, stop):
    return ref[:, :, :, start:stop].reshape(-1, stop - start)


def term_dot(a, b):
    return lax.dot_general(a, b, (((0,), (0,)), ((), ())), preferred_element_type=jnp.float32)


def own_kernel(place_ref, prev_ref, next_ref, own_ref, outer_ref, mid_ref, fa):
    chips, frames, strip, _ = own_ref.shape
    core = place_ref[0]
    nothing = jnp.zeros((strip, 384), jnp.bfloat16)

    @pl.when(core == 0)
    def _():
        for chip in range(chips):
            at = chip // 2 * 2 * frames
            for j in range(frames):
                put(fa, chip * frames + j, nothing if j == 0 else own_ref[chip, j - 1, :, :384], prev_ref[at + j])
        mid_ref[...] = term_dot(lanes(own_ref, 0, 384), lanes(own_ref, 256, 512))

    @pl.when(core != 0)
    def _():
        for chip in range(chips):
            at = chip // 2 * 2 * frames + frames
            for j in range(frames):
                put(fa, chip * frames + j, nothing if j == frames - 1 else own_ref[chip, j + 1, :, :384], next_ref[at + j])
        mid_ref[:, :128] = term_dot(lanes(own_ref, 0, 384), lanes(own_ref, 512, 640))
        mid_ref[:, 128:] = jnp.zeros((384, 128), jnp.float32)

    outer_ref[...] = term_dot(fa[...], lanes(own_ref, 256, 640))


def own_term(place, prev_ok, next_ok, own):
    smem = pl.BlockSpec(memory_space=pltpu.SMEM)
    vmem = pl.BlockSpec(memory_space=pltpu.VMEM)
    chips, frames, strip, _ = own.shape
    return pl.pallas_call(
        own_kernel,
        out_shape=(jax.ShapeDtypeStruct((384, 384), jnp.float32), jax.ShapeDtypeStruct((384, 256), jnp.float32)),
        in_specs=[smem] * 3 + [vmem],
        out_specs=(vmem, vmem),
        scratch_shapes=[pltpu.VMEM((chips * frames * strip, 384), jnp.bfloat16)],
        compiler_params=pltpu.CompilerParams(vmem_limit_bytes=20 << 20),
        name="own_term",
    )(place, prev_ok, next_ok, own)


def term_kernel(place_ref, prev_ref, next_ref, own_ref, sib_ref, halo_ref, outer_ref, mid_ref, out_ref, fa, fh, gh):
    chips, frames, strip, _ = own_ref.shape
    core, xl, wrapped = place_ref[0], place_ref[1], place_ref[2]

    def halo(chip):
        return halo_ref[(chip // 2 + wrapped) % 2 * 2 + chip % 2]

    @pl.when(core == 0)
    def _():
        for chip in range(chips):
            at = chip // 2 * 2 * frames
            put(fh, chip, halo(chip), prev_ref[at])
            gh[pl.ds(chip * strip, strip), :] = own_ref[chip, 0, :, 256:]
            for j in range(frames):
                its = own_ref[chip, frames - 1, :, :384] if j == 0 else sib_ref[chip, j - 1, :, :384]
                put(fa, chip * frames + j, its, prev_ref[at + frames + j])

    @pl.when(core != 0)
    def _():
        for chip in range(chips):
            at = chip // 2 * 2 * frames
            put(fh, chip, halo(chip), next_ref[at + 2 * frames - 1])
            gh[pl.ds(chip * strip, strip), :] = own_ref[chip, frames - 1, :, 256:]
            for j in range(frames):
                its = own_ref[chip, 0, :, :384] if j == frames - 1 else sib_ref[chip, j + 1, :, :384]
                put(fa, chip * frames + j, its, next_ref[at + j])

    def center(start, stop):
        return mid_ref[:, :stop - start] + term_dot(lanes(sib_ref, 0, 384), lanes(sib_ref, start, stop))

    outer = outer_ref[...] + term_dot(fa[...], lanes(sib_ref, 256, 640)) + term_dot(fh[...], gh[...])
    left = lax.broadcasted_iota(jnp.int32, (384, 128), 1) < 64
    rolled = pltpu.roll(outer[:, :128], 64, 1)

    def store(start, stop, value):
        @pl.when(xl == 0)
        def _():
            out_ref[:, start:stop] = value[:320]

        @pl.when(xl != 0)
        def _():
            out_ref[64:, start:stop] = value[:256]
            out_ref[:64, start:stop] = value[256:320]

    store(0, 256, outer[:, 128:])

    @pl.when(core == 0)
    def _():
        mid = center(256, 512)
        store(256, 384, jnp.where(left, rolled, mid[:, :128]))
        store(384, 512, mid[:, 128:])

    @pl.when(core != 0)
    def _():
        store(256, 384, jnp.where(left, rolled, jnp.zeros_like(rolled)))
        store(384, 512, center(512, 640))


def x_term(place, prev_ok, next_ok, own, sib, halo, outer, mid):
    smem = pl.BlockSpec(memory_space=pltpu.SMEM)
    vmem = pl.BlockSpec(memory_space=pltpu.VMEM)
    chips, frames, strip, _ = own.shape
    few = pltpu.VMEM((chips * strip, 384), jnp.bfloat16)
    return pl.pallas_call(
        term_kernel,
        out_shape=jax.ShapeDtypeStruct((320, 512), jnp.float32),
        in_specs=[smem] * 3 + [vmem] * 5,
        out_specs=vmem,
        scratch_shapes=[pltpu.VMEM((chips * frames * strip, 384), jnp.bfloat16), few, few],
        compiler_params=pltpu.CompilerParams(vmem_limit_bytes=20 << 20),
        name="x_term",
    )(place, prev_ok, next_ok, own, sib, halo, outer, mid)


def out_kernel(place_ref, prev_ref, next_ref, f_ref, g_ref, skip_ref, halo_ref, edge_ref, *refs):
    weights, (out_ref, back_ref, f_lo, f_hi, g_lo, g_hi, blocks, weight) = refs[:4], refs[4:]
    frames, strip, width = f_ref.shape
    tokens = frames * strip
    core, at, xl, y, parity = [place_ref[i] for i in range(5)]
    count, rows = weights[0].shape[:2]

    def put(dst, j, value, ok):
        dst[pl.ds(j * strip, strip), :] = jnp.where(ok != 0, value, jnp.zeros_like(value))

    for src, lo, hi, lanes in ((f_ref, f_lo, f_hi, slice(0, width)), (g_ref, g_lo, g_hi, slice(width, 2 * width))):
        halo, edge = halo_ref[:, lanes], edge_ref[1 - core, :, lanes]
        for j in range(frames):
            put(lo, j, jnp.where(core == 0, halo, edge) if j == 0 else src[j - 1], prev_ref[at + j])
            put(hi, j, jnp.where(core == 0, edge, halo) if j == frames - 1 else src[j + 1], next_ref[at + j])

    for i in range(count):
        odd = parity if i < 2 else 1 - parity
        low, high = (3 + odd, jnp.where(odd == 0, 5, 0)) if i % 2 == 0 else (1 + odd, 7 - odd)
        for half in range(2):
            blocks[half, jnp.where(core == 0, low, high)] = weights[half][i]
            blocks[half, jnp.where(core == 0, high, low)] = weights[2 + half][i]
    for half in range(2):
        for i in range(2 * count):
            start = (half * 2 * count + i) * rows
            weight[start:start + rows, :] = blocks[(half + xl) % 2, (y - i + 2 * count) % (2 * count)]

    def dot(a, b):
        return jnp.dot(a, b, preferred_element_type=jnp.float32)

    def dot_t(a, b):
        return lax.dot_general(a, b, (((1,), (1,)), ((), ())), preferred_element_type=jnp.float32)

    f = f_ref[...].reshape(tokens, width)
    g = g_ref[...].reshape(tokens, width)
    taps = [weight[:, k * width:(k + 1) * width] for k in range(3)]
    mixed = dot(f_lo[...], taps[0]) + dot(f, taps[1]) + dot(f_hi[...], taps[2])
    mixed = mixed.reshape(frames, strip, width) + skip_ref[...].astype(jnp.float32)
    out_ref[...] = mixed.astype(jnp.bfloat16)
    back = dot_t(g_hi[...], taps[0]) + dot_t(g, taps[1]) + dot_t(g_lo[...], taps[2])
    back_ref[...] = back.reshape(frames, strip, width).astype(jnp.bfloat16)


def outputs(place, prev_ok, next_ok, features, cotangent, skip_input, halo, edge, *weights):
    frames, strip, width = features.shape
    smem = pl.BlockSpec(memory_space=pltpu.SMEM)
    vmem = pl.BlockSpec(memory_space=pltpu.VMEM)
    buf = pltpu.VMEM((frames * strip, width), jnp.bfloat16)
    out = jax.ShapeDtypeStruct(features.shape, jnp.bfloat16)
    return pl.pallas_call(
        out_kernel,
        out_shape=(out, out),
        in_specs=[smem] * 3 + [vmem] * 9,
        out_specs=(vmem, vmem),
        scratch_shapes=[buf] * 4 + [pltpu.VMEM((2, 8, 40, 3 * width), jnp.bfloat16), pltpu.VMEM((width, 3 * width), jnp.bfloat16)],
        compiler_params=pltpu.CompilerParams(vmem_limit_bytes=28 << 20),
        name="outputs",
    )(place, prev_ok, next_ok, features, cotangent, skip_input, halo, edge, *weights)


def shards(features, skip_input, cotangent, temporal_weight, clip_lengths, cycle_start):
    frames, strip, width = features.shape
    core, xl, xh, z, y = [lax.axis_index(a) for a in ("c", "xl", "xh", "z", "y")]
    n_x, n_y, n_z = lax.axis_size(X), lax.axis_size("y"), lax.axis_size("z")
    n_dp = lax.axis_size(DP)
    total_frames = frames * n_dp

    packed = pack(features, cotangent)
    _, temporal_weight = lax.optimization_barrier((packed, temporal_weight))

    def from_y(even, odd):
        pairs = []
        for plane in range(n_z):
            distance = (even, odd)[plane % 2]
            for side in range(2 if 2 * distance < n_y else 1):
                base = (2 * plane + side) * n_y
                pairs += [(base + i, base + (i + (1 - 2 * side) * distance) % n_y) for i in range(n_y)]
        return lax.ppermute(temporal_weight, ("z", "c", "y"), pairs)

    w_far, w_near = from_y(3, 4), from_y(1, 2)

    both = [(0, 1), (1, 0)]
    own = lax.all_to_all(packed, X, 0, 0, tiled=True).reshape(n_x, frames, strip, width)
    ends = [jnp.concatenate([features[i], cotangent[i]], axis=1) for i in (0, -1)]
    edges = lax.all_gather(jnp.where(core == 0, ends[1], ends[0]), "c")
    across = [(d, (d - 1) % n_dp if d % 2 == 0 else (d + 1) % n_dp) for d in range(n_dp)]
    halo = lax.ppermute(jnp.where(core == 0, ends[0], ends[1]), DP, across)
    own, w_far, w_near, halo, edges = lax.optimization_barrier((own, w_far, w_near, halo, edges))
    sib = lax.ppermute(own, "c", both)
    z_next = [(2 * i, (2 * i - 1) % (2 * n_z)) for i in range(n_z)] + [(2 * i + 1, (2 * i + 2) % (2 * n_z)) for i in range(n_z)]
    edge = jnp.where(core == 0, own[:, 0, :, :384], own[:, -1, :, :384])
    halo_x = lax.ppermute(edge, ("z", "c"), z_next)

    _, clip_lengths, cycle_start = lax.optimization_barrier((edge, clip_lengths, cycle_start))
    first = (jnp.arange(2, dtype=jnp.int32) * n_z + z)[:, None] * (2 * frames)
    chip_frames = (first + jnp.arange(2 * frames, dtype=jnp.int32)).reshape(-1)
    prev_all, next_all = border_flags(clip_lengths, cycle_start, chip_frames, total_frames)
    wrapped = jnp.where(core == 0, z == 0, z == n_z - 1)
    place = jnp.stack([core, xl, wrapped.astype(jnp.int32)]).astype(jnp.int32)
    outer, mid = own_term(place, prev_all, next_all, own)
    term = x_term(place, prev_all, next_all, own, sib, halo_x, outer, mid)

    _, w_far, w_near = lax.optimization_barrier((term, w_far, w_near))
    parity = z % 2
    pair = jnp.stack([jnp.where((parity == 1) & (core == 1), temporal_weight, w_far), w_near])
    pair_far = lax.ppermute(pair, "z", [(i, i ^ 1) for i in range(n_z)])
    def other_xl(i, planes):
        xh_z, side, half = i // 4, i // 2 % 2, i % 2
        far_xh, far_z = (xh_z // n_z + side) % 2, xh_z % n_z ^ planes
        return ((far_xh * n_z + far_z) * 2 + side) * 2 + 1 - half

    place_x = ("xh", "z", "c", "xl")
    pair_xl, pair_diag = [
        lax.ppermute(pair, place_x, [(i, other_xl(i, planes)) for i in range(8 * n_z)]) for planes in (0, 1)
    ]

    part = lax.all_to_all(term.reshape(n_y, 320 // n_y, 512), "y", 0, 0, tiled=True)
    part, pair_far, pair_xl = lax.optimization_barrier((part, pair_far, pair_xl))
    part = part.sum(0)
    local_rows = part.shape[0]
    n_xz = 2 * n_z
    pieces = jnp.pad(part, ((0, 48 - local_rows), (0, 0))).reshape(6, 8, 2, 256).transpose(0, 2, 1, 3).reshape(n_z, 8, 256)
    _, pair_far, pair_xl, pair_diag = lax.optimization_barrier((pieces, pair_far, pair_xl, pair_diag))
    blocks, blocks_far = jnp.concatenate([pair, pair_far]), jnp.concatenate([pair_xl, pair_diag])
    blocks_sib = lax.ppermute(blocks, "c", both)
    mine = lax.all_to_all(pieces, "z", 0, 0, tiled=True)
    mine = mine.sum(0) * (1.0 / math.sqrt(total_frames * strip * lax.axis_size(FSDP)))
    mine = jnp.broadcast_to(mine[None], (n_xz, 8, 256))
    weights = (blocks, blocks_far, blocks_sib, lax.ppermute(blocks_far, "c", both))
    _, weights = lax.optimization_barrier((mine, weights))
    gathered = lax.all_to_all(mine, ("xh", "z"), 0, 0, tiled=True)
    place_out = jnp.stack([core, xh * (2 * frames) + core * frames, xl, y, parity]).astype(jnp.int32)
    block_out, grad_features = outputs(
        place_out, prev_all, next_all, features, cotangent, skip_input, halo, edges, *weights
    )
    gathered, block_out, grad_features = lax.optimization_barrier((gathered, block_out, grad_features))
    gathered = lax.all_gather(gathered, "c")

    def flat(a):
        a = a.reshape(2, 6, 2, 8, 256).transpose(0, 1, 3, 2, 4)
        return a.reshape(2, 48, 512)[:, :local_rows]

    low, high = flat(gathered[0]), flat(gathered[1])

    def outer_tap(b):
        return [b[0, :, :320], b[1, :, 256:320], b[1, :, :256]]

    tap_1 = [low[0, :, 384:], high[0, :, 384:], low[0, :, 320:384], low[1, :, 320:], high[1, :, 384:]]
    grad_weight = jnp.concatenate(outer_tap(low) + tap_1 + outer_tap(high), axis=1)

    return (block_out, grad_features, grad_weight)


def solution(mesh):
    split = Mesh(mesh.devices.reshape(2, 12, 2, 2, 8), DP + FSDP)
    tokens = P(DP, FSDP, None)
    in_specs = (tokens, tokens, tokens, P(FSDP, None), P(), P())
    out_specs = (tokens, tokens, P(FSDP, None))
    return jax.shard_map(shards, mesh=split, in_specs=in_specs, out_specs=out_specs, check_vma=False)
```

```python
import math

import jax
import jax.numpy as jnp
from jax import lax
from jax.experimental import pallas as pl
from jax.experimental.pallas import tpu as pltpu
from jax.sharding import Mesh, PartitionSpec as P

DP = ("xh", "z", "c")
FSDP = ("xl", "y")
X = ("xh", "xl")


def border_flags(clip_lengths, cycle_start, frame_index, total):
    clip = jnp.arange(clip_lengths.shape[0], dtype=jnp.int32)
    starts = jnp.sum(jnp.where(clip[None, :] < clip[:, None], clip_lengths[None, :], 0), axis=1)
    position = jnp.mod(frame_index - cycle_start[0], total)
    following = jnp.mod(frame_index + 1 - cycle_start[0], total)
    first_here = jnp.any(starts[:, None] == position[None, :], axis=0)
    first_next = jnp.any(starts[:, None] == following[None, :], axis=0)
    return (1 - first_here.astype(jnp.int32), 1 - first_next.astype(jnp.int32))


def pack_kernel(f_hbm, g_hbm, out_hbm, f_ref, g_ref, out_ref, in_sems, out_sems):
    steps = f_ref.shape[0]
    frames, strip, width = f_ref.shape[1:]
    rows = frames * strip

    def fetch(i):
        return [
            pltpu.make_async_copy(src.at[pl.ds(i * frames, frames)], dst.at[i], in_sems.at[i, k])
            for k, (src, dst) in enumerate(((f_hbm, f_ref), (g_hbm, g_ref)))
        ]

    def send(i):
        return pltpu.make_async_copy(out_ref.at[i], out_hbm.at[:, pl.ds(i * rows, rows), :], out_sems.at[i])

    for i in range(steps):
        for copy in fetch(i):
            copy.start()
    for i in range(steps):
        for copy in fetch(i):
            copy.wait()
        f = f_ref[i].reshape(rows, width)
        g = g_ref[i].reshape(rows, width)
        f_mid, g_mid = f[:, 256:384], g[:, 256:384]
        f_rolled, g_rolled = [pltpu.roll(m.astype(jnp.float32), 64, 1).astype(jnp.bfloat16) for m in (f_mid, g_mid)]
        left = lax.broadcasted_iota(jnp.int32, f_mid.shape, 1) < 64
        for xh in range(2):
            for xl in range(2):
                j = 2 * xh + xl
                out_ref[i, j, :, :256] = f[:, 384 * xl:384 * xl + 256]
                out_ref[i, j, :, 256:384] = jnp.where(left, f_rolled if xl else f_mid, g_mid if xh else g_rolled)
                out_ref[i, j, :, 384:] = g[:, 384 * xh:384 * xh + 256]
        send(i).start()
    for i in range(steps):
        send(i).wait()


def pack(features, cotangent):
    frames, strip, width = features.shape
    steps = 2
    hbm = pl.BlockSpec(memory_space=pltpu.HBM)
    part = pltpu.VMEM((steps, frames // steps, strip, width), jnp.bfloat16)
    return pl.pallas_call(
        pack_kernel,
        out_shape=jax.ShapeDtypeStruct((4, frames * strip, width), jnp.bfloat16),
        in_specs=[hbm] * 2,
        out_specs=hbm,
        scratch_shapes=[
            part, part, pltpu.VMEM((steps, 4, frames * strip // steps, width), jnp.bfloat16),
            pltpu.SemaphoreType.DMA((steps, 2)), pltpu.SemaphoreType.DMA((steps,)),
        ],
        compiler_params=pltpu.CompilerParams(vmem_limit_bytes=60 << 20),
        name="pack",
    )(features, cotangent)


def put(dst, slot, value, ok):
    rows = value.shape[0]
    dst[pl.ds(slot * rows, rows), :] = jnp.where(ok != 0, value, jnp.zeros_like(value))


def lanes(ref, start, stop):
    return ref[:, :, :, start:stop].reshape(-1, stop - start)


def term_dot(a, b):
    return lax.dot_general(a, b, (((0,), (0,)), ((), ())), preferred_element_type=jnp.float32)


def own_kernel(place_ref, prev_ref, next_ref, own_ref, outer_ref, mid_ref, fa):
    chips, frames, strip, _ = own_ref.shape
    core = place_ref[0]
    nothing = jnp.zeros((strip, 384), jnp.bfloat16)

    @pl.when(core == 0)
    def _():
        for chip in range(chips):
            at = chip // 2 * 2 * frames
            for j in range(frames):
                put(fa, chip * frames + j, nothing if j == 0 else own_ref[chip, j - 1, :, :384], prev_ref[at + j])
        mid_ref[...] = term_dot(lanes(own_ref, 0, 384), lanes(own_ref, 256, 512))

    @pl.when(core != 0)
    def _():
        for chip in range(chips):
            at = chip // 2 * 2 * frames + frames
            for j in range(frames):
                put(fa, chip * frames + j, nothing if j == frames - 1 else own_ref[chip, j + 1, :, :384], next_ref[at + j])
        mid_ref[:, :128] = term_dot(lanes(own_ref, 0, 384), lanes(own_ref, 512, 640))
        mid_ref[:, 128:] = jnp.zeros((384, 128), jnp.float32)

    outer_ref[...] = term_dot(fa[...], lanes(own_ref, 256, 640))


def own_term(place, prev_ok, next_ok, own):
    smem = pl.BlockSpec(memory_space=pltpu.SMEM)
    vmem = pl.BlockSpec(memory_space=pltpu.VMEM)
    chips, frames, strip, _ = own.shape
    return pl.pallas_call(
        own_kernel,
        out_shape=(jax.ShapeDtypeStruct((384, 384), jnp.float32), jax.ShapeDtypeStruct((384, 256), jnp.float32)),
        in_specs=[smem] * 3 + [vmem],
        out_specs=(vmem, vmem),
        scratch_shapes=[pltpu.VMEM((chips * frames * strip, 384), jnp.bfloat16)],
        compiler_params=pltpu.CompilerParams(vmem_limit_bytes=20 << 20),
        name="own_term",
    )(place, prev_ok, next_ok, own)


def term_kernel(place_ref, prev_ref, next_ref, own_ref, sib_ref, halo_ref, outer_ref, mid_ref, out_ref, fa, fh, gh):
    chips, frames, strip, _ = own_ref.shape
    core, xl, wrapped = place_ref[0], place_ref[1], place_ref[2]

    def halo(chip):
        return halo_ref[(chip // 2 + wrapped) % 2 * 2 + chip % 2]

    @pl.when(core == 0)
    def _():
        for chip in range(chips):
            at = chip // 2 * 2 * frames
            put(fh, chip, halo(chip), prev_ref[at])
            gh[pl.ds(chip * strip, strip), :] = own_ref[chip, 0, :, 256:]
            for j in range(frames):
                its = own_ref[chip, frames - 1, :, :384] if j == 0 else sib_ref[chip, j - 1, :, :384]
                put(fa, chip * frames + j, its, prev_ref[at + frames + j])

    @pl.when(core != 0)
    def _():
        for chip in range(chips):
            at = chip // 2 * 2 * frames
            put(fh, chip, halo(chip), next_ref[at + 2 * frames - 1])
            gh[pl.ds(chip * strip, strip), :] = own_ref[chip, frames - 1, :, 256:]
            for j in range(frames):
                its = own_ref[chip, 0, :, :384] if j == frames - 1 else sib_ref[chip, j + 1, :, :384]
                put(fa, chip * frames + j, its, next_ref[at + j])

    def center(start, stop):
        return mid_ref[:, :stop - start] + term_dot(lanes(sib_ref, 0, 384), lanes(sib_ref, start, stop))

    outer = outer_ref[...] + term_dot(fa[...], lanes(sib_ref, 256, 640)) + term_dot(fh[...], gh[...])
    left = lax.broadcasted_iota(jnp.int32, (384, 128), 1) < 64
    rolled = pltpu.roll(outer[:, :128], 64, 1)

    def store(start, stop, value):
        @pl.when(xl == 0)
        def _():
            out_ref[:, start:stop] = value[:320]

        @pl.when(xl != 0)
        def _():
            out_ref[64:, start:stop] = value[:256]
            out_ref[:64, start:stop] = value[256:320]

    store(0, 256, outer[:, 128:])

    @pl.when(core == 0)
    def _():
        mid = center(256, 512)
        store(256, 384, jnp.where(left, rolled, mid[:, :128]))
        store(384, 512, mid[:, 128:])

    @pl.when(core != 0)
    def _():
        store(256, 384, jnp.where(left, rolled, jnp.zeros_like(rolled)))
        store(384, 512, center(512, 640))


def x_term(place, prev_ok, next_ok, own, sib, halo, outer, mid):
    smem = pl.BlockSpec(memory_space=pltpu.SMEM)
    vmem = pl.BlockSpec(memory_space=pltpu.VMEM)
    chips, frames, strip, _ = own.shape
    few = pltpu.VMEM((chips * strip, 384), jnp.bfloat16)
    return pl.pallas_call(
        term_kernel,
        out_shape=jax.ShapeDtypeStruct((320, 512), jnp.float32),
        in_specs=[smem] * 3 + [vmem] * 5,
        out_specs=vmem,
        scratch_shapes=[pltpu.VMEM((chips * frames * strip, 384), jnp.bfloat16), few, few],
        compiler_params=pltpu.CompilerParams(vmem_limit_bytes=20 << 20),
        name="x_term",
    )(place, prev_ok, next_ok, own, sib, halo, outer, mid)


def out_kernel(place_ref, prev_ref, next_ref, f_ref, g_ref, skip_ref, halo_ref, edge_ref, *refs):
    weights, (out_ref, back_ref, f_lo, f_hi, g_lo, g_hi, blocks, weight) = refs[:4], refs[4:]
    frames, strip, width = f_ref.shape
    tokens = frames * strip
    core, at, xl, y, parity = [place_ref[i] for i in range(5)]
    count, rows = weights[0].shape[:2]

    def put(dst, j, value, ok):
        dst[pl.ds(j * strip, strip), :] = jnp.where(ok != 0, value, jnp.zeros_like(value))

    for src, lo, hi, lanes in ((f_ref, f_lo, f_hi, slice(0, width)), (g_ref, g_lo, g_hi, slice(width, 2 * width))):
        halo, edge = halo_ref[:, lanes], edge_ref[1 - core, :, lanes]
        for j in range(frames):
            put(lo, j, jnp.where(core == 0, halo, edge) if j == 0 else src[j - 1], prev_ref[at + j])
            put(hi, j, jnp.where(core == 0, edge, halo) if j == frames - 1 else src[j + 1], next_ref[at + j])

    for i in range(count):
        odd = parity if i < 2 else 1 - parity
        low, high = (3 + odd, jnp.where(odd == 0, 5, 0)) if i % 2 == 0 else (1 + odd, 7 - odd)
        for half in range(2):
            blocks[half, jnp.where(core == 0, low, high)] = weights[half][i]
            blocks[half, jnp.where(core == 0, high, low)] = weights[2 + half][i]
    for half in range(2):
        for i in range(2 * count):
            start = (half * 2 * count + i) * rows
            weight[start:start + rows, :] = blocks[(half + xl) % 2, (y - i + 2 * count) % (2 * count)]

    def dot(a, b):
        return jnp.dot(a, b, preferred_element_type=jnp.float32)

    def dot_t(a, b):
        return lax.dot_general(a, b, (((1,), (1,)), ((), ())), preferred_element_type=jnp.float32)

    f = f_ref[...].reshape(tokens, width)
    g = g_ref[...].reshape(tokens, width)
    taps = [weight[:, k * width:(k + 1) * width] for k in range(3)]
    mixed = dot(f_lo[...], taps[0]) + dot(f, taps[1]) + dot(f_hi[...], taps[2])
    mixed = mixed.reshape(frames, strip, width) + skip_ref[...].astype(jnp.float32)
    out_ref[...] = mixed.astype(jnp.bfloat16)
    back = dot_t(g_hi[...], taps[0]) + dot_t(g, taps[1]) + dot_t(g_lo[...], taps[2])
    back_ref[...] = back.reshape(frames, strip, width).astype(jnp.bfloat16)


def outputs(place, prev_ok, next_ok, features, cotangent, skip_input, halo, edge, *weights):
    frames, strip, width = features.shape
    smem = pl.BlockSpec(memory_space=pltpu.SMEM)
    vmem = pl.BlockSpec(memory_space=pltpu.VMEM)
    buf = pltpu.VMEM((frames * strip, width), jnp.bfloat16)
    out = jax.ShapeDtypeStruct(features.shape, jnp.bfloat16)
    return pl.pallas_call(
        out_kernel,
        out_shape=(out, out),
        in_specs=[smem] * 3 + [vmem] * 9,
        out_specs=(vmem, vmem),
        scratch_shapes=[buf] * 4 + [pltpu.VMEM((2, 8, 40, 3 * width), jnp.bfloat16), pltpu.VMEM((width, 3 * width), jnp.bfloat16)],
        compiler_params=pltpu.CompilerParams(vmem_limit_bytes=28 << 20),
        name="outputs",
    )(place, prev_ok, next_ok, features, cotangent, skip_input, halo, edge, *weights)


def shards(features, skip_input, cotangent, temporal_weight, clip_lengths, cycle_start):
    frames, strip, width = features.shape
    core, xl, xh, z, y = [lax.axis_index(a) for a in ("c", "xl", "xh", "z", "y")]
    n_x, n_y, n_z = lax.axis_size(X), lax.axis_size("y"), lax.axis_size("z")
    n_dp = lax.axis_size(DP)
    total_frames = frames * n_dp

    packed = pack(features, cotangent)
    _, temporal_weight = lax.optimization_barrier((packed, temporal_weight))

    def from_y(even, odd):
        pairs = []
        for plane in range(n_z):
            distance = (even, odd)[plane % 2]
            for side in range(2 if 2 * distance < n_y else 1):
                base = (2 * plane + side) * n_y
                pairs += [(base + i, base + (i + (1 - 2 * side) * distance) % n_y) for i in range(n_y)]
        return lax.ppermute(temporal_weight, ("z", "c", "y"), pairs)

    w_far, w_near = from_y(3, 4), from_y(1, 2)

    both = [(0, 1), (1, 0)]
    own = lax.all_to_all(packed, X, 0, 0, tiled=True).reshape(n_x, frames, strip, width)
    ends = [jnp.concatenate([features[i], cotangent[i]], axis=1) for i in (0, -1)]
    edges = lax.all_gather(jnp.where(core == 0, ends[1], ends[0]), "c")
    across = [(d, (d - 1) % n_dp if d % 2 == 0 else (d + 1) % n_dp) for d in range(n_dp)]
    halo = lax.ppermute(jnp.where(core == 0, ends[0], ends[1]), DP, across)
    own, w_far, w_near, halo, edges = lax.optimization_barrier((own, w_far, w_near, halo, edges))
    sib = lax.ppermute(own, "c", both)
    z_next = [(2 * i, (2 * i - 1) % (2 * n_z)) for i in range(n_z)] + [(2 * i + 1, (2 * i + 2) % (2 * n_z)) for i in range(n_z)]
    edge = jnp.where(core == 0, own[:, 0, :, :384], own[:, -1, :, :384])
    halo_x = lax.ppermute(edge, ("z", "c"), z_next)

    _, clip_lengths, cycle_start = lax.optimization_barrier((edge, clip_lengths, cycle_start))
    first = (jnp.arange(2, dtype=jnp.int32) * n_z + z)[:, None] * (2 * frames)
    chip_frames = (first + jnp.arange(2 * frames, dtype=jnp.int32)).reshape(-1)
    prev_all, next_all = border_flags(clip_lengths, cycle_start, chip_frames, total_frames)
    wrapped = jnp.where(core == 0, z == 0, z == n_z - 1)
    place = jnp.stack([core, xl, wrapped.astype(jnp.int32)]).astype(jnp.int32)
    outer, mid = own_term(place, prev_all, next_all, own)
    term = x_term(place, prev_all, next_all, own, sib, halo_x, outer, mid)

    _, w_far, w_near = lax.optimization_barrier((term, w_far, w_near))
    parity = z % 2
    pair = jnp.stack([jnp.where((parity == 1) & (core == 1), temporal_weight, w_far), w_near])
    pair_far = lax.ppermute(pair, "z", [(i, i ^ 1) for i in range(n_z)])
    def other_xl(i, planes):
        xh_z, side, half = i // 4, i // 2 % 2, i % 2
        far_xh, far_z = (xh_z // n_z + side) % 2, xh_z % n_z ^ planes
        return ((far_xh * n_z + far_z) * 2 + side) * 2 + 1 - half

    place_x = ("xh", "z", "c", "xl")
    pair_xl, pair_diag = [
        lax.ppermute(pair, place_x, [(i, other_xl(i, planes)) for i in range(8 * n_z)]) for planes in (0, 1)
    ]

    part = lax.all_to_all(term.reshape(n_y, 320 // n_y, 512), "y", 0, 0, tiled=True)
    part, pair_far = lax.optimization_barrier((part, pair_far))
    part = part.sum(0)
    local_rows = part.shape[0]
    n_xz = 2 * n_z
    pieces = jnp.pad(part, ((0, 48 - local_rows), (0, 0))).reshape(6, 8, 2, 256).transpose(0, 2, 1, 3).reshape(n_z, 8, 256)
    _, pair_far, pair_xl, pair_diag = lax.optimization_barrier((pieces, pair_far, pair_xl, pair_diag))
    blocks, blocks_far = jnp.concatenate([pair, pair_far]), jnp.concatenate([pair_xl, pair_diag])
    blocks_sib = lax.ppermute(blocks, "c", both)
    mine = lax.all_to_all(pieces, "z", 0, 0, tiled=True)
    mine = mine.sum(0) * (1.0 / math.sqrt(total_frames * strip * lax.axis_size(FSDP)))
    mine = jnp.broadcast_to(mine[None], (n_xz, 8, 256))
    weights = (blocks, blocks_far, blocks_sib, lax.ppermute(blocks_far, "c", both))
    _, weights = lax.optimization_barrier((mine, weights))
    gathered = lax.all_to_all(mine, ("xh", "z"), 0, 0, tiled=True)
    place_out = jnp.stack([core, xh * (2 * frames) + core * frames, xl, y, parity]).astype(jnp.int32)
    block_out, grad_features = outputs(
        place_out, prev_all, next_all, features, cotangent, skip_input, halo, edges, *weights
    )
    gathered, block_out, grad_features = lax.optimization_barrier((gathered, block_out, grad_features))
    gathered = lax.all_gather(gathered, "c")

    def flat(a):
        a = a.reshape(2, 6, 2, 8, 256).transpose(0, 1, 3, 2, 4)
        return a.reshape(2, 48, 512)[:, :local_rows]

    low, high = flat(gathered[0]), flat(gathered[1])

    def outer_tap(b):
        return [b[0, :, :320], b[1, :, 256:320], b[1, :, :256]]

    tap_1 = [low[0, :, 384:], high[0, :, 384:], low[0, :, 320:384], low[1, :, 320:], high[1, :, 384:]]
    grad_weight = jnp.concatenate(outer_tap(low) + tap_1 + outer_tap(high), axis=1)

    return (block_out, grad_features, grad_weight)


def solution(mesh):
    split = Mesh(mesh.devices.reshape(2, 12, 2, 2, 8), DP + FSDP)
    tokens = P(DP, FSDP, None)
    in_specs = (tokens, tokens, tokens, P(FSDP, None), P(), P())
    out_specs = (tokens, tokens, P(FSDP, None))
    return jax.shard_map(shards, mesh=split, in_specs=in_specs, out_specs=out_specs, check_vma=False)
```
